256 devices in a mesh: gx: 8 (over y, core), gy: 4 (over z_lo), gz: 8 (over x, z_hi).
Axes of the slice: x: 4, y: 4, z: 8 (z_hi: 2, z_lo: 4; z = z_hi * 4 + z_lo), core: 2. Of those that a mesh axis runs over, the one named last changes fastest.
Arguments:
- stiffness: float32 [64, 48, 1024], P('gx', 'gy', 'gz'), may hold values from 0.5 to 5
- density: float32 [64, 48, 1024], P('gx', 'gy', 'gz'), may hold values from 1 to 4
- load: float32 [3, 64, 48, 1024], P(None, 'gx', 'gy', 'gz'), may hold values from -6 to 6
- alive: int32 [4, 64, 48, 1024], P(None, 'gx', 'gy', 'gz'), may hold values 0 or 1
- surf_coords: float32 [4096, 3, 128], P(('gx', 'gy', 'gz')), may hold values from 0 to 1
- surf_nodes: int32 [4096, 128], P(('gx', 'gy', 'gz')), may hold values from 0 to 12287
- routes: int32 [4, 4096], P(None, ('gx', 'gy', 'gz')), may hold values from 0 to 7, as said below
- pairs: int32 [4, 256, 64, 2], P(None, ('gx', 'gy', 'gz')), may hold values from 0 to 31, as said below
Outputs:
- element_velocity: float32 [3, 64, 48, 1024], P(None, 'gx', 'gy', 'gz')
- element_stress: float32 [6, 64, 48, 1024], P(None, 'gx', 'gy', 'gz')
The draws below stay inside these ranges and needn't reach their ends.
Inputs may be any that keep to these rules, and one draw needn't show every extreme that they name: `routes`: in every step a device sends at most 4 of its blocks to one box, and all devices of a gz column send exactly 4 blocks to one common box of that column. `pairs`: every slot named is live at that box and step whenever the box holds a block at all.
All inputs are finite; a program needn't handle non-finite values. No bound on the sum of `alive` on one device may be relied on, other than what follows from the above.
Results may differ from the reference program's by a relative error of at most 0.0003.
Values sent between devices are 32-bit elements; how exact they have to be, the bound alone decides.
No kernel may reach another device: no remote copies, remote signals or barrier semaphores. Data moves between devices by JAX's collectives and lax.ppermute only.
A program may use at most 64 MiB of HBM per device.

```python
import math
import jax
import jax.numpy as jnp
from jax import lax

CX = 8
CY = 12
CZ = 128
SB = 16
NPAIR = 64
BNODES = 128
STEPS = 4
NX = 64
NY = 48
NZ = 1024
BLOCKS = 4096
N_GX = 8
N_GY = 4
N_GZ = 8


def contact_plan(key):
    devices = N_GX * N_GY * N_GZ
    columns = N_GX * N_GY
    capacity = max(SB // 4, SB // N_GZ)
    entries = N_GZ * capacity
    key_target = jax.random.fold_in(key, 101)
    key_noise = jax.random.fold_in(key, 202)
    key_shuffle = jax.random.fold_in(key, 303)
    key_picks = jax.random.fold_in(key, 404)
    target = jax.random.randint(key_target, (STEPS, columns), 0, N_GZ)
    target_device = jnp.repeat(target, N_GZ, axis=1)
    entry = jnp.arange(entries, dtype=jnp.int32)
    entry_box = entry // capacity
    noise = jax.random.randint(key_noise, (STEPS, devices, entries), 0, 65536)
    score = jnp.where(entry_box[None, None, :] == target_device[:, :, None], 0, 1 + noise) * entries + entry
    order = jnp.argsort(score, axis=-1)
    chosen = entry_box[order[..., :SB]]
    shuffle = jax.random.randint(key_shuffle, (STEPS, devices, SB), 0, 65536) * SB + jnp.arange(SB, dtype=jnp.int32)
    placing = jnp.argsort(shuffle, axis=-1)
    route_table = jnp.take_along_axis(chosen, placing, axis=-1)
    counts = jnp.sum((route_table[..., None] == jnp.arange(N_GZ, dtype=jnp.int32)).astype(jnp.int32), axis=2)
    counts = counts.reshape(STEPS, columns, N_GZ, N_GZ).transpose(0, 1, 3, 2).reshape(STEPS, devices, N_GZ)
    live = jnp.arange(capacity, dtype=jnp.int32)[None, None, None, :] < counts[..., None]
    live = live.reshape(STEPS, devices, entries)
    live_first = jnp.argsort(jnp.where(live, 0, 1) * entries + entry, axis=-1)
    how_many = jnp.maximum(jnp.sum(live.astype(jnp.int32), axis=-1), 1)
    picks = jax.random.randint(key_picks, (STEPS, devices, NPAIR * 2), 0, 65536) % how_many[..., None]
    slot_table = jnp.take_along_axis(live_first, picks, axis=-1).reshape(STEPS, devices, NPAIR, 2)
    return (route_table.reshape(STEPS, devices * SB).astype(jnp.int32), slot_table.astype(jnp.int32))


def draw_routes(key, part):
    return contact_plan(key)[0]


def draw_pairs(key, part):
    return contact_plan(key)[1]


def plant(values, own_key, smallest, top_value):
    place = [jax.random.randint(jax.random.fold_in(own_key, axis), (), 0, length) for axis, length in enumerate(values.shape)]
    widest = values.shape.index(max(values.shape))
    next_to = place[:widest] + [(place[widest] + 1) % values.shape[widest]] + place[widest + 1:]
    return values.at[tuple(place)].set(smallest).at[tuple(next_to)].set(top_value)


def shard_levels(stream_key, dims, split, least, top_value):
    def one(axis_at, blocks):
        draws = jax.random.uniform(jax.random.fold_in(jax.random.fold_in(stream_key, 6), axis_at), (blocks,), jnp.float32, least / len(split), top_value / len(split))
        return jnp.repeat(jnp.exp(draws), dims[axis_at] // blocks).reshape((-1,) + (1,) * (len(dims) - axis_at - 1))

    loudness = one(*split[0])
    for cut in split[1:]:
        loudness = loudness * one(*cut)
    return loudness


def scatter_about(stream_key, extent, spread, bound, cuts=(), kind=jnp.bfloat16):
    array = spread * jax.random.normal(stream_key, extent, jnp.float32)
    if cuts:
        array = array * shard_levels(stream_key, extent, cuts, -0.22, 0.18)
    return jnp.clip(array, -bound, bound).astype(kind)


def setup_inputs(seed: int = 0) -> dict:
    key_of = jax.random.split(jax.random.key(seed), 9)
    stiffness = jnp.clip(jnp.exp(math.log(5.0) - 2.3025851 * jax.random.uniform(key_of[0], (NX, NY, NZ), jnp.float32) ** shard_levels(key_of[0], (NX, NY, NZ), ((0, 8), (1, 4), (2, 8)), -0.2, 0.2)), 0.5, 5.0)
    density = jnp.clip(jnp.exp(math.log(4.0) - 1.3862944 * jax.random.uniform(key_of[1], (NX, NY, NZ), jnp.float32) ** shard_levels(key_of[1], (NX, NY, NZ), ((0, 8), (1, 4), (2, 8)), -0.2, 0.2)), 1.0, 4.0)
    load = scatter_about(key_of[2], (3, NX, NY, NZ), 1.0, 6.0, ((1, 8), (2, 4), (3, 8)), jnp.float32)
    alive = plant((jax.random.randint(key_of[3], (STEPS, NX, NY, NZ), 0, 10) < 9).astype(jnp.int32), jax.random.fold_in(key_of[3], 1), 0, 1)
    surf_coords = jnp.clip(1.0 * jax.random.uniform(key_of[4], (BLOCKS, 3, BNODES), jnp.float32) ** shard_levels(key_of[4], (BLOCKS, 3, BNODES), ((0, 256),), -0.2, 0.2), 0.0, 1.0)
    surf_nodes = plant(jax.random.randint(key_of[5], (BLOCKS, BNODES), 0, CX * CY * CZ), jax.random.fold_in(key_of[5], 1), 0, (CX * CY * CZ) - 1).astype(jnp.int32)
    routes = draw_routes(jax.random.fold_in(key_of[8], 71), 0)
    pairs = draw_pairs(jax.random.fold_in(key_of[8], 71), 0)
    return dict(stiffness=stiffness, density=density, load=load, alive=alive, surf_coords=surf_coords, surf_nodes=surf_nodes, routes=routes, pairs=pairs)


REPULSION = 1.0
KERNEL_SCALE = 0.08
TIME_STEP = 0.2
HIGHEST = lax.Precision.HIGHEST
CORNERS = [(0, 0, 0), (0, 0, 1), (0, 1, 0), (0, 1, 1), (1, 0, 0), (1, 0, 1), (1, 1, 0), (1, 1, 1)]


def corner(field, offsets):
    size_x = field.shape[1] - 1
    size_y = field.shape[2] - 1
    size_z = field.shape[3] - 1
    return field[:, offsets[0]:offsets[0] + size_x, offsets[1]:offsets[1] + size_y, offsets[2]:offsets[2] + size_z]


def element_stress(disp, modulus):
    grads = []
    for axis in range(3):
        parts = []
        for first in (0, 1):
            for second in (0, 1):
                upper = [first, second]
                upper.insert(axis, 1)
                lower = [first, second]
                lower.insert(axis, 0)
                parts.append(corner(disp, upper) - corner(disp, lower))
        grads.append(0.25 * (parts[0] + parts[1] + parts[2] + parts[3]))
    strain_xx = grads[0][0]
    strain_yy = grads[1][1]
    strain_zz = grads[2][2]
    strain_xy = 0.5 * (grads[1][0] + grads[0][1])
    strain_yz = 0.5 * (grads[2][1] + grads[1][2])
    strain_zx = 0.5 * (grads[0][2] + grads[2][0])
    trace = strain_xx + strain_yy + strain_zz
    return jnp.stack([modulus * (2.0 * strain_xx + trace), modulus * (2.0 * strain_yy + trace),
                      modulus * (2.0 * strain_zz + trace), modulus * 2.0 * strain_xy,
                      modulus * 2.0 * strain_yz, modulus * 2.0 * strain_zx])


def node_forces(stress, load):
    rows = ((stress[0], stress[3], stress[5]), (stress[3], stress[1], stress[4]), (stress[5], stress[4], stress[2]))
    total = jnp.float32(0.0)
    for offsets in CORNERS:
        signs = [2.0 * offsets[0] - 1.0, 2.0 * offsets[1] - 1.0, 2.0 * offsets[2] - 1.0]
        pieces = []
        for index in range(3):
            row = rows[index]
            pieces.append(-0.25 * (signs[0] * row[0] + signs[1] * row[1] + signs[2] * row[2]) + 0.125 * load[index])
        term = jnp.stack(pieces)
        total = total + jnp.pad(term, ((0, 0), (offsets[0], 1 - offsets[0]), (offsets[1], 1 - offsets[1]), (offsets[2], 1 - offsets[2])))
    return total


def node_mass(density):
    share = 0.125 * density
    total = jnp.float32(0.0)
    for offsets in CORNERS:
        total = total + jnp.pad(share, ((offsets[0], 1 - offsets[0]), (offsets[1], 1 - offsets[1]), (offsets[2], 1 - offsets[2])))
    return total


def element_mean(vel):
    total = jnp.float32(0.0)
    for offsets in CORNERS:
        total = total + corner(vel, offsets)
    return 0.125 * total


def selection(route_row, boxes, capacity):
    hits = route_row[None, :] == boxes[:, None]
    rank = jnp.cumsum(hits.astype(jnp.int32), axis=1) - 1
    chosen = hits[:, None, :] & (rank[:, None, :] == jnp.arange(capacity, dtype=jnp.int32)[None, :, None])
    return chosen.astype(jnp.float32)


def pair_forces(first, second, valid_first, valid_second):
    diff = first[:, :, :, None] - second[:, :, None, :]
    dist = jnp.sum(diff * diff, axis=1)
    weight = REPULSION * jnp.exp(-dist / KERNEL_SCALE) * (valid_first * valid_second)[:, None, None]
    return jnp.sum(diff * weight[:, None, :, :], axis=3)


def owner_forces(received, valid, pair_list):
    first = received[pair_list[:, 0]]
    second = received[pair_list[:, 1]]
    forces = pair_forces(first, second, valid[pair_list[:, 0]], valid[pair_list[:, 1]])
    onehot = (pair_list[:, 0][:, None] == jnp.arange(received.shape[0], dtype=jnp.int32)[None, :]).astype(jnp.float32)
    return jnp.einsum('pk,pxn->kxn', onehot, forces, precision=HIGHEST)


def reference(stiffness, density, load, alive, surf_coords, surf_nodes, routes, pairs):
    devices = N_GX * N_GY * N_GZ
    columns = N_GX * N_GY
    capacity = max(SB // 4, SB // N_GZ)
    nodes_shape = (3, NX + 1, NY + 1, NZ + 1)
    mass = node_mass(density)
    disp = jnp.zeros(nodes_shape, jnp.float32)
    vel = jnp.zeros(nodes_shape, jnp.float32)
    earlier = disp
    owner = jnp.arange(BLOCKS, dtype=jnp.int32) // SB
    index_x = owner // (N_GY * N_GZ)
    index_y = (owner // N_GZ) % N_GY
    index_z = owner % N_GZ
    local_i = surf_nodes // (CY * CZ)
    local_j = (surf_nodes // CZ) % CY
    local_k = surf_nodes % CZ
    global_i = index_x[:, None] * CX + local_i
    global_j = index_y[:, None] * CY + local_j
    global_k = index_z[:, None] * CZ + local_k
    flat_ids = (global_i * (NY + 1) + global_j) * (NZ + 1) + global_k
    boxes = jnp.arange(N_GZ, dtype=jnp.int32)
    for step in range(STEPS):
        lagged = earlier.reshape(3, -1)
        positions = jnp.moveaxis(lagged[:, flat_ids], 0, 1) + surf_coords
        positions = positions.reshape(devices, SB, 3, BNODES)
        route_rows = routes[step].reshape(devices, SB)
        chosen = jax.vmap(lambda row: selection(row, boxes, capacity))(route_rows)
        send = jnp.einsum('dbks,dsxn->dbkxn', chosen, positions, precision=HIGHEST)
        valid = jnp.sum(chosen, axis=3)
        send = send.reshape(columns, N_GZ, N_GZ, capacity, 3, BNODES).transpose(0, 2, 1, 3, 4, 5)
        send = send.reshape(devices, N_GZ * capacity, 3, BNODES)
        valid = valid.reshape(columns, N_GZ, N_GZ, capacity).transpose(0, 2, 1, 3).reshape(devices, N_GZ * capacity)
        slot_force = lax.map(lambda item: owner_forces(item[0], item[1], item[2]), (send, valid, pairs[step]))
        back = slot_force.reshape(columns, N_GZ, N_GZ, capacity, 3, BNODES).transpose(0, 2, 1, 3, 4, 5)
        back = back.reshape(devices, N_GZ, capacity, 3, BNODES)
        block_force = jnp.einsum('dbks,dbkxn->dsxn', chosen, back, precision=HIGHEST)
        block_force = jnp.moveaxis(block_force.reshape(BLOCKS, 3, BNODES), 1, 0)
        contact = jnp.zeros((3, lagged.shape[1]), jnp.float32).at[:, flat_ids].add(block_force)
        modulus = stiffness * alive[step].astype(jnp.float32)
        force = node_forces(element_stress(disp, modulus), load) + contact.reshape(nodes_shape)
        vel = vel + TIME_STEP * force / mass[None]
        earlier = disp
        disp = disp + TIME_STEP * vel
    final_modulus = stiffness * alive[STEPS - 1].astype(jnp.float32)
    return element_mean(vel), element_stress(disp, final_modulus)
```

```python
import functools
import math
import jax
import jax.numpy as jnp
from jax import lax
from jax.experimental import pallas as pl
from jax.experimental.pallas import tpu as pltpu
from jax.sharding import PartitionSpec as P

F32 = jnp.float32
BF16 = jnp.bfloat16
SCALE = math.sqrt(math.log2(math.e) / 0.08)
TIME_STEP = 0.2
PARAMS = pltpu.CompilerParams(vmem_limit_bytes=48 * 2**20)


def split2(x):
    hi = x.astype(BF16)
    return hi, (x - hi.astype(F32)).astype(BF16)


def iota(shape, dim):
    return lax.broadcasted_iota(jnp.int32, shape, dim)


def plan_kernel(me_ref, all_ref, list_ref, *, around):
    me = me_ref[0]
    lane = iota((1, 128), 1)
    block_of = iota((128, 128), 0).astype(F32)
    eye = iota((128, 128), 0) == iota((128, 128), 1)
    upper = (iota((128, 128), 0) < iota((128, 128), 1)).astype(BF16)
    place = iota((512, 128), 0).astype(F32)
    for step in range(4):
        keys = all_ref[0, 48 + step : 49 + step, :]
        for src in range(1, 8):
            keys = keys + all_ref[src, 48 + step : 49 + step, :]
        key_col = jnp.sum(jnp.where(eye, keys, 0.0), axis=1, keepdims=True)
        base = jnp.zeros((1, 1), F32)
        total = jnp.zeros((8, 512), F32)
        for row in range(4):
            even = all_ref[2 * row, 52 + step : 53 + step, :]
            odd = all_ref[2 * row + 1, 52 + step : 53 + step, :]
            low = lane < 64
            first = jnp.where(low, even, pltpu.roll(odd, 64, 1))
            second = jnp.where(low, pltpu.roll(even, 64, 1), odd)
            box = jnp.where(low, 64.0 * row, 64.0 * row + 32.0)
            hit_first = key_col == first + box
            hit_second = key_col == second + box
            p_block = jnp.sum(jnp.where(hit_first, block_of, 0.0), axis=0, keepdims=True)
            r_block = jnp.sum(jnp.where(hit_second, block_of, 0.0), axis=0, keepdims=True)
            live = jnp.sum(jnp.where(hit_first, 1.0, 0.0), axis=0, keepdims=True) * jnp.sum(
                jnp.where(hit_second, 1.0, 0.0), axis=0, keepdims=True
            )
            p_local = p_block - (16 * me - 16).astype(F32)
            mine = (p_local >= 16.0) & (p_local < 32.0) & (live > 0.0)
            sel = jnp.where(mine, 1.0, 0.0)
            before = jnp.dot(
                jnp.broadcast_to(sel, (8, 128)).astype(BF16), upper, preferred_element_type=F32
            )[0:1]
            spot = jnp.where(mine, before + base, -1.0)
            base = base + jnp.sum(sel, axis=1, keepdims=True)
            onehot = jnp.where(place == spot, 1.0, 0.0).astype(BF16)
            codes = jnp.where(
                iota((8, 128), 0) == 0,
                jnp.broadcast_to(p_local, (8, 128)),
                jnp.broadcast_to(r_block, (8, 128)),
            )
            codes = jnp.where(jnp.broadcast_to(mine, (8, 128)), codes, 0.0).astype(BF16)
            total = total + lax.dot_general(
                codes, onehot, (((1,), (1,)), ((), ())), preferred_element_type=F32
            )
        list_ref[step : step + 1, :] = (total[0:1] * 128.0 + total[1:2]).astype(jnp.int32)
        list_ref[4 + step : 5 + step, :] = jnp.broadcast_to(base, (1, 512)).astype(jnp.int32)


def one_hots(nodes_ref, rows_ref, lanes_ref):
    for s in range(16):
        ids = nodes_ref[s : s + 1, :]
        at = slice(128 * s, 128 * s + 128)
        rows_ref[:, at] = jnp.where(iota((96, 128), 0) == ids // 128, 1.0, 0.0).astype(BF16)
        lanes_ref[:, at] = jnp.where(iota((128, 128), 0) == ids % 128, 1.0, 0.0).astype(BF16)


def pair_loop(list_ref, step, first_row, all_ref, base, force_ref):
    def body(q, carry):
        code = list_ref[step, q]
        p_local = code // 128
        r_block = code % 128
        p_block = p_local + base
        r_src, r_row = r_block // 16, first_row + (r_block % 16) * 3
        p_src, p_row = p_block // 16, first_row + (p_block % 16) * 3
        xi, xj = [], []
        for c in range(3):
            xi.append(jnp.broadcast_to(all_ref[p_src, pl.ds(p_row + c, 1), :] * SCALE, (8, 128)))
            wide = jnp.broadcast_to(all_ref[r_src, pl.ds(r_row + c, 1), :] * SCALE, (8, 128))
            xj.append(pltpu.roll(wide, 0, 1, stride=1, stride_axis=0))
        acc = [jnp.zeros((8, 128), F32)] * 3
        for k in range(16):
            diff = [xi[c] - (pltpu.roll(xj[c], 8 * k, 1) if k else xj[c]) for c in range(3)]
            dist = diff[0] * diff[0] + diff[1] * diff[1] + diff[2] * diff[2]
            w = jnp.exp2(-dist)
            acc = [acc[c] + w * diff[c] for c in range(3)]
        for c in range(3):
            force_ref[p_local - 16, c] += acc[c]
        return carry

    lax.fori_loop(0, list_ref[4 + step, 0], body, 0)


def scatter(force_ref, rows_ref, lanes_ref, lhs_ref):
    for s in range(16):
        at = slice(128 * s, 128 * s + 128)
        hot = rows_ref[:, at].astype(F32)
        for c in range(3):
            f = jnp.sum(force_ref[s, c], axis=0, keepdims=True) * (1.0 / SCALE)
            hi, lo = split2(f)
            lhs_ref[96 * c : 96 * c + 96, at] = (hot * hi.astype(F32)).astype(BF16)
            lhs_ref[288 + 96 * c : 384 + 96 * c, at] = (hot * lo.astype(F32)).astype(BF16)
    out = lax.dot_general(
        lhs_ref[...], lanes_ref[...], (((1,), (1,)), ((), ())), preferred_element_type=F32
    )
    return out[:288] + out[288:]


def contact_kernel(list_ref, me_ref, all_ref, nodes_ref, *rest, steps, first_rows):
    outs = rest[: len(steps)]
    rows_ref, lanes_ref, lhs_ref, force_ref = rest[len(steps) :]
    one_hots(nodes_ref, rows_ref, lanes_ref)
    base = 16 * me_ref[0] - 16
    for step, first_row, out_ref in zip(steps, first_rows, outs):
        force_ref[...] = jnp.zeros_like(force_ref)
        pair_loop(list_ref, step, first_row, all_ref, base, force_ref)
        out_ref[...] = scatter(force_ref, rows_ref, lanes_ref, lhs_ref)


def contact(lists, me, everyone, nodes, steps, first_rows):
    return pl.pallas_call(
        functools.partial(contact_kernel, steps=steps, first_rows=first_rows),
        out_shape=[jax.ShapeDtypeStruct((288, 128), F32) for _ in steps],
        in_specs=[
            pl.BlockSpec(memory_space=pltpu.SMEM),
            pl.BlockSpec(memory_space=pltpu.SMEM),
            pl.BlockSpec(memory_space=pltpu.VMEM),
            pl.BlockSpec(memory_space=pltpu.VMEM),
        ],
        out_specs=[pl.BlockSpec(memory_space=pltpu.VMEM) for _ in steps],
        scratch_shapes=[
            pltpu.VMEM((96, 2048), BF16),
            pltpu.VMEM((128, 2048), BF16),
            pltpu.VMEM((576, 2048), BF16),
            pltpu.VMEM((16, 3, 8, 128), F32),
        ],
        compiler_params=PARAMS,
    )(lists, me, everyone, nodes)


def gather_kernel(disp_ref, coords_ref, nodes_ref, out_ref, rows_ref, lanes_ref):
    one_hots(nodes_ref, rows_ref, lanes_ref)
    hot = jnp.concatenate([rows_ref[...], rows_ref[...]], axis=0)
    for c in range(3):
        field = jnp.concatenate(list(split2(disp_ref[96 * c : 96 * c + 96, :])), axis=0)
        picked = lax.dot_general(field, hot, (((0,), (0,)), ((), ())), preferred_element_type=F32)
        value = jnp.sum(picked * lanes_ref[...].astype(F32), axis=0, keepdims=True)
        for s in range(16):
            row = value[:, 128 * s : 128 * s + 128] + coords_ref[3 * s + c : 3 * s + c + 1, :]
            for dest in range(8):
                out_ref[dest, 3 * s + c : 3 * s + c + 1, :] = row


def gather_positions(disp, coords, nodes):
    return pl.pallas_call(
        gather_kernel,
        out_shape=jax.ShapeDtypeStruct((8, 48, 128), F32),
        scratch_shapes=[pltpu.VMEM((96, 2048), BF16), pltpu.VMEM((128, 2048), BF16)],
        compiler_params=PARAMS,
    )(disp, coords, nodes)


def first_payload(surf_coords, routes, pairs, me):
    earlier = iota((16, 16), 0) > iota((16, 16), 1)
    same = routes[:, :, None] == routes[:, None, :]
    rank = jnp.sum(jnp.where(same & earlier[None], 1, 0), axis=2)
    keys = (routes * 32 + me * 4 + rank).astype(F32)
    keys = jnp.where((iota((4, 128), 1) // 16) == me, jnp.tile(keys, (1, 8)), 0.0)
    both = jnp.swapaxes(pairs[:, 0], 1, 2).reshape(4, 128).astype(F32)
    return jnp.concatenate([surf_coords.reshape(48, 128), keys, both], axis=0)


def exchange(blocks):
    return lax.all_to_all(blocks, "gz", split_axis=0, concat_axis=0, tiled=True)


def make_lists(everyone, me):
    return pl.pallas_call(
        functools.partial(plan_kernel, around=()),
        out_shape=jax.ShapeDtypeStruct((8, 512), jnp.int32),
        in_specs=[pl.BlockSpec(memory_space=pltpu.SMEM), pl.BlockSpec(memory_space=pltpu.VMEM)],
        compiler_params=PARAMS,
    )(me, everyone)


CORNERS = [(0, 0, 0), (0, 0, 1), (0, 1, 0), (0, 1, 1), (1, 0, 0), (1, 0, 1), (1, 1, 0), (1, 1, 1)]


def padded_2(x, sides, width):
    for axis, dim in sides:
        count, length = (lax.axis_size(axis), x.shape[dim])
        up = [(i, (i + 1) % count) for i in range(count - 1)]
        down = [(j, i) for i, j in up]
        last = lax.slice_in_dim(x, length - width, length, axis=dim)
        first = lax.slice_in_dim(x, 0, width, axis=dim)
        before = lax.ppermute(last, axis, up)
        after = lax.ppermute(first, axis, down)
        x = jnp.concatenate([before, x, after], axis=dim)
    return x


def corner(field, offsets):
    size_x = field.shape[1] - 1
    size_y = field.shape[2] - 1
    size_z = field.shape[3] - 1
    return field[
        :,
        offsets[0] : offsets[0] + size_x,
        offsets[1] : offsets[1] + size_y,
        offsets[2] : offsets[2] + size_z,
    ]


def element_stress(disp, modulus):
    grads = []
    for axis in range(3):
        parts = []
        for first in (0, 1):
            for second in (0, 1):
                upper = [first, second]
                upper.insert(axis, 1)
                lower = [first, second]
                lower.insert(axis, 0)
                parts.append(corner(disp, upper) - corner(disp, lower))
        grads.append(0.25 * (parts[0] + parts[1] + parts[2] + parts[3]))
    strain_xx = grads[0][0]
    strain_yy = grads[1][1]
    strain_zz = grads[2][2]
    strain_xy = 0.5 * (grads[1][0] + grads[0][1])
    strain_yz = 0.5 * (grads[2][1] + grads[1][2])
    strain_zx = 0.5 * (grads[0][2] + grads[2][0])
    trace = strain_xx + strain_yy + strain_zz
    return jnp.stack(
        [
            modulus * (2.0 * strain_xx + trace),
            modulus * (2.0 * strain_yy + trace),
            modulus * (2.0 * strain_zz + trace),
            modulus * 2.0 * strain_xy,
            modulus * 2.0 * strain_yz,
            modulus * 2.0 * strain_zx,
        ]
    )


def node_forces(stress, load):
    rows = (
        (stress[0], stress[3], stress[5]),
        (stress[3], stress[1], stress[4]),
        (stress[5], stress[4], stress[2]),
    )
    total = jnp.float32(0.0)
    for offsets in CORNERS:
        signs = [2.0 * offsets[0] - 1.0, 2.0 * offsets[1] - 1.0, 2.0 * offsets[2] - 1.0]
        pieces = []
        for index in range(3):
            row = rows[index]
            pieces.append(
                -0.25 * (signs[0] * row[0] + signs[1] * row[1] + signs[2] * row[2])
                + 0.125 * load[index]
            )
        term = jnp.stack(pieces)
        total = total + jnp.pad(
            term,
            (
                (0, 0),
                (offsets[0], 1 - offsets[0]),
                (offsets[1], 1 - offsets[1]),
                (offsets[2], 1 - offsets[2]),
            ),
        )
    return total


def node_mass(density):
    share = 0.125 * density
    total = jnp.float32(0.0)
    for offsets in CORNERS:
        total = total + jnp.pad(
            share,
            (
                (offsets[0], 1 - offsets[0]),
                (offsets[1], 1 - offsets[1]),
                (offsets[2], 1 - offsets[2]),
            ),
        )
    return total


def element_mean(vel):
    total = jnp.float32(0.0)
    for offsets in CORNERS:
        total = total + corner(vel, offsets)
    return 0.125 * total


def fold_rim(padded, dim):
    length = padded.shape[dim]
    inner = lax.slice_in_dim(padded, 1, length - 1, axis=dim)
    lower = lax.slice_in_dim(padded, 0, 1, axis=dim)
    upper = lax.slice_in_dim(padded, length - 1, length, axis=dim)
    first = lax.slice_in_dim(inner, 0, 1, axis=dim) + lower
    middle = lax.slice_in_dim(inner, 1, length - 3, axis=dim)
    last = lax.slice_in_dim(inner, length - 3, length - 2, axis=dim) + upper
    return jnp.concatenate([first, middle, last], axis=dim)


def shared_sum(partial_value):
    padded = padded_2(partial_value, (("gx", 1), ("gy", 2), ("gz", 3)), 1)
    return fold_rim(fold_rim(fold_rim(padded, 1), 2), 3)


def owned(field):
    return field[:, :8, :12, :128].reshape(288, 128)


def partial_of(contact_rows):
    return jnp.pad(contact_rows.reshape(3, 8, 12, 128), ((0, 0), (0, 1), (0, 1), (0, 1)))


def per_device(stiffness, density, load, alive, surf_coords, surf_nodes, routes, pairs):
    me = lax.axis_index("gz")
    me_arr = jnp.reshape(me, (1,)).astype(jnp.int32)
    coords = surf_coords.reshape(48, 128)
    payload = first_payload(surf_coords, routes, pairs, me)
    everyone = exchange(jnp.broadcast_to(payload[None], (8,) + payload.shape))
    mass = shared_sum(node_mass(density)[None])[0]
    lists = make_lists(everyone, me_arr)
    c0, c1 = contact(lists, me_arr, everyone, surf_nodes, (0, 1), (0, 0))
    zero = jnp.zeros((6,) + stiffness.shape, F32)
    force = shared_sum(node_forces(zero, load) + partial_of(c0))
    vel = TIME_STEP * force / mass[None]
    disp1 = TIME_STEP * vel
    spots = exchange(gather_positions(owned(disp1), coords, surf_nodes))
    modulus = [stiffness * alive[t].astype(F32) for t in range(4)]
    force = shared_sum(node_forces(element_stress(disp1, modulus[1]), load) + partial_of(c1))
    vel = vel + TIME_STEP * force / mass[None]
    disp2 = disp1 + TIME_STEP * vel
    spots3 = exchange(gather_positions(owned(disp2), coords, surf_nodes))
    (c2,) = contact(lists, me_arr, spots, surf_nodes, (2,), (0,))
    force = shared_sum(node_forces(element_stress(disp2, modulus[2]), load) + partial_of(c2))
    vel = vel + TIME_STEP * force / mass[None]
    disp = disp2 + TIME_STEP * vel
    (c3,) = contact(lists, me_arr, spots3, surf_nodes, (3,), (0,))
    force = shared_sum(node_forces(element_stress(disp, modulus[3]), load) + partial_of(c3))
    vel = vel + TIME_STEP * force / mass[None]
    disp = disp + TIME_STEP * vel
    return (element_mean(vel), element_stress(disp, modulus[3]))


def solution(mesh):
    return jax.shard_map(
        per_device,
        mesh=mesh,
        in_specs=(
            P("gx", "gy", "gz"),
            P("gx", "gy", "gz"),
            P(None, "gx", "gy", "gz"),
            P(None, "gx", "gy", "gz"),
            P(("gx", "gy", "gz"), None, None),
            P(("gx", "gy", "gz"), None),
            P(None, ("gx", "gy", "gz")),
            P(None, ("gx", "gy", "gz"), None, None),
        ),
        out_specs=(P(None, "gx", "gy", "gz"), P(None, "gx", "gy", "gz")),
        check_vma=False,
    )
```

```python
import functools
import math
import jax
import jax.numpy as jnp
from jax import lax
from jax.experimental import pallas as pl
from jax.experimental.pallas import tpu as pltpu
from jax.sharding import PartitionSpec as P

F32 = jnp.float32
BF16 = jnp.bfloat16
SCALE = math.sqrt(math.log2(math.e) / 0.08)
DT = 0.2
PARAMS = pltpu.CompilerParams(vmem_limit_bytes=56 * 2**20)
VMEM = pl.BlockSpec(memory_space=pltpu.VMEM)
SMEM = pl.BlockSpec(memory_space=pltpu.SMEM)
KEYS, PAIRS, NODES, PLANES = 48, 52, 56, 72
ROWS_1 = 128
LATE, PLANES_2 = 48, 96
ROWS_2 = 144


def split2(x):
    hi = x.astype(BF16)
    return hi, (x - hi.astype(F32)).astype(BF16)


def iota(shape, dim):
    return lax.broadcasted_iota(jnp.int32, shape, dim)


def rim_lanes(shape):
    lane = iota(shape, len(shape) - 1)
    return (lane >= 126) | (lane < 3)


def roll_last(x, shift):
    shift = shift % x.shape[-1]
    return pltpu.roll(x, shift, x.ndim - 1) if shift else x


def pack(tiles):
    total = None
    for f, tile in enumerate(tiles):
        part = roll_last(jnp.where(rim_lanes(tile.shape), tile, 0.0), 8 * f)
        total = part if total is None else total + part
    return total


def unpack(packed, f):
    return jnp.where(rim_lanes(packed.shape), roll_last(packed, -8 * f), 0.0)


def both(main, rim):
    return jnp.concatenate([main, rim], axis=-1)


def fill16(x):
    pad = 16 - x.shape[-2]
    if not pad:
        return x
    return jnp.concatenate([x, jnp.zeros(x.shape[:-2] + (pad, x.shape[-1]), x.dtype)], axis=-2)


def next_y(x):
    return pltpu.roll(x, x.shape[1] - 1, 1)


def prev_y(x):
    return pltpu.roll(x, 1, 1)


def next_z(x):
    return roll_last(x, -1)


def prev_z(x):
    return roll_last(x, 1)


def planes_to_rows(packed, square_ref, count):
    square_ref[...] = jnp.zeros_like(square_ref)
    for i in range(packed.shape[0]):
        square_ref[13 * i : 13 * i + 13, :] = packed[i, 0:13, :]
    return jnp.transpose(roll_last(square_ref[...], 2))[0:count]


def rows_to_planes(rows, square_ref, planes):
    full = jnp.concatenate([rows, jnp.zeros((128 - rows.shape[0], 128), F32)], axis=0)
    square_ref[...] = roll_last(jnp.transpose(full), -2)
    return jnp.stack([fill16(square_ref[13 * i : 13 * i + 13, :]) for i in range(planes)])


def neighbour_planes(all_ref, first_row, count, me, last, square_ref, planes):
    low = all_ref[jnp.maximum(me - 1, 0), first_row : first_row + count, :]
    up = all_ref[jnp.minimum(me + 1, last), first_row : first_row + count, :]
    kind = iota((count, 128), 0) % 8
    low = jnp.where((kind < 2) & (me > 0), low, 0.0)
    up = jnp.where((kind >= 2) & (me < last), up, 0.0)
    return rows_to_planes(low + up, square_ref, planes)


def prep_kernel(coords_ref, rows_ref, nodes_ref, stiff_ref, dens_ref, load_ref, alive_ref, out_ref, square_ref):
    fields = [load_ref[0], load_ref[1], load_ref[2], dens_ref[...]]
    for step in (1, 2, 3):
        fields.append(stiff_ref[...] * alive_ref[step].astype(F32))
    rows = planes_to_rows(pack([fill16(f) for f in fields]), square_ref, 56)
    nodes = nodes_ref[...].astype(F32)
    for dest in range(8):
        out_ref[dest, 0:48, :] = coords_ref[...]
        out_ref[dest, 48:56, :] = rows_ref[...]
        out_ref[dest, 56:72, :] = nodes
        out_ref[dest, 72:128, :] = rows


def plan_kernel(me_ref, all_ref, list_ref):
    me = me_ref[0]
    lane = iota((1, 128), 1)
    block_of = iota((128, 128), 0).astype(F32)
    eye = iota((128, 128), 0) == iota((128, 128), 1)
    upper = (iota((128, 128), 0) < iota((128, 128), 1)).astype(BF16)
    place = iota((512, 128), 0).astype(F32)
    own, low, up0, up1 = [], [], [], []
    for src in range(8):
        ids = all_ref[src, NODES : NODES + 16, :]
        k = ids - 128.0 * jnp.floor(ids * (1.0 / 128.0))

        def some(want):
            return jnp.max(jnp.where(k == want, 1.0, 0.0), axis=1, keepdims=True)

        one = jnp.ones((16, 1), F32)
        own.append(one * jnp.where(me == src, 1.0, 0.0))
        low.append(some(127.0) * jnp.where(me == src + 1, 1.0, 0.0))
        is_up = jnp.where(me == src - 1, 1.0, 0.0)
        up0.append(some(0.0) * is_up)
        up1.append(some(1.0) * is_up)
    own, low, up0, up1 = [jnp.concatenate(x, axis=0) for x in (own, low, up0, up1)]
    allowed = [own + low + up0, own, own + low + jnp.maximum(up0, up1), own + up0]
    for step in range(4):
        keys = all_ref[0, KEYS + step : KEYS + 1 + step, :]
        for src in range(1, 8):
            keys = keys + all_ref[src, KEYS + step : KEYS + 1 + step, :]
        key_col = jnp.sum(jnp.where(eye, keys, 0.0), axis=1, keepdims=True)
        first_col = jnp.where(allowed[step] > 0.0, key_col, -1.0)
        base = jnp.zeros((1, 1), F32)
        total = jnp.zeros((8, 512), F32)
        for row in range(4):
            even = all_ref[2 * row, PAIRS + step : PAIRS + 1 + step, :]
            odd = all_ref[2 * row + 1, PAIRS + step : PAIRS + 1 + step, :]
            left = lane < 64
            first = jnp.where(left, even, pltpu.roll(odd, 64, 1))
            second = jnp.where(left, pltpu.roll(even, 64, 1), odd)
            box = jnp.where(left, 64.0 * row, 64.0 * row + 32.0)
            hit_first = first_col == first + box
            hit_second = key_col == second + box
            p_block = jnp.sum(jnp.where(hit_first, block_of, 0.0), axis=0, keepdims=True)
            r_block = jnp.sum(jnp.where(hit_second, block_of, 0.0), axis=0, keepdims=True)
            live = jnp.sum(jnp.where(hit_first, 1.0, 0.0), axis=0, keepdims=True) * jnp.sum(
                jnp.where(hit_second, 1.0, 0.0), axis=0, keepdims=True
            )
            p_slot = p_block - (16 * me - 16).astype(F32)
            mine = live > 0.0
            sel = jnp.where(mine, 1.0, 0.0)
            before = jnp.dot(
                jnp.broadcast_to(sel, (8, 128)).astype(BF16), upper, preferred_element_type=F32
            )[0:1]
            spot = jnp.where(mine, before + base, -1.0)
            base = base + jnp.sum(sel, axis=1, keepdims=True)
            onehot = jnp.where(place == spot, 1.0, 0.0).astype(BF16)
            codes = jnp.where(
                iota((8, 128), 0) == 0,
                jnp.broadcast_to(p_slot, (8, 128)),
                jnp.broadcast_to(r_block, (8, 128)),
            )
            codes = jnp.where(jnp.broadcast_to(mine, (8, 128)), codes, 0.0).astype(BF16)
            total = total + lax.dot_general(
                codes, onehot, (((1,), (1,)), ((), ())), preferred_element_type=F32
            )
        code = jnp.where(
            iota((1, 512), 1).astype(F32) < base, total[0:1] * 128.0 + total[1:2], 48.0 * 128.0
        )
        list_ref[step : step + 1, :] = code.astype(jnp.int32)
        list_ref[4 + step : 5 + step, :] = jnp.broadcast_to(base, (1, 512)).astype(jnp.int32)


UNROLL = 4


def fill_table(all_ref, first_row, table_ref):
    def body(src, carry):
        for row in range(48):
            wide = jnp.broadcast_to(all_ref[src, first_row + row : first_row + row + 1, :] * SCALE, (8, 128))
            table_ref[src * 16 + row // 3, row % 3] = pltpu.roll(wide, 0, 1, stride=1, stride_axis=0)
        return carry

    lax.fori_loop(0, 8, body, 0)


def pair_loop(list_ref, step, me, table_ref, force_ref):
    force_ref[...] = jnp.zeros_like(force_ref)

    def one(q):
        code = list_ref[step, q]
        slot = lax.shift_right_logical(code, 7)
        r = code & 127
        p = jnp.minimum(slot + (16 * me - 16), 127)
        xi = [jnp.broadcast_to(table_ref[p, c, 0:1, :], (8, 128)) for c in range(3)]
        xj = [table_ref[r, c] for c in range(3)]
        acc = [jnp.zeros((8, 128), F32)] * 3
        for k in range(16):
            diff = [xi[c] - roll_last(xj[c], 8 * k) for c in range(3)]
            dist = diff[0] * diff[0] + diff[1] * diff[1] + diff[2] * diff[2]
            w = jnp.exp2(-dist)
            acc = [acc[c] + w * diff[c] for c in range(3)]
        return slot, acc

    def body(g, carry):
        done = [one(g * UNROLL + u) for u in range(UNROLL)]
        for slot, acc in done:
            for c in range(3):
                force_ref[slot, c] += acc[c]
        return carry

    lax.fori_loop(0, (list_ref[4 + step, 0] + (UNROLL - 1)) // UNROLL, body, 0)


def row_and_lane(ids):
    line = jnp.floor(ids * (1.0 / 128.0))
    lane = ids - 128.0 * line
    i = jnp.floor((line + 0.5) * (1.0 / 12.0))
    return line + 4.0 * i, lane


def one_hot(at, rows=128):
    return jnp.where(iota((rows, 128), 0).astype(F32) == at, 1.0, 0.0)


def block_force(force_ref, slot, c):
    return jnp.sum(force_ref[slot, c], axis=0, keepdims=True) * (1.0 / SCALE)


def scatter_own(force_ref, all_ref, me, lhs_ref, lanes_ref):
    for s in range(16):
        at = slice(128 * s, 128 * s + 128)
        row, lane = row_and_lane(all_ref[me, NODES + s : NODES + s + 1, :])
        hot = one_hot(row)
        lanes_ref[:, at] = one_hot(lane).astype(BF16)
        for c in range(3):
            hi, lo = split2(block_force(force_ref, 16 + s, c))
            lhs_ref[128 * c : 128 * c + 128, at] = (hot * hi.astype(F32)).astype(BF16)
            lhs_ref[384 + 128 * c : 512 + 128 * c, at] = (hot * lo.astype(F32)).astype(BF16)
    out = lax.dot_general(
        lhs_ref[...], lanes_ref[...], (((1,), (1,)), ((), ())), preferred_element_type=F32
    )
    return (out[:384] + out[384:]).reshape(3, 8, 16, 128)


def scatter_rim(force_ref, all_ref, me, last, square_ref, low, ups):
    square_ref[...] = jnp.zeros_like(square_ref)
    sides = ([(jnp.maximum(me - 1, 0), 0, (127.0,))] if low else []) + [
        (jnp.minimum(me + 1, last), 32, ups)
    ]
    for src, first_slot, wants in sides:
        total = jnp.zeros((16, 128), F32)
        for s in range(16):
            row, lane = row_and_lane(all_ref[src, NODES + s : NODES + s + 1, :])
            hot = one_hot(row).astype(BF16)
            lines = []
            for want in wants:
                for c in range(3):
                    f = jnp.where(lane == want, block_force(force_ref, first_slot + s, c), 0.0)
                    lines.append(f)
            lines += [jnp.zeros((8 - len(lines), 128), F32)]
            hi, lo = split2(jnp.concatenate(lines, axis=0))
            total = total + lax.dot_general(
                jnp.concatenate([hi, lo], axis=0), hot, (((1,), (1,)), ((), ())), preferred_element_type=F32
            )
        summed = total[0:8] + total[8:16]
        for w, want in enumerate(wants):
            for c in range(3):
                at = int(want + 8 * c) % 128
                square_ref[at : at + 1, :] = summed[3 * w + c : 3 * w + c + 1]
    return jnp.transpose(square_ref[...]).reshape(8, 16, 128)


def node_sum(elements):
    e = 0.125 * elements
    e = e + prev_z(e)
    e = e + prev_y(e)
    zero = jnp.zeros((1,) + e.shape[1:], F32)
    return jnp.concatenate([e, zero], axis=0) + jnp.concatenate([zero, e], axis=0)


def first_contact_kernel(
    me_ref, list_ref, all_ref, load_ref, dens_ref, stiff_ref, alive_ref,
    fm_ref, c0_ref, m1_ref, up_ref, down_ref,
    table_ref, force_ref, lhs_ref, lanes_ref, square_ref,
):
    me, last = me_ref[0], 7
    planes = neighbour_planes(all_ref, PLANES, 56, me, last, square_ref, 8)
    fields = [load_ref[0], load_ref[1], load_ref[2], dens_ref[...]]
    sums = [node_sum(both(fill16(f), unpack(planes, n))) for n, f in enumerate(fields)]
    m1 = both(fill16(stiff_ref[...] * alive_ref[1].astype(F32)), unpack(planes, 4))
    m1_ref[...] = m1
    fill_table(all_ref, 0, table_ref)
    pair_loop(list_ref, 0, me, table_ref, force_ref)
    own = scatter_own(force_ref, all_ref, me, lhs_ref, lanes_ref)
    rim = scatter_rim(force_ref, all_ref, me, last, square_ref, True, (0.0,))
    zero = jnp.zeros((1, 16, 256), F32)
    for c in range(3):
        full = jnp.concatenate([both(own[c], unpack(rim, c)), zero], axis=0)
        c0_ref[c] = full
        sums[c] = sums[c] + full
    for n in range(4):
        fm_ref[n] = sums[n]
    ups = [s[7] for s in sums] + [s[8] for s in sums] + [m1[7]]
    downs = [s[0] for s in sums]
    send_planes(ups, up_ref)
    send_planes(downs, down_ref)


def send_planes(planes, out_ref):
    count = len(planes)
    for n, plane in enumerate(planes):
        out_ref[n] = plane[:, :128]
    for g in range(0, count, 16):
        out_ref[count + g // 16] = pack([p[:, 128:] for p in planes[g : g + 16]])


def get_plane(ref, n, count):
    return both(ref[n], unpack(ref[count + n // 16], n % 16))


def step_contact_kernel(me_ref, list_ref, all_ref, out_ref, table_ref, force_ref, lhs_ref, lanes_ref):
    me = me_ref[0]
    fill_table(all_ref, 0, table_ref)
    pair_loop(list_ref, 1, me, table_ref, force_ref)
    out_ref[...] = scatter_own(force_ref, all_ref, me, lhs_ref, lanes_ref)


def x_extended_1(fm_ref, m1_ref, ups_ref, downs_ref):
    out = []
    for n in range(4):
        own = fm_ref[n]
        low, add = get_plane(ups_ref, n, 9), get_plane(ups_ref, 4 + n, 9)
        high = get_plane(downs_ref, n, 4)
        out.append(
            jnp.concatenate([low[None], (own[0] + add)[None], own[1:8], (own[8] + high)[None]], axis=0)
        )
    m1 = jnp.concatenate(
        [get_plane(ups_ref, 8, 9)[None], m1_ref[...], jnp.zeros((1, 16, 256), F32)], axis=0
    )
    return out, m1


def rows16(x, j):
    return fill16(x[:, j, :])


def y_send_1_kernel(fm_ref, m1_ref, ups_ref, downs_ref, up_ref, down_ref):
    fields, m1 = x_extended_1(fm_ref, m1_ref, ups_ref, downs_ref)
    ups = [rows16(f, 11) for f in fields] + [rows16(f, 12) for f in fields] + [rows16(m1, 11)]
    send_planes(ups, up_ref)
    send_planes([rows16(f, 0) for f in fields], down_ref)


def stress_of(disp, modulus):
    grads = []
    for u in disp:
        s, d = u[1:] + u[:-1], u[1:] - u[:-1]
        sn = next_y(s)
        ss, sd = sn + s, sn - s
        ds = next_y(d) + d
        grads.append((ds + next_z(ds), sd + next_z(sd), next_z(ss) - ss))
    m = 0.25 * modulus
    exx, eyy, ezz = grads[0][0], grads[1][1], grads[2][2]
    trace = exx + eyy + ezz
    return (
        m * (2.0 * exx + trace),
        m * (2.0 * eyy + trace),
        m * (2.0 * ezz + trace),
        m * (grads[1][0] + grads[0][1]),
        m * (grads[2][1] + grads[1][2]),
        m * (grads[0][2] + grads[2][0]),
    )


def force_of(stress):
    xx, yy, zz, xy, yz, zx = stress
    out = []
    for a, b, c in ((xx, xy, zx), (xy, yy, yz), (zx, yz, zz)):
        az, bz, cz = a + prev_z(a), b + prev_z(b), prev_z(c) - c
        ay = az + prev_y(az)
        bc = (prev_y(bz) - bz) + (prev_y(cz) + cz)
        out.append(-0.25 * ((ay[:-1] - ay[1:]) + (bc[:-1] + bc[1:])))
    return out


def shift_rows(x, by):
    return pltpu.roll(x, by % x.shape[1], 1)


def gather_rows(disp, coords_ref, all_ids, lanes_ref, rows_ref):
    hot = rows_ref[...]
    values = []
    for c in range(3):
        hi, lo = split2(disp[c])
        field = jnp.concatenate([hi, lo], axis=0)
        picked = lax.dot_general(field, hot, (((0,), (0,)), ((), ())), preferred_element_type=F32)
        values.append(jnp.sum(picked * lanes_ref[...].astype(F32), axis=0, keepdims=True))
    return values


def second_step_kernel(
    flags_ref, fm_ref, c0_ref, m1_ref, xu_ref, xd_ref, yu_ref, yd_ref, c1_ref, coords_ref, nodes_ref,
    out_ref, state_ref, rows_ref, lanes_ref, square_ref,
):
    fields, m1 = x_extended_1(fm_ref, m1_ref, xu_ref, xd_ref)
    row = iota((10, 16, 256), 1)

    def extend(x, low, add, high):
        x = x + jnp.where(row == 0, add[:10, None, :], 0.0)
        if high is not None:
            x = x + jnp.where(row == 12, high[:10, None, :], 0.0)
        x = shift_rows(jnp.where(row < 13, x, 0.0), 1)
        return jnp.where(row == 0, low[:10, None, :], x)

    zero = jnp.zeros((16, 256), F32)
    fields = [
        extend(fields[n], get_plane(yu_ref, n, 9), get_plane(yu_ref, 4 + n, 9), get_plane(yd_ref, n, 4))
        for n in range(4)
    ]
    m1 = extend(m1, get_plane(yu_ref, 8, 9), zero, None)
    mass = fields[3]
    inv = jnp.where(mass > 0.0, DT / jnp.where(mass > 0.0, mass, 1.0), 0.0)
    disp1 = [DT * (inv * fields[c]) for c in range(3)]
    edge = jnp.zeros((1, 16, 256), F32)
    force = force_of([jnp.concatenate([x, edge], axis=0) for x in stress_of(disp1, m1[:9])])
    inv9 = inv[1:]
    flag_z = flags_ref[2]
    lane = iota((9, 16, 256), 2)
    rowj = iota((9, 16, 256), 1)
    packs = []
    disp2s, vel2s = [], []
    for c in range(3):
        c1 = jnp.concatenate([c1_ref[c], jnp.zeros((1, 16, 128), F32)], axis=0)
        c1 = shift_rows(both(c1, jnp.zeros((9, 16, 128), F32)), 1)
        c0 = shift_rows(c0_ref[c], 1)
        total = fields[c][1:]
        accel = inv9 * (total - c0)
        vel2 = inv9 * total + inv9 * force[c] + (accel + inv9 * c1)
        disp2 = disp1[c][1:] + DT * vel2
        good = (rowj > 0) & (rowj < 14)
        back = [shift_rows(jnp.where(good, x, 0.0), -1) for x in (disp2, vel2, accel)]
        disp2s.append(back[0])
        vel2s.append(back[1])
        state_ref[c] = back[0]
        state_ref[3 + c] = back[1]
        state_ref[6 + c] = back[2]
    state_ref[9] = shift_rows(jnp.where(good, inv9, 0.0), -1)
    for s in range(16):
        at = slice(128 * s, 128 * s + 128)
        r, l = row_and_lane(nodes_ref[s : s + 1, :].astype(F32))
        hot = one_hot(r).astype(BF16)
        rows_ref[0:128, at] = hot
        rows_ref[128:256, at] = hot
        lanes_ref[:, at] = one_hot(l).astype(BF16)
    for first, disp in (
        (0, [shift_rows(d[1:9], -1)[:, :, :128] for d in disp1]),
        (LATE, [d[0:8, :, :128] for d in disp2s]),
    ):
        values = gather_rows([d.reshape(128, 128) for d in disp], None, None, lanes_ref, rows_ref)
        for s in range(16):
            for c in range(3):
                line = values[c][:, 128 * s : 128 * s + 128] + coords_ref[3 * s + c : 3 * s + c + 1, :]
                for dest in range(8):
                    out_ref[dest, first + 3 * s + c : first + 3 * s + c + 1, :] = line
    rows = planes_to_rows(pack([x[:, :, :128] for x in disp2s + vel2s]), square_ref, 48)
    for dest in range(8):
        out_ref[dest, PLANES_2:ROWS_2, :] = rows


UPS = 13
DOWNS = 23


def late_contact_kernel(
    me_ref, list_ref, first_ref, all_ref, state_ref, stiff_ref, alive_ref,
    own_ref, up_ref, down_ref,
    table_ref, force_ref, lhs_ref, lanes_ref, square_ref,
):
    me, last = me_ref[0], 7
    zplanes = neighbour_planes(all_ref, PLANES_2, 48, me, last, square_ref, 9)
    mplanes = neighbour_planes(first_ref, PLANES, 56, me, last, square_ref, 8)
    at_last = me == last
    lane = iota((9, 16, 128), 2)
    inv = state_ref[9]
    zero = jnp.zeros((1, 16, 256), F32)

    def with_rim(own, n):
        rim = jnp.where((lane == 0) & at_last, own[:, :, 128:], unpack(zplanes, n))
        return both(own[:, :, :128], rim)

    contacts = []
    for step, first_row, low, ups in ((2, 0, True, (0.0, 1.0)), (3, LATE, False, (0.0,))):
        fill_table(all_ref, first_row, table_ref)
        pair_loop(list_ref, step, me, table_ref, force_ref)
        own = scatter_own(force_ref, first_ref, me, lhs_ref, lanes_ref)
        rim = scatter_rim(force_ref, first_ref, me, last, square_ref, low, ups)
        contacts.append(
            [jnp.concatenate([both(own[c], unpack(rim, c)), zero], axis=0) for c in range(3)]
        )
    for c in range(3):
        own_ref[c] = with_rim(state_ref[c], c)
        own_ref[3 + c] = with_rim(state_ref[3 + c], 3 + c) + state_ref[6 + c] + inv * contacts[0][c]
        own_ref[6 + c] = state_ref[6 + c] + inv * contacts[1][c]
    own_ref[9] = inv
    for n, step in ((10, 2), (11, 3)):
        m = both(fill16(stiff_ref[...] * alive_ref[step].astype(F32)), unpack(mplanes, 3 + step))
        own_ref[n] = jnp.concatenate([m, zero], axis=0)
    send_planes([own_ref[n, i] for n, i in UP_LIST], up_ref)
    send_planes([own_ref[n, i] for n, i in DOWN_LIST(0)], down_ref)


UP_LIST = (
    [(n, 6) for n in range(3)] + [(n, 7) for n in range(3)] + [(n, 7) for n in (3, 4, 5, 9)]
    + [(10, 6), (10, 7), (11, 7)]
)


def DOWN_LIST(base):
    return (
        [(n, p) for p in (0, 1, 2) for n in range(3)]
        + [(n, p) for p in (0, 1) for n in (3, 4, 5)]
        + [(n, 0) for n in (6, 7, 8)]
        + [(9, 0), (9, 1), (10, 0), (10, 1), (11, 0)]
    )


def UP_PLANE(n, i):
    return UP_LIST.index((n, i)) if (n, i) in UP_LIST else None


def DOWN_PLANE(n, i):
    lst = DOWN_LIST(0)
    return lst.index((n, i)) if (n, i) in lst else None


def x_extended_2(own_ref, ups_ref, downs_ref, at_last):
    zero = jnp.zeros((16, 256), F32)
    out = []
    for n in range(12):
        planes = []
        for i in (6, 7):
            at = UP_PLANE(n, i)
            planes.append(zero if at is None else get_plane(ups_ref, at, UPS))
        own = own_ref[n]
        for i in range(8):
            planes.append(own[i])
        for i in range(3):
            at = DOWN_PLANE(n, i)
            got = zero if at is None else get_plane(downs_ref, at, DOWNS)
            if i == 0:
                got = jnp.where(at_last, own[8], got)
            planes.append(got)
        out.append(jnp.stack(planes))
    return out


def y_send_2_kernel(flags_ref, own_ref, ups_ref, downs_ref, up_ref, down_ref):
    fields = x_extended_2(own_ref, ups_ref, downs_ref, flags_ref[0] > 0)
    up_list = [(n, j + 4) for n, j in UP_LIST]
    send_planes([fill16(fields[n][:, j, :]) for n, j in up_list], up_ref)
    send_planes([fill16(fields[n][:, j, :]) for n, j in DOWN_LIST(0)], down_ref)


def last_kernel(
    flags_ref, own_ref, xu_ref, xd_ref, yu_ref, yd_ref, vel_ref, stress_ref
):
    fields = x_extended_2(own_ref, xu_ref, xd_ref, flags_ref[0] > 0)
    y_last = flags_ref[1] > 0
    row = iota((13, 24, 256), 1)
    wide = []
    for n in range(12):
        x = jnp.concatenate([fields[n], jnp.zeros((13, 8, 256), F32)], axis=1)
        keep = (row < 12) | ((row == 12) & y_last)
        x = shift_rows(jnp.where(keep, x, 0.0), 2)
        for t, j in enumerate((6, 7)):
            at = UP_PLANE(n, j)
            if at is not None:
                x = x + jnp.where(row == t, get_plane(yu_ref, at, UPS)[:13, None, :], 0.0)
        for t in range(3):
            at = DOWN_PLANE(n, t)
            if at is not None:
                x = x + jnp.where(row == 14 + t, get_plane(yd_ref, at, DOWNS)[:13, None, :], 0.0)
        wide.append(x)
    disp2, vh3, g3, inv, m2, m3 = wide[0:3], wide[3:6], wide[6:9], wide[9], wide[10], wide[11]
    force = force_of(stress_of(disp2, m2[:12]))
    vel3 = [vh3[c][1:12] + inv[1:12] * force[c] for c in range(3)]
    disp3 = [disp2[c][1:12] + DT * vel3[c] for c in range(3)]
    force = force_of(stress_of(disp3, m3[1:11]))
    vel4 = [vel3[c][1:10] + (inv[2:11] * force[c] + g3[c][2:11]) for c in range(3)]
    disp4 = [disp3[c][1:10] + DT * vel4[c] for c in range(3)]
    stress = stress_of(disp4, m3[2:10])
    for n in range(6):
        stress_ref[n] = stress[n][:, 2:14, :128]
    for c in range(3):
        s = vel4[c][1:] + vel4[c][:-1]
        s = s + next_y(s)
        s = s + next_z(s)
        vel_ref[c] = 0.125 * s[:, 2:14, :128]


def call(kernel, outs, specs, scratch=()):
    return pl.pallas_call(
        kernel,
        out_shape=[jax.ShapeDtypeStruct(s, d) for s, d in outs],
        in_specs=specs,
        out_specs=[VMEM] * len(outs),
        scratch_shapes=list(scratch),
        compiler_params=PARAMS,
    )


def small_rows(routes, pairs, me):
    earlier = iota((16, 16), 0) > iota((16, 16), 1)
    same = routes[:, :, None] == routes[:, None, :]
    rank = jnp.sum(jnp.where(same & earlier[None], 1, 0), axis=2)
    keys = (routes * 32 + me * 4 + rank).astype(F32)
    keys = jnp.where((iota((4, 128), 1) // 16) == me, jnp.tile(keys, (1, 8)), 0.0)
    both_lists = jnp.swapaxes(pairs[:, 0], 1, 2).reshape(4, 128).astype(F32)
    return jnp.concatenate([keys, both_lists], axis=0)


def share(blocks):
    return lax.all_to_all(blocks, "gz", split_axis=0, concat_axis=0, tiled=True)


def neighbours(up, down, axis):
    count = lax.axis_size(axis)
    ahead = [(i, i + 1) for i in range(count - 1)]
    return lax.ppermute(up, axis, ahead), lax.ppermute(down, axis, [(j, i) for i, j in ahead])


TABLE = pltpu.VMEM((128, 3, 8, 128), F32)
FORCE = pltpu.VMEM((49, 3, 8, 128), F32)
LHS = pltpu.VMEM((768, 2048), BF16)
LANES = pltpu.VMEM((128, 2048), BF16)
SQUARE = pltpu.VMEM((128, 128), F32)


def per_device(stiffness, density, load, alive, surf_coords, surf_nodes, routes, pairs):
    index = [lax.axis_index(a) for a in ("gx", "gy", "gz")]
    me = jnp.reshape(index[2], (1,)).astype(jnp.int32)
    flags = jnp.stack(
        [(i == lax.axis_size(a) - 1).astype(jnp.int32) for i, a in zip(index, ("gx", "gy", "gz"))]
    )
    coords = surf_coords.reshape(48, 128)
    rows = small_rows(routes, pairs, index[2])
    (payload,) = call(prep_kernel, [((8, ROWS_1, 128), F32)], [VMEM] * 7, [SQUARE])(
        coords, rows, surf_nodes, stiffness, density, load, alive
    )
    everyone = share(payload)
    (lists,) = call(plan_kernel, [((8, 512), jnp.int32)], [SMEM, VMEM])(me, everyone)
    fm, c0, m1, up, down = call(
        first_contact_kernel,
        [((4, 9, 16, 256), F32), ((3, 9, 16, 256), F32), ((8, 16, 256), F32), ((10, 16, 128), F32),
         ((5, 16, 128), F32)],
        [SMEM, SMEM] + [VMEM] * 5,
        [TABLE, FORCE, LHS, LANES, SQUARE],
    )(me, lists, everyone, load, density, stiffness, alive)
    xu, xd = neighbours(up, down, "gx")
    (c1,) = call(
        step_contact_kernel, [((3, 8, 16, 128), F32)], [SMEM, SMEM, VMEM], [TABLE, FORCE, LHS, LANES]
    )(me, lists, everyone)
    up, down = call(y_send_1_kernel, [((10, 16, 128), F32), ((5, 16, 128), F32)], [VMEM] * 4)(
        fm, m1, xu, xd
    )
    yu, yd = neighbours(up, down, "gy")
    payload, state = call(
        second_step_kernel,
        [((8, ROWS_2, 128), F32), ((10, 9, 16, 256), F32)],
        [SMEM] + [VMEM] * 10,
        [pltpu.VMEM((256, 2048), BF16), LANES, SQUARE],
    )(flags, fm, c0, m1, xu, xd, yu, yd, c1, coords, surf_nodes)
    late = share(payload)
    own, up, down = call(
        late_contact_kernel,
        [((12, 9, 16, 256), F32), ((UPS + 1, 16, 128), F32), ((DOWNS + 2, 16, 128), F32)],
        [SMEM, SMEM] + [VMEM] * 5,
        [TABLE, FORCE, LHS, LANES, SQUARE],
    )(me, lists, everyone, late, state, stiffness, alive)
    xu, xd = neighbours(up, down, "gx")
    up, down = call(
        y_send_2_kernel,
        [((UPS + 1, 16, 128), F32), ((DOWNS + 2, 16, 128), F32)],
        [SMEM] + [VMEM] * 3,
    )(flags, own, xu, xd)
    yu, yd = neighbours(up, down, "gy")
    vel, stress = call(
        last_kernel,
        [((3, 8, 12, 128), F32), ((6, 8, 12, 128), F32)],
        [SMEM] + [VMEM] * 5,
    )(flags, own, xu, xd, yu, yd)
    return vel, stress


def solution(mesh):
    return jax.shard_map(
        per_device,
        mesh=mesh,
        in_specs=(
            P("gx", "gy", "gz"),
            P("gx", "gy", "gz"),
            P(None, "gx", "gy", "gz"),
            P(None, "gx", "gy", "gz"),
            P(("gx", "gy", "gz"), None, None),
            P(("gx", "gy", "gz"), None),
            P(None, ("gx", "gy", "gz")),
            P(None, ("gx", "gy", "gz"), None, None),
        ),
        out_specs=(P(None, "gx", "gy", "gz"), P(None, "gx", "gy", "gz")),
        check_vma=False,
    )
```

```python
import functools
import math
import jax
import jax.numpy as jnp
from jax import lax
from jax.experimental import pallas as pl
from jax.experimental.pallas import tpu as pltpu
from jax.sharding import PartitionSpec as P

F32 = jnp.float32
BF16 = jnp.bfloat16
SCALE = math.sqrt(math.log2(math.e) / 0.08)
DT = 0.2
PARAMS = pltpu.CompilerParams(vmem_limit_bytes=56 * 2**20)
VMEM = pl.BlockSpec(memory_space=pltpu.VMEM)
SMEM = pl.BlockSpec(memory_space=pltpu.SMEM)
KEYS, PAIRS, NODES, PLANES = 48, 52, 56, 72
ROWS_1 = 104
LATE, PLANES_2 = 48, 96
ROWS_2 = 128
PLANE_ROWS = 32


def split2(x):
    hi = x.astype(BF16)
    return hi, (x - hi.astype(F32)).astype(BF16)


def iota(shape, dim):
    return lax.broadcasted_iota(jnp.int32, shape, dim)


def rim_lanes(shape, above=3):
    lane = iota(shape, len(shape) - 1)
    return (lane >= 126) | (lane < above)


def roll_last(x, shift):
    shift = shift % x.shape[-1]
    return pltpu.roll(x, shift, x.ndim - 1) if shift else x


def pack(tiles, stride=8):
    total = None
    for f, tile in enumerate(tiles):
        part = roll_last(jnp.where(rim_lanes(tile.shape, min(stride - 2, 3)), tile, 0.0), stride * f)
        total = part if total is None else total + part
    return total


def unpack(packed, f, stride=8):
    return jnp.where(
        rim_lanes(packed.shape, min(stride - 2, 3)), roll_last(packed, -stride * f), 0.0
    )


def both(main, rim):
    return jnp.concatenate([main, rim], axis=-1)


def fill16(x):
    pad = 16 - x.shape[-2]
    if not pad:
        return x
    return jnp.concatenate([x, jnp.zeros(x.shape[:-2] + (pad, x.shape[-1]), x.dtype)], axis=-2)


def next_x(x):
    return pltpu.roll(x, x.shape[1] - 1, 1)


def prev_x(x):
    return pltpu.roll(x, 1, 1)


def next_z(x):
    return roll_last(x, -1)


def prev_z(x):
    return roll_last(x, 1)


def planes_to_rows(packed, square_ref):
    square_ref[...] = jnp.zeros_like(square_ref)
    for j in range(packed.shape[0]):
        square_ref[9 * j : 9 * j + 9, :] = packed[j, 0:9, :]
    return jnp.transpose(roll_last(square_ref[...], 2))[0:PLANE_ROWS]


def rows_to_planes(rows, square_ref, planes):
    full = jnp.concatenate([rows, jnp.zeros((128 - PLANE_ROWS, 128), F32)], axis=0)
    square_ref[...] = roll_last(jnp.transpose(full), -2)
    return jnp.stack([fill16(square_ref[9 * j : 9 * j + 9, :]) for j in range(planes)])


def neighbour_planes(all_ref, first_row, stride, me, square_ref, planes):
    low = all_ref[jnp.maximum(me - 1, 0), first_row : first_row + PLANE_ROWS, :]
    up = all_ref[jnp.minimum(me + 1, 7), first_row : first_row + PLANE_ROWS, :]
    kind = iota((PLANE_ROWS, 128), 0) % stride
    low = jnp.where((kind < 2) & (me > 0), low, 0.0)
    up = jnp.where((kind >= 2) & (me < 7), up, 0.0)
    return rows_to_planes(low + up, square_ref, planes)


def spread(x, first):
    to = (iota((x.shape[1], 128), 1) == iota((x.shape[1], 128), 0) + first).astype(BF16)
    return jnp.dot(x.astype(BF16), to, preferred_element_type=F32)


def prep_kernel(
    at_ref, coords_ref, routes_ref, pairs_ref, nodes_ref, stiff_ref, dens_ref, load_ref, alive_ref,
    out_ref, square_ref,
):
    me = at_ref[2]
    fields = [load_ref[0], load_ref[1], load_ref[2], dens_ref[...]]
    for step in (1, 2, 3):
        fields.append(stiff_ref[...] * alive_ref[step].astype(F32))
    rows = planes_to_rows(pack([fill16(f) for f in fields], 4), square_ref)
    nodes = nodes_ref[...].astype(F32)
    routes = routes_ref[...].astype(F32)
    rank = jnp.zeros((4, 16), F32)
    later = iota((4, 16), 1)
    for s in range(15):
        same = jnp.broadcast_to(routes[:, s : s + 1], (4, 16)) == routes
        rank = rank + jnp.where(same & (later > s), 1.0, 0.0)
    keys = spread(routes * 32.0 + rank + 4.0 * me.astype(F32), 16 * me)
    lists = spread(pairs_ref[:, 0, :].astype(F32), 0) + spread(pairs_ref[:, 1, :].astype(F32), 64)
    for dest in range(8):
        for c in range(3):
            out_ref[dest, 16 * c : 16 * c + 16, :] = coords_ref[c]
        out_ref[dest, KEYS : KEYS + 4, :] = keys
        out_ref[dest, PAIRS : PAIRS + 4, :] = lists
        out_ref[dest, NODES : NODES + 16, :] = nodes
        out_ref[dest, PLANES:ROWS_1, :] = rows


def plan_kernel(at_ref, all_ref, list_ref):
    me = at_ref[2]
    lane = iota((1, 128), 1)
    block_of = iota((128, 128), 0).astype(F32)
    eye = iota((128, 128), 0) == iota((128, 128), 1)
    upper = (iota((128, 128), 0) < iota((128, 128), 1)).astype(BF16)
    place = iota((128, 128), 0).astype(F32)
    own, low, up0, up1 = [], [], [], []
    for src in range(8):
        ids = all_ref[src, NODES : NODES + 16, :]
        k = ids - 128.0 * jnp.floor(ids * (1.0 / 128.0))

        def some(want):
            return jnp.max(jnp.where(k == want, 1.0, 0.0), axis=1, keepdims=True)

        one = jnp.ones((16, 1), F32)
        own.append(one * jnp.where(me == src, 1.0, 0.0))
        low.append(some(127.0) * jnp.where(me == src + 1, 1.0, 0.0))
        is_up = jnp.where(me == src - 1, 1.0, 0.0)
        up0.append(some(0.0) * is_up)
        up1.append(some(1.0) * is_up)
    own, low, up0, up1 = [jnp.concatenate(x, axis=0) for x in (own, low, up0, up1)]
    allowed = [own + low + up0, own, own + low + jnp.maximum(up0, up1), own + up0]
    for step in range(4):
        keys = all_ref[0, KEYS + step : KEYS + 1 + step, :]
        for src in range(1, 8):
            keys = keys + all_ref[src, KEYS + step : KEYS + 1 + step, :]
        key_col = jnp.sum(jnp.where(eye, keys, 0.0), axis=1, keepdims=True)
        first_col = jnp.where(allowed[step] > 0.0, key_col, -1.0)
        base = jnp.zeros((1, 1), F32)
        spots, codes = [], []
        for row in range(4):
            even = all_ref[2 * row, PAIRS + step : PAIRS + 1 + step, :]
            odd = all_ref[2 * row + 1, PAIRS + step : PAIRS + 1 + step, :]
            left = lane < 64
            first = jnp.where(left, even, pltpu.roll(odd, 64, 1))
            second = jnp.where(left, pltpu.roll(even, 64, 1), odd)
            box = jnp.where(left, 64.0 * row, 64.0 * row + 32.0)
            hit_first = first_col == first + box
            hit_second = key_col == second + box
            p_block = jnp.sum(jnp.where(hit_first, block_of, 0.0), axis=0, keepdims=True)
            r_block = jnp.sum(jnp.where(hit_second, block_of, 0.0), axis=0, keepdims=True)
            live = jnp.sum(jnp.where(hit_first, 1.0, 0.0), axis=0, keepdims=True) * jnp.sum(
                jnp.where(hit_second, 1.0, 0.0), axis=0, keepdims=True
            )
            p_slot = p_block - (16 * me - 16).astype(F32)
            mine = live > 0.0
            sel = jnp.where(mine, 1.0, 0.0)
            before = jnp.dot(
                jnp.broadcast_to(sel, (8, 128)).astype(BF16), upper, preferred_element_type=F32
            )[0:1]
            spots.append(jnp.where(mine, before + base, -1.0))
            base = base + jnp.sum(sel, axis=1, keepdims=True)
            code = jnp.where(
                iota((8, 128), 0) == 0,
                jnp.broadcast_to(p_slot, (8, 128)),
                jnp.broadcast_to(r_block, (8, 128)),
            )
            codes.append(jnp.where(jnp.broadcast_to(mine, (8, 128)), code, 0.0).astype(BF16))
        list_ref[4 + step : 5 + step, :] = jnp.broadcast_to(base, (1, 512)).astype(jnp.int32)
        count = jnp.max(base)
        for part in range(4):

            def write(part=part, spots=spots, codes=codes, base=base):
                total = jnp.zeros((8, 128), F32)
                for row in range(4):
                    onehot = jnp.where(place == spots[row] - 128.0 * part, 1.0, 0.0).astype(BF16)
                    total = total + lax.dot_general(
                        codes[row], onehot, (((1,), (1,)), ((), ())), preferred_element_type=F32
                    )
                used = (lane + 128 * part).astype(F32) < base
                code = jnp.where(used, total[0:1] * 128.0 + total[1:2], 48.0 * 128.0)
                list_ref[step : step + 1, 128 * part : 128 * part + 128] = code.astype(jnp.int32)

            if part == 0:
                write()
            else:
                pl.when(count + 8.0 > 128.0 * part)(write)


UNROLL = 8


def fill_table(all_ref, first_row, table_ref):
    def body(src, carry):
        for row in range(48):
            wide = jnp.broadcast_to(all_ref[src, first_row + row : first_row + row + 1, :] * SCALE, (8, 128))
            table_ref[src * 16 + row % 16, row // 16] = pltpu.roll(wide, 0, 1, stride=1, stride_axis=0)
        return carry

    lax.fori_loop(0, 8, body, 0)


def pair_loop(list_ref, step, me, table_ref, force_ref):
    force_ref[...] = jnp.zeros_like(force_ref)

    def one(q):
        code = list_ref[step, q]
        slot = lax.shift_right_logical(code, 7)
        r = code & 127
        p = jnp.minimum(slot + (16 * me - 16), 127)
        xi = [jnp.broadcast_to(table_ref[p, c, 0:1, :], (8, 128)) for c in range(3)]
        xj = [table_ref[r, c] for c in range(3)]
        acc = [jnp.zeros((8, 128), F32)] * 3
        for k in range(16):
            diff = [xi[c] - roll_last(xj[c], 8 * k) for c in range(3)]
            dist = diff[0] * diff[0] + diff[1] * diff[1] + diff[2] * diff[2]
            w = jnp.exp2(-dist)
            acc = [acc[c] + w * diff[c] for c in range(3)]
        return slot, acc

    def body(g, carry):
        done = [one(g * UNROLL + u) for u in range(UNROLL)]
        for slot, acc in done:
            for c in range(3):
                force_ref[slot, c] += acc[c]
        return carry

    lax.fori_loop(0, (list_ref[4 + step, 0] + (UNROLL - 1)) // UNROLL, body, 0)


def row_and_lane(ids):
    line = jnp.floor(ids * (1.0 / 128.0))
    lane = ids - 128.0 * line
    i = jnp.floor((line + 0.5) * (1.0 / 12.0))
    return 8.0 * line - 95.0 * i, lane


def one_hot(at, rows):
    return jnp.where(iota((rows, 128), 0).astype(F32) == at, 1.0, 0.0)


def block_force(force_ref, slot, c):
    return jnp.sum(force_ref[slot, c], axis=0, keepdims=True) * (1.0 / SCALE)


def scatter_own(force_ref, all_ref, me, lhs_ref, lanes_ref):
    for s in range(16):
        at = slice(128 * s, 128 * s + 128)
        row, lane = row_and_lane(all_ref[me, NODES + s : NODES + s + 1, :])
        hot = one_hot(row, 96)
        lanes_ref[:, at] = one_hot(lane, 128).astype(BF16)
        for c in range(3):
            hi, lo = split2(block_force(force_ref, 16 + s, c))
            lhs_ref[96 * c : 96 * c + 96, at] = (hot * hi.astype(F32)).astype(BF16)
            lhs_ref[288 + 96 * c : 384 + 96 * c, at] = (hot * lo.astype(F32)).astype(BF16)
    out = lax.dot_general(
        lhs_ref[...], lanes_ref[...], (((1,), (1,)), ((), ())), preferred_element_type=F32
    )
    return (out[:288] + out[288:]).reshape(3, 12, 8, 128)


def scatter_rim(force_ref, all_ref, me, square_ref, low, ups):
    square_ref[...] = jnp.zeros_like(square_ref)
    sides = ([(jnp.maximum(me - 1, 0), 0, (127.0,))] if low else []) + [
        (jnp.minimum(me + 1, 7), 32, ups)
    ]
    for src, first_slot, wants in sides:
        total = jnp.zeros((16, 128), F32)
        for s in range(16):
            row, lane = row_and_lane(all_ref[src, NODES + s : NODES + s + 1, :])
            hot = one_hot(row, 128).astype(BF16)
            lines = []
            for want in wants:
                for c in range(3):
                    f = jnp.where(lane == want, block_force(force_ref, first_slot + s, c), 0.0)
                    lines.append(f)
            lines += [jnp.zeros((8 - len(lines), 128), F32)]
            hi, lo = split2(jnp.concatenate(lines, axis=0))
            total = total + lax.dot_general(
                jnp.concatenate([hi, lo], axis=0), hot, (((1,), (1,)), ((), ())), preferred_element_type=F32
            )
        summed = total[0:8] + total[8:16]
        for w, want in enumerate(wants):
            for c in range(3):
                at = int(want + 8 * c) % 128
                square_ref[at : at + 1, :] = summed[3 * w + c : 3 * w + c + 1]
    return fill16(jnp.transpose(square_ref[...])[0:96].reshape(12, 8, 128))


def node_sum(elements):
    e = 0.125 * elements
    e = e + prev_z(e)
    e = e + prev_x(e)
    zero = jnp.zeros((1,) + e.shape[1:], F32)
    return jnp.concatenate([e, zero], axis=0) + jnp.concatenate([zero, e], axis=0)


def send_planes(planes, out_ref):
    count = len(planes)
    for n, plane in enumerate(planes):
        out_ref[n] = plane[:, :128]
    for g in range(0, count, 16):
        out_ref[count + g // 16] = pack([p[:, 128:] for p in planes[g : g + 16]])


def get_plane(ref, n, count):
    return both(ref[n], unpack(ref[count + n // 16], n % 16))


def row_plane(x, i):
    return fill16(x[:, i, :])


def first_contact_kernel(
    at_ref, list_ref, all_ref, load_ref, dens_ref, stiff_ref, alive_ref,
    fm_ref, c0_ref, m1_ref, up_ref, down_ref,
    table_ref, force_ref, lhs_ref, lanes_ref, square_ref,
):
    me = at_ref[2]
    planes = neighbour_planes(all_ref, PLANES, 4, me, square_ref, 12)
    fields = [load_ref[0], load_ref[1], load_ref[2], dens_ref[...]]
    sums = [node_sum(both(fill16(f), unpack(planes, n, 4))) for n, f in enumerate(fields)]
    m1 = both(fill16(stiff_ref[...] * alive_ref[1].astype(F32)), unpack(planes, 4, 4))
    zero = jnp.zeros((1, 16, 256), F32)
    m1 = jnp.concatenate([m1, zero], axis=0)
    m1_ref[...] = m1
    fm_ref[3] = sums[3]
    for c in range(3):
        fm_ref[c] = sums[c]
    fill_table(all_ref, 0, table_ref)
    pair_loop(list_ref, 0, me, table_ref, force_ref)
    own = scatter_own(force_ref, all_ref, me, lhs_ref, lanes_ref)
    rim = scatter_rim(force_ref, all_ref, me, square_ref, True, (0.0,))
    for c in range(3):
        full = jnp.concatenate([both(fill16(own[c]), unpack(rim, c)), zero], axis=0)
        c0_ref[c] = full
        fm_ref[c] = fm_ref[c] + full
    ups = [row_plane(fm_ref[n], 7) for n in range(4)] + [row_plane(fm_ref[n], 8) for n in range(4)]
    send_planes(ups + [row_plane(m1, 7)], up_ref)
    send_planes([row_plane(fm_ref[n], 0) for n in range(4)], down_ref)


def step_contact_kernel(at_ref, list_ref, all_ref, out_ref, table_ref, force_ref, lhs_ref, lanes_ref):
    me = at_ref[2]
    fill_table(all_ref, 0, table_ref)
    pair_loop(list_ref, 1, me, table_ref, force_ref)
    out_ref[...] = scatter_own(force_ref, all_ref, me, lhs_ref, lanes_ref)


def shift_rows(x, by):
    return pltpu.roll(x, by % x.shape[1], 1)


def x_extended_1(fm_ref, m1_ref, ups_ref, downs_ref, pick):
    lines = sorted(pick)
    row = iota((len(lines), 16, 256), 1)

    def lift(plane):
        return jnp.stack([jnp.broadcast_to(plane[j : j + 1], (16, 256)) for j in lines])

    def take(x):
        return jnp.stack([x[j] for j in lines])

    def extend(x, low, add, high):
        if add is not None:
            x = x + jnp.where(row == 0, lift(add), 0.0) + jnp.where(row == 8, lift(high), 0.0)
            x = jnp.where(row < 9, x, 0.0)
        else:
            x = jnp.where(row < 8, x, 0.0)
        return jnp.where(row == 0, lift(low), shift_rows(x, 1))

    out = [
        extend(
            take(fm_ref[n]),
            get_plane(ups_ref, n, 9),
            get_plane(ups_ref, 4 + n, 9),
            get_plane(downs_ref, n, 4),
        )
        for n in range(4)
    ]
    return out, extend(take(m1_ref[...]), get_plane(ups_ref, 8, 9), None, None)


def y_send_1_kernel(fm_ref, m1_ref, ups_ref, downs_ref, up_ref, down_ref):
    fields, m1 = x_extended_1(fm_ref, m1_ref, ups_ref, downs_ref, (0, 11, 12))
    send_planes([f[1] for f in fields] + [f[2] for f in fields] + [m1[1]], up_ref)
    send_planes([f[0] for f in fields], down_ref)


def stress_of(disp, modulus):
    grads = []
    for u in disp:
        s, d = u[1:] + u[:-1], u[1:] - u[:-1]
        sn = next_x(s)
        ss, xd = sn + s, sn - s
        yd = next_x(d) + d
        grads.append((xd + next_z(xd), yd + next_z(yd), next_z(ss) - ss))
    m = 0.25 * modulus
    exx, eyy, ezz = grads[0][0], grads[1][1], grads[2][2]
    trace = exx + eyy + ezz
    return (
        m * (2.0 * exx + trace),
        m * (2.0 * eyy + trace),
        m * (2.0 * ezz + trace),
        m * (grads[1][0] + grads[0][1]),
        m * (grads[2][1] + grads[1][2]),
        m * (grads[0][2] + grads[2][0]),
    )


def force_of(stress):
    xx, yy, zz, xy, yz, zx = stress
    out = []
    for a, b, c in ((xx, xy, zx), (xy, yy, yz), (zx, yz, zz)):
        az, bz, cz = a + prev_z(a), b + prev_z(b), prev_z(c) - c
        ac = (prev_x(az) - az) + (prev_x(cz) + cz)
        by = prev_x(bz) + bz
        out.append(-0.25 * ((ac[:-1] + ac[1:]) + (by[:-1] - by[1:])))
    return out


def gather_rows(disp, lanes_ref, rows_ref):
    hot = rows_ref[...]
    values = []
    for c in range(3):
        hi, lo = split2(disp[c])
        field = jnp.concatenate([hi, lo], axis=0)
        picked = lax.dot_general(field, hot, (((0,), (0,)), ((), ())), preferred_element_type=F32)
        values.append(jnp.sum(picked * lanes_ref[...].astype(F32), axis=0, keepdims=True))
    return values


def second_step_kernel(
    fm_ref, c0_ref, m1_ref, xu_ref, xd_ref, yu_ref, yd_ref, c1_ref, coords_ref, nodes_ref,
    out_ref, state_ref, rows_ref, lanes_ref, square_ref,
):
    fields, m1 = x_extended_1(fm_ref, m1_ref, xu_ref, xd_ref, range(13))
    zero = jnp.zeros((1, 16, 256), F32)
    for n in range(4):
        low, add = get_plane(yu_ref, n, 9), get_plane(yu_ref, 4 + n, 9)
        own = fields[n]
        fields[n] = jnp.concatenate(
            [low[None], (own[0] + add)[None], own[1:12], (own[12] + get_plane(yd_ref, n, 4))[None]],
            axis=0,
        )
    m1 = jnp.concatenate([get_plane(yu_ref, 8, 9)[None], m1[:12]], axis=0)
    mass = fields[3]
    inv = jnp.where(mass > 0.0, DT / jnp.where(mass > 0.0, mass, 1.0), 0.0)
    disp1 = [DT * (inv * fields[c]) for c in range(3)]
    force = force_of([jnp.concatenate([x, zero], axis=0) for x in stress_of(disp1, m1)])
    inv = inv[1:]
    row = iota((13, 16, 256), 1)
    good = (row > 0) & (row < 10)
    disp2s, vel2s = [], []
    for c in range(3):
        c1 = jnp.concatenate([fill16(c1_ref[c]), jnp.zeros((1, 16, 128), F32)], axis=0)
        c1 = shift_rows(both(c1, jnp.zeros((13, 16, 128), F32)), 1)
        total = fields[c][1:]
        accel = inv * (total - shift_rows(c0_ref[c], 1))
        vel2 = inv * total + inv * force[c] + (accel + inv * c1)
        disp2 = disp1[c][1:] + DT * vel2
        back = [shift_rows(jnp.where(good, x, 0.0), -1) for x in (disp2, vel2, accel)]
        disp2s.append(back[0])
        vel2s.append(back[1])
        state_ref[c] = back[0]
        state_ref[3 + c] = back[1]
        state_ref[6 + c] = back[2]
    state_ref[9] = shift_rows(jnp.where(good, inv, 0.0), -1)
    for s in range(16):
        at = slice(128 * s, 128 * s + 128)
        r, l = row_and_lane(nodes_ref[s : s + 1, :].astype(F32))
        hot = one_hot(r, 96).astype(BF16)
        rows_ref[0:96, at] = hot
        rows_ref[96:192, at] = hot
        lanes_ref[:, at] = one_hot(l, 128).astype(BF16)
    for first, disp in (
        (0, [shift_rows(d[1:13], -1)[:, :8, :128] for d in disp1]),
        (LATE, [d[0:12, :8, :128] for d in disp2s]),
    ):
        values = gather_rows([d.reshape(96, 128) for d in disp], lanes_ref, rows_ref)
        for c in range(3):
            block = jnp.concatenate(
                [values[c][:, 128 * s : 128 * s + 128] for s in range(16)], axis=0
            ) + coords_ref[c]
            for dest in range(8):
                out_ref[dest, first + 16 * c : first + 16 * c + 16, :] = block
    rows = planes_to_rows(pack([x[:, :, :128] for x in disp2s + vel2s], 5), square_ref)
    for dest in range(8):
        out_ref[dest, PLANES_2:ROWS_2, :] = rows


UP_LIST = (
    [(n, 0) for n in range(3)] + [(n, 1) for n in range(3)] + [(n, 1) for n in (3, 4, 5, 9)]
    + [(10, 0), (10, 1), (11, 1)]
)
DOWN_LIST = (
    [(n, p) for p in (0, 1, 2) for n in range(3)]
    + [(n, p) for p in (0, 1) for n in (3, 4, 5)]
    + [(n, 0) for n in (6, 7, 8)]
    + [(9, 0), (9, 1), (10, 0), (10, 1), (11, 0)]
)
UPS, DOWNS = len(UP_LIST), len(DOWN_LIST)


def plane_of(ref, listed, n, p):
    return get_plane(ref, listed.index((n, p)), len(listed)) if (n, p) in listed else None


def late_contact_kernel(
    at_ref, list_ref, first_ref, all_ref, state_ref, stiff_ref, alive_ref,
    own_ref, up_ref, down_ref,
    table_ref, force_ref, lhs_ref, lanes_ref, square_ref,
):
    me = at_ref[2]
    zplanes = neighbour_planes(all_ref, PLANES_2, 5, me, square_ref, 13)
    mplanes = neighbour_planes(first_ref, PLANES, 4, me, square_ref, 12)
    top = (iota((13, 16, 128), 2) == 0) & (me == 7)
    zero = jnp.zeros((1, 16, 256), F32)

    def with_rim(own, n):
        return both(own[:, :, :128], jnp.where(top, own[:, :, 128:], unpack(zplanes, n, 5)))

    inv = state_ref[9]
    own_ref[9] = inv
    for c in range(3):
        own_ref[c] = with_rim(state_ref[c], c)
        own_ref[3 + c] = with_rim(state_ref[3 + c], 3 + c) + state_ref[6 + c]
        own_ref[6 + c] = state_ref[6 + c]
    for n, step in ((10, 2), (11, 3)):
        m = both(fill16(stiff_ref[...] * alive_ref[step].astype(F32)), unpack(mplanes, 3 + step, 4))
        own_ref[n] = jnp.concatenate([m, zero], axis=0)
    for step, first_row, low, ups, n in ((2, 0, True, (0.0, 1.0), 3), (3, LATE, False, (0.0,), 6)):
        fill_table(all_ref, first_row, table_ref)
        pair_loop(list_ref, step, me, table_ref, force_ref)
        own = scatter_own(force_ref, first_ref, me, lhs_ref, lanes_ref)
        rim = scatter_rim(force_ref, first_ref, me, square_ref, low, ups)
        for c in range(3):
            full = both(fill16(own[c]), unpack(rim, c))
            own_ref[n + c, 0:12] = own_ref[n + c, 0:12] + own_ref[9, 0:12] * full
    send_planes([row_plane(own_ref[n], 6 + p) for n, p in UP_LIST], up_ref)
    send_planes([row_plane(own_ref[n], p) for n, p in DOWN_LIST], down_ref)


def x_extended_2(own_ref, ups_ref, downs_ref, at_last, lines):
    row = iota((len(lines), 16, 256), 1)
    keep = (row < 8) | ((row == 8) & at_last)

    def lift(plane):
        return jnp.stack([jnp.broadcast_to(plane[j : j + 1], (16, 256)) for j in lines])

    out = []
    for n in range(12):
        x = jnp.stack([own_ref[n, j] for j in lines])
        x = shift_rows(jnp.where(keep, x, 0.0), 2)
        for ref, listed, first, count in ((ups_ref, UP_LIST, 0, 2), (downs_ref, DOWN_LIST, 10, 3)):
            for p in range(count):
                got = plane_of(ref, listed, n, p)
                if got is not None:
                    add = lift(got)
                    if first + p == 10:
                        x = jnp.where((row == 10) & jnp.logical_not(at_last), add, x)
                    else:
                        x = jnp.where(row == first + p, add, x)
        out.append(x)
    return out


def y_send_2_kernel(at_ref, own_ref, ups_ref, downs_ref, up_ref, down_ref):
    fields = x_extended_2(own_ref, ups_ref, downs_ref, at_ref[0] == 7, (0, 1, 2, 10, 11))
    send_planes([fields[n][3 + p] for n, p in UP_LIST], up_ref)
    send_planes([fields[n][p] for n, p in DOWN_LIST], down_ref)


def last_kernel(at_ref, own_ref, xu_ref, xd_ref, yu_ref, yd_ref, vel_ref, stress_ref):
    fields = x_extended_2(own_ref, xu_ref, xd_ref, at_ref[0] == 7, range(13))
    y_last = at_ref[1] == 3
    none = jnp.zeros((16, 256), F32)
    wide = []
    for n in range(12):
        planes = [plane_of(yu_ref, UP_LIST, n, p) for p in (0, 1)]
        planes += [fields[n][j] for j in range(12)]
        after = [plane_of(yd_ref, DOWN_LIST, n, p) for p in (0, 1, 2)]
        after = [none if p is None else p for p in after]
        after[0] = jnp.where(y_last, fields[n][12], after[0])
        planes = [none if p is None else p for p in planes] + after
        wide.append(jnp.stack(planes))
    disp2, vh3, g3, inv, m2, m3 = wide[0:3], wide[3:6], wide[6:9], wide[9], wide[10], wide[11]
    force = force_of(stress_of(disp2, m2[:16]))
    vel3 = [vh3[c][1:16] + inv[1:16] * force[c] for c in range(3)]
    disp3 = [disp2[c][1:16] + DT * vel3[c] for c in range(3)]
    force = force_of(stress_of(disp3, m3[1:15]))
    vel4 = [vel3[c][1:14] + (inv[2:15] * force[c] + g3[c][2:15]) for c in range(3)]
    disp4 = [disp3[c][1:14] + DT * vel4[c] for c in range(3)]
    stress = stress_of(disp4, m3[2:14])
    for n in range(6):
        stress_ref[n] = shift_rows(stress[n][:, :, :128], -2)[:, :8, :]
    for c in range(3):
        s = vel4[c][1:] + vel4[c][:-1]
        s = s + next_x(s)
        s = s + next_z(s)
        vel_ref[c] = shift_rows(0.125 * s[:, :, :128], -2)[:, :8, :]


def call(kernel, outs, specs, scratch=()):
    return pl.pallas_call(
        kernel,
        out_shape=[jax.ShapeDtypeStruct(s, d) for s, d in outs],
        in_specs=specs,
        out_specs=[VMEM] * len(outs),
        scratch_shapes=list(scratch),
        compiler_params=PARAMS,
    )


def share(blocks):
    return lax.all_to_all(blocks, "gz", split_axis=0, concat_axis=0, tiled=True)


def neighbours(up, down, axis):
    count = lax.axis_size(axis)
    ahead = [(i, i + 1) for i in range(count - 1)]
    return lax.ppermute(up, axis, ahead), lax.ppermute(down, axis, [(j, i) for i, j in ahead])


TABLE = pltpu.VMEM((128, 3, 8, 128), F32)
FORCE = pltpu.VMEM((49, 3, 8, 128), F32)
LHS = pltpu.VMEM((576, 2048), BF16)
LANES = pltpu.VMEM((128, 2048), BF16)
SQUARE = pltpu.VMEM((128, 128), F32)


def per_device(stiffness, density, load, alive, surf_coords, surf_nodes, routes, pairs):
    at = jnp.stack([lax.axis_index(a) for a in ("gx", "gy", "gz")]).astype(jnp.int32)
    stiffness, density = jnp.swapaxes(stiffness, 0, 1), jnp.swapaxes(density, 0, 1)
    load, alive = jnp.swapaxes(load, 1, 2), jnp.swapaxes(alive, 1, 2)
    coords = jnp.swapaxes(surf_coords, 0, 1)
    pairs = jnp.swapaxes(pairs[:, 0], 1, 2)
    (payload,) = call(prep_kernel, [((8, ROWS_1, 128), F32)], [SMEM] + [VMEM] * 8, [SQUARE])(
        at, coords, routes, pairs, surf_nodes, stiffness, density, load, alive
    )
    everyone = share(payload)
    (lists,) = call(plan_kernel, [((8, 512), jnp.int32)], [SMEM, VMEM])(at, everyone)
    fm, c0, m1, up, down = call(
        first_contact_kernel,
        [((4, 13, 16, 256), F32), ((3, 13, 16, 256), F32), ((13, 16, 256), F32), ((10, 16, 128), F32),
         ((5, 16, 128), F32)],
        [SMEM, SMEM] + [VMEM] * 5,
        [TABLE, FORCE, LHS, LANES, SQUARE],
    )(at, lists, everyone, load, density, stiffness, alive)
    xu, xd = neighbours(up, down, "gx")
    (c1,) = call(
        step_contact_kernel, [((3, 12, 8, 128), F32)], [SMEM, SMEM, VMEM], [TABLE, FORCE, LHS, LANES]
    )(at, lists, everyone)
    up, down = call(y_send_1_kernel, [((10, 16, 128), F32), ((5, 16, 128), F32)], [VMEM] * 4)(
        fm, m1, xu, xd
    )
    yu, yd = neighbours(up, down, "gy")
    payload, state = call(
        second_step_kernel,
        [((8, ROWS_2, 128), F32), ((10, 13, 16, 256), F32)],
        [VMEM] * 10,
        [pltpu.VMEM((192, 2048), BF16), LANES, SQUARE],
    )(fm, c0, m1, xu, xd, yu, yd, c1, coords, surf_nodes)
    late = share(payload)
    own, up, down = call(
        late_contact_kernel,
        [((12, 13, 16, 256), F32), ((UPS + 1, 16, 128), F32), ((DOWNS + 2, 16, 128), F32)],
        [SMEM, SMEM] + [VMEM] * 5,
        [TABLE, FORCE, LHS, LANES, SQUARE],
    )(at, lists, everyone, late, state, stiffness, alive)
    xu, xd = neighbours(up, down, "gx")
    up, down = call(
        y_send_2_kernel,
        [((UPS + 1, 16, 128), F32), ((DOWNS + 2, 16, 128), F32)],
        [SMEM] + [VMEM] * 3,
    )(at, own, xu, xd)
    yu, yd = neighbours(up, down, "gy")
    vel, stress = call(
        last_kernel,
        [((3, 12, 8, 128), F32), ((6, 12, 8, 128), F32)],
        [SMEM] + [VMEM] * 5,
    )(at, own, xu, xd, yu, yd)
    return jnp.swapaxes(vel, 1, 2), jnp.swapaxes(stress, 1, 2)


def solution(mesh):
    return jax.shard_map(
        per_device,
        mesh=mesh,
        in_specs=(
            P("gx", "gy", "gz"),
            P("gx", "gy", "gz"),
            P(None, "gx", "gy", "gz"),
            P(None, "gx", "gy", "gz"),
            P(("gx", "gy", "gz"), None, None),
            P(("gx", "gy", "gz"), None),
            P(None, ("gx", "gy", "gz")),
            P(None, ("gx", "gy", "gz"), None, None),
        ),
        out_specs=(P(None, "gx", "gy", "gz"), P(None, "gx", "gy", "gz")),
        check_vma=False,
    )
```

```python
import functools
import math
import jax
import jax.numpy as jnp
from jax import lax
from jax.experimental import pallas as pl
from jax.experimental.pallas import tpu as pltpu
from jax.sharding import PartitionSpec as P

F32 = jnp.float32
BF16 = jnp.bfloat16
SCALE = math.sqrt(math.log2(math.e) / 0.08)
DT = 0.2
PARAMS = pltpu.CompilerParams(vmem_limit_bytes=56 * 2**20)
VMEM = pl.BlockSpec(memory_space=pltpu.VMEM)
SMEM = pl.BlockSpec(memory_space=pltpu.SMEM)
KEYS, PAIRS, NODES, PLANES = 48, 52, 56, 72
ROWS_1 = 104
LATE, PLANES_2 = 48, 96
ROWS_2 = 128
PLANE_ROWS = 32


def split2(x):
    hi = x.astype(BF16)
    return hi, (x - hi.astype(F32)).astype(BF16)


def iota(shape, dim):
    return lax.broadcasted_iota(jnp.int32, shape, dim)


def rim_lanes(shape, above=3):
    lane = iota(shape, len(shape) - 1)
    return (lane >= 126) | (lane < above)


def roll_last(x, shift):
    shift = shift % x.shape[-1]
    return pltpu.roll(x, shift, x.ndim - 1) if shift else x


def pack(tiles, stride=8):
    total = None
    for f, tile in enumerate(tiles):
        part = roll_last(jnp.where(rim_lanes(tile.shape, min(stride - 2, 3)), tile, 0.0), stride * f)
        total = part if total is None else total + part
    return total


def unpack(packed, f, stride=8):
    return jnp.where(
        rim_lanes(packed.shape, min(stride - 2, 3)), roll_last(packed, -stride * f), 0.0
    )


def both(main, rim):
    return jnp.concatenate([main, rim], axis=-1)


def fill16(x):
    pad = 16 - x.shape[-2]
    if not pad:
        return x
    return jnp.concatenate([x, jnp.zeros(x.shape[:-2] + (pad, x.shape[-1]), x.dtype)], axis=-2)


def next_x(x):
    return pltpu.roll(x, x.shape[1] - 1, 1)


def prev_x(x):
    return pltpu.roll(x, 1, 1)


def next_z(x):
    return roll_last(x, -1)


def prev_z(x):
    return roll_last(x, 1)


def planes_to_rows(packed, square_ref):
    square_ref[...] = jnp.zeros_like(square_ref)
    for j in range(packed.shape[0]):
        square_ref[9 * j : 9 * j + 9, :] = packed[j, 0:9, :]
    return jnp.transpose(roll_last(square_ref[...], 2))[0:PLANE_ROWS]


def rows_to_planes(rows, square_ref, planes):
    full = jnp.concatenate([rows, jnp.zeros((128 - PLANE_ROWS, 128), F32)], axis=0)
    square_ref[...] = roll_last(jnp.transpose(full), -2)
    return jnp.stack([fill16(square_ref[9 * j : 9 * j + 9, :]) for j in range(planes)])


def neighbour_planes(all_ref, first_row, stride, me, square_ref, planes):
    low = all_ref[jnp.maximum(me - 1, 0), first_row : first_row + PLANE_ROWS, :]
    up = all_ref[jnp.minimum(me + 1, 7), first_row : first_row + PLANE_ROWS, :]
    kind = iota((PLANE_ROWS, 128), 0) % stride
    low = jnp.where((kind < 2) & (me > 0), low, 0.0)
    up = jnp.where((kind >= 2) & (me < 7), up, 0.0)
    return rows_to_planes(low + up, square_ref, planes)


def spread(x, first):
    to = (iota((x.shape[1], 128), 1) == iota((x.shape[1], 128), 0) + first).astype(BF16)
    return jnp.dot(x.astype(BF16), to, preferred_element_type=F32)


def prep_kernel(
    at_ref, coords_ref, routes_ref, pairs_ref, nodes_ref, stiff_ref, dens_ref, load_ref, alive_ref,
    out_ref, square_ref,
):
    me = at_ref[2]
    fields = [load_ref[0], load_ref[1], load_ref[2], dens_ref[...]]
    for step in (1, 2, 3):
        fields.append(stiff_ref[...] * alive_ref[step].astype(F32))
    rows = planes_to_rows(pack([fill16(f) for f in fields], 4), square_ref)
    nodes = nodes_ref[...].astype(F32)
    routes = routes_ref[...].astype(F32)
    rank = jnp.zeros((4, 16), F32)
    later = iota((4, 16), 1)
    for s in range(15):
        same = jnp.broadcast_to(routes[:, s : s + 1], (4, 16)) == routes
        rank = rank + jnp.where(same & (later > s), 1.0, 0.0)
    keys = spread(routes * 32.0 + rank + 4.0 * me.astype(F32), 16 * me)
    lists = spread(pairs_ref[:, 0, :].astype(F32), 0) + spread(pairs_ref[:, 1, :].astype(F32), 64)
    for dest in range(8):
        for c in range(3):
            out_ref[dest, 16 * c : 16 * c + 16, :] = coords_ref[c]
        out_ref[dest, KEYS : KEYS + 4, :] = keys
        out_ref[dest, PAIRS : PAIRS + 4, :] = lists
        out_ref[dest, NODES : NODES + 16, :] = nodes
        out_ref[dest, PLANES:ROWS_1, :] = rows


def plan_kernel(at_ref, all_ref, list_ref, task_ref):
    me = at_ref[2]
    lane = iota((1, 128), 1)
    block_of = iota((128, 128), 0).astype(F32)
    eye = iota((128, 128), 0) == iota((128, 128), 1)
    upper = (iota((128, 128), 0) < iota((128, 128), 1)).astype(BF16)
    place = iota((128, 128), 0).astype(F32)
    row8 = iota((8, 128), 0)
    src_of = iota((128, 1), 0) // 16

    def nodes_at(src, wants, real):
        ids = all_ref[src, NODES : NODES + 16, :]
        k = ids - 128.0 * jnp.floor(ids * (1.0 / 128.0))
        hit = k == wants[0]
        for want in wants[1:]:
            hit = hit | (k == want)
        count = jnp.sum(jnp.where(hit, 1.0, 0.0), axis=1, keepdims=True)
        return jnp.where(src_of == real, jnp.concatenate([count] * 8, axis=0), 0.0)

    low = nodes_at(jnp.maximum(me - 1, 0), (127.0,), me - 1)
    up = jnp.minimum(me + 1, 7)
    up0, up01 = nodes_at(up, (0.0,), me + 1), nodes_at(up, (0.0, 1.0), me + 1)
    rims = {0: low + up0, 2: low + up01, 3: up0}
    mine_first = (16 * me).astype(F32)

    def prefix(x):
        return jnp.dot(jnp.broadcast_to(x, (8, 128)).astype(BF16), upper, preferred_element_type=F32)[0:1]

    for step in range(4):
        keys = all_ref[0, KEYS + step : KEYS + 1 + step, :]
        for src in range(1, 8):
            keys = keys + all_ref[src, KEYS + step : KEYS + 1 + step, :]
        key_col = jnp.sum(jnp.where(eye, keys, 0.0), axis=1, keepdims=True)
        base = jnp.zeros((1, 1), F32)
        tasks = jnp.zeros((1, 1), F32)
        spots, codes = [], []
        for row in range(4):
            even = all_ref[2 * row, PAIRS + step : PAIRS + 1 + step, :]
            odd = all_ref[2 * row + 1, PAIRS + step : PAIRS + 1 + step, :]
            left = lane < 64
            first = jnp.where(left, even, pltpu.roll(odd, 64, 1))
            second = jnp.where(left, pltpu.roll(even, 64, 1), odd)
            box = jnp.where(left, 64.0 * row, 64.0 * row + 32.0)
            hit_first = key_col == first + box
            hit_second = key_col == second + box
            p_block = jnp.sum(jnp.where(hit_first, block_of + 1.0, 0.0), axis=0, keepdims=True) - 1.0
            r_block = jnp.sum(jnp.where(hit_second, block_of + 1.0, 0.0), axis=0, keepdims=True) - 1.0
            p_slot = p_block - mine_first
            live = r_block >= 0.0
            mine = live & (p_slot >= 0.0) & (p_slot < 16.0)
            sel = jnp.where(mine, 1.0, 0.0)
            spots.append(jnp.where(mine, prefix(sel) + base, -1.0))
            base = base + jnp.sum(sel, axis=1, keepdims=True)
            code = jnp.where(
                row8 == 0, jnp.broadcast_to(p_slot, (8, 128)), jnp.broadcast_to(r_block, (8, 128))
            )
            codes.append(jnp.where(jnp.broadcast_to(mine, (8, 128)), code, 0.0).astype(BF16))
            if step in rims:
                count = jnp.sum(jnp.where(hit_first, rims[step], 0.0), axis=0, keepdims=True)
                count = jnp.where(live, count, 0.0)
                start = prefix(count) + tasks
                tasks = tasks + jnp.sum(count, axis=1, keepdims=True)
                high = jnp.floor(start * (1.0 / 256.0))
                rim_block = jnp.where(p_slot < 0.0, p_slot + 16.0, p_slot)
                some = jnp.broadcast_to(count > 0.0, (8, 128))
                table = jnp.zeros((8, 128), F32)
                for n, line in enumerate((rim_block, r_block, high, start - 256.0 * high, start, count)):
                    table = jnp.where(row8 == n, jnp.broadcast_to(line, (8, 128)), table)
                task_ref[step, row] = jnp.where(some, table, 0.0)
        list_ref[4 + step : 5 + step, :] = jnp.broadcast_to(base, (1, 512)).astype(jnp.int32)
        list_ref[8 + step : 9 + step, :] = jnp.broadcast_to(tasks, (1, 512)).astype(jnp.int32)
        count = jnp.max(base)
        for part in range(4):

            def write(part=part, spots=spots, codes=codes, base=base, step=step):
                total = jnp.zeros((8, 128), F32)
                for row in range(4):
                    onehot = jnp.where(place == spots[row] - 128.0 * part, 1.0, 0.0).astype(BF16)
                    total = total + lax.dot_general(
                        codes[row], onehot, (((1,), (1,)), ((), ())), preferred_element_type=F32
                    )
                used = (lane + 128 * part).astype(F32) < base
                code = jnp.where(used, total[0:1] * 128.0 + total[1:2], 16.0 * 128.0)
                list_ref[step : step + 1, 128 * part : 128 * part + 128] = code.astype(jnp.int32)

            if part == 0:
                write()
            else:
                pl.when(count + 8.0 > 128.0 * part)(write)


UNROLL = 8


def pair_loop(list_ref, step, first_row, me, all_ref, turned_ref, force_ref, sum_ref):
    force_ref[...] = jnp.zeros_like(force_ref)
    for c in range(3):
        turned_ref[16, :, c] = jnp.zeros((4, 8, 128), F32)
        for s in range(16):
            wide = jnp.broadcast_to(all_ref[me, first_row + 16 * c + s : first_row + 16 * c + s + 1, :] * SCALE, (8, 128))
            for a in range(4):
                turned_ref[s, a, c] = roll_last(wide, 32 * a)

    def one(q):
        code = list_ref[step, q]
        slot = lax.shift_right_logical(code, 7)
        src = lax.shift_right_logical(code & 127, 4)
        line = first_row + (code & 15)
        xj = []
        for c in range(3):
            wide = jnp.broadcast_to(all_ref[src, pl.ds(line + 16 * c, 1), :] * SCALE, (8, 128))
            wide = pltpu.roll(wide, 0, 1, stride=1, stride_axis=0)
            xj.append([roll_last(wide, 8 * b) for b in range(4)])
        out = []
        for a in range(4):
            xi = [turned_ref[slot, a, c] for c in range(3)]
            acc = [None] * 3
            for b in range(4):
                diff = [xi[c] - xj[c][b] for c in range(3)]
                dist = diff[0] * diff[0] + diff[1] * diff[1] + diff[2] * diff[2]
                w = jnp.exp2(-dist)
                acc = [w * diff[c] if b == 0 else acc[c] + w * diff[c] for c in range(3)]
            out.append(acc)
        return slot, out

    def body(g, carry):
        done = [one(g * UNROLL + u) for u in range(UNROLL)]
        for slot, out in done:
            for a in range(4):
                for c in range(3):
                    force_ref[slot, a, c] += out[a][c]
        return carry

    lax.fori_loop(0, (list_ref[4 + step, 0] + (UNROLL - 1)) // UNROLL, body, 0)
    for c in range(3):
        total = force_ref[0:16, 0, c]
        for a in range(1, 4):
            total = total + roll_last(force_ref[0:16, a, c], -32 * a)
        sum_ref[c] = jnp.sum(total, axis=1) * (1.0 / SCALE)


def row_and_lane(ids):
    line = jnp.floor(ids * (1.0 / 128.0))
    lane = ids - 128.0 * line
    i = jnp.floor((line + 0.5) * (1.0 / 12.0))
    return 8.0 * line - 95.0 * i, lane


def one_hot(at, rows):
    return jnp.where(iota((rows, 128), 0).astype(F32) == at, 1.0, 0.0)


def scatter_own(sum_ref, all_ref, me, lhs_ref, lanes_ref):
    for s in range(16):
        at = slice(128 * s, 128 * s + 128)
        row, lane = row_and_lane(all_ref[me, NODES + s : NODES + s + 1, :])
        hot = one_hot(row, 96)
        lanes_ref[:, at] = one_hot(lane, 128).astype(BF16)
        for c in range(3):
            hi, lo = split2(sum_ref[c, s : s + 1, :])
            lhs_ref[96 * c : 96 * c + 96, at] = (hot * hi.astype(F32)).astype(BF16)
            lhs_ref[288 + 96 * c : 384 + 96 * c, at] = (hot * lo.astype(F32)).astype(BF16)
    out = lax.dot_general(
        lhs_ref[...], lanes_ref[...], (((1,), (1,)), ((), ())), preferred_element_type=F32
    )
    return (out[:288] + out[288:]).reshape(3, 12, 8, 128)


def split3(x):
    hi, rest = x.astype(BF16), x
    rest = rest - hi.astype(F32)
    mid = rest.astype(BF16)
    return jnp.concatenate([hi, mid, (rest - mid.astype(F32)).astype(BF16)], axis=0)


def contact_rim(list_ref, task_ref, step, first_row, me, pos_ref, ids_ref, rim, square_ref):
    all_ref, near_ref, info_ref, sum_ref = rim
    low, up = jnp.maximum(me - 1, 0), jnp.minimum(me + 1, 7)
    for c in range(3):
        at = first_row + 16 * c
        block = jnp.concatenate([pos_ref[src, at : at + 16, :] for src in range(8)], axis=0)
        all_ref[c] = split3(block * SCALE)
        block = jnp.concatenate([pos_ref[low, at : at + 16, :], pos_ref[up, at : at + 16, :]], axis=0)
        near_ref[c] = split3(block * SCALE)
    ids = jnp.concatenate(
        [ids_ref[low, NODES : NODES + 16, :], ids_ref[up, NODES : NODES + 16, :]], axis=0
    )
    line, lane = row_and_lane(ids)
    below = iota((32, 128), 0) < 16
    ghost = (below & (lane == 127.0)) | (jnp.logical_not(below) & (lane == 0.0))
    if step == 2:
        ghost = ghost | (jnp.logical_not(below) & (lane == 1.0))
    upper = (iota((128, 128), 0) < iota((128, 128), 1)).astype(BF16)
    rank = jnp.dot(jnp.where(ghost, 1.0, 0.0).astype(BF16), upper, preferred_element_type=F32)
    info_ref[0] = jnp.where(ghost, rank, 255.0).astype(BF16)
    info_ref[1] = line.astype(BF16)
    info_ref[2] = jnp.where(below, 0.0, lane + 1.0).astype(BF16)
    sum_ref[...] = jnp.zeros_like(sum_ref)
    tasks = list_ref[8 + step, 0]

    def pick(table, hot):
        return lax.dot_general(table, hot, (((0,), (0,)), ((), ())), preferred_element_type=F32)

    def body(part, carry):
        first = part * 128
        number = (iota((128, 128), 0) + first).astype(F32)
        found = jnp.zeros((8, 128), F32)
        for row in range(4):
            entry = task_ref[step, row]
            start, count = entry[4:5], entry[5:6]
            hot = jnp.where((number >= start) & (number < start + count), 1.0, 0.0).astype(BF16)
            found = found + lax.dot_general(
                entry.astype(BF16), hot, (((1,), (1,)), ((), ())), preferred_element_type=F32
            )
        here = (iota((1, 128), 1) + first).astype(F32)
        nth = here - (256.0 * found[2:3] + found[3:4])
        live = here < tasks.astype(F32)
        hot_p = jnp.where(iota((32, 128), 0).astype(F32) == found[0:1], 1.0, 0.0).astype(BF16)
        hot_r = jnp.where(iota((128, 128), 0).astype(F32) == found[1:2], 1.0, 0.0).astype(BF16)
        match = pick(info_ref[0], hot_p) == nth
        line = jnp.sum(jnp.where(match, pick(info_ref[1], hot_p), 0.0), axis=0, keepdims=True)
        plane = jnp.sum(jnp.where(match, pick(info_ref[2], hot_p), 0.0), axis=0, keepdims=True)
        hot_p3 = jnp.concatenate([hot_p] * 3, axis=0)
        hot_r3 = jnp.concatenate([hot_r] * 3, axis=0)
        xi, xj = [], []
        for c in range(3):
            xi.append(jnp.sum(jnp.where(match, pick(near_ref[c], hot_p3), 0.0), axis=0, keepdims=True))
            xj.append(pick(all_ref[c], hot_r3))
        diff = [xi[c] - xj[c] for c in range(3)]
        dist = diff[0] * diff[0] + diff[1] * diff[1] + diff[2] * diff[2]
        w = jnp.exp2(-dist)
        lines = []
        for want in range(3):
            for c in range(3):
                f = jnp.sum(w * diff[c], axis=0, keepdims=True) * (1.0 / SCALE)
                lines.append(jnp.where(live & (plane == want), f, 0.0))
        lines.append(jnp.zeros((7, 128), F32))
        hi, lo = split2(jnp.concatenate(lines, axis=0))
        hot = one_hot(line, 128).astype(BF16)
        got = lax.dot_general(
            jnp.concatenate([hi, lo], axis=0), hot, (((1,), (1,)), ((), ())), preferred_element_type=F32
        )
        sum_ref[...] += got[0:16] + got[16:32]
        return carry

    lax.fori_loop(0, (tasks + 127) // 128, body, 0)
    square_ref[...] = jnp.zeros_like(square_ref)
    for want, k in enumerate((127, 0, 1)):
        for c in range(3):
            at = (k + 8 * c) % 128
            square_ref[at : at + 1, :] = sum_ref[3 * want + c : 3 * want + c + 1, :]
    return fill16(jnp.transpose(square_ref[...])[0:96].reshape(12, 8, 128))


def node_sum(elements):
    e = 0.125 * elements
    e = e + prev_z(e)
    e = e + prev_x(e)
    zero = jnp.zeros((1,) + e.shape[1:], F32)
    return jnp.concatenate([e, zero], axis=0) + jnp.concatenate([zero, e], axis=0)


def send_planes(planes, out_ref):
    count = len(planes)
    for n, plane in enumerate(planes):
        out_ref[n] = plane[:, :128]
    for g in range(0, count, 16):
        out_ref[count + g // 16] = pack([p[:, 128:] for p in planes[g : g + 16]])


def get_plane(ref, n, count):
    return both(ref[n], unpack(ref[count + n // 16], n % 16))


def row_plane(x, i):
    return fill16(x[:, i, :])


def first_contact_kernel(
    at_ref, list_ref, task_ref, all_ref, load_ref, dens_ref, stiff_ref, alive_ref,
    fm_ref, c0_ref, m1_ref, up_ref, down_ref,
    turned_ref, force_ref, sum_ref, lhs_ref, lanes_ref, square_ref, *rim,
):
    me = at_ref[2]
    planes = neighbour_planes(all_ref, PLANES, 4, me, square_ref, 12)
    fields = [load_ref[0], load_ref[1], load_ref[2], dens_ref[...]]
    sums = [node_sum(both(fill16(f), unpack(planes, n, 4))) for n, f in enumerate(fields)]
    m1 = both(fill16(stiff_ref[...] * alive_ref[1].astype(F32)), unpack(planes, 4, 4))
    zero = jnp.zeros((1, 16, 256), F32)
    m1 = jnp.concatenate([m1, zero], axis=0)
    m1_ref[...] = m1
    fm_ref[3] = sums[3]
    for c in range(3):
        fm_ref[c] = sums[c]
    pair_loop(list_ref, 0, 0, me, all_ref, turned_ref, force_ref, sum_ref)
    own = scatter_own(sum_ref, all_ref, me, lhs_ref, lanes_ref)
    rim = contact_rim(list_ref, task_ref, 0, 0, me, all_ref, all_ref, rim, square_ref)
    for c in range(3):
        full = jnp.concatenate([both(fill16(own[c]), unpack(rim, c)), zero], axis=0)
        c0_ref[c] = full
        fm_ref[c] = fm_ref[c] + full
    ups = [row_plane(fm_ref[n], 7) for n in range(4)] + [row_plane(fm_ref[n], 8) for n in range(4)]
    send_planes(ups + [row_plane(m1, 7)], up_ref)
    send_planes([row_plane(fm_ref[n], 0) for n in range(4)], down_ref)


def step_contact_kernel(
    at_ref, list_ref, all_ref, out_ref, turned_ref, force_ref, sum_ref, lhs_ref, lanes_ref
):
    me = at_ref[2]
    pair_loop(list_ref, 1, 0, me, all_ref, turned_ref, force_ref, sum_ref)
    out_ref[...] = scatter_own(sum_ref, all_ref, me, lhs_ref, lanes_ref)


def shift_rows(x, by):
    return pltpu.roll(x, by % x.shape[1], 1)


def x_extended_1(fm_ref, m1_ref, ups_ref, downs_ref, pick):
    lines = sorted(pick)
    row = iota((len(lines), 16, 256), 1)

    def lift(plane):
        return jnp.stack([jnp.broadcast_to(plane[j : j + 1], (16, 256)) for j in lines])

    def take(x):
        return jnp.stack([x[j] for j in lines])

    def extend(x, low, add, high):
        if add is not None:
            x = x + jnp.where(row == 0, lift(add), 0.0) + jnp.where(row == 8, lift(high), 0.0)
            x = jnp.where(row < 9, x, 0.0)
        else:
            x = jnp.where(row < 8, x, 0.0)
        return jnp.where(row == 0, lift(low), shift_rows(x, 1))

    out = [
        extend(
            take(fm_ref[n]),
            get_plane(ups_ref, n, 9),
            get_plane(ups_ref, 4 + n, 9),
            get_plane(downs_ref, n, 4),
        )
        for n in range(4)
    ]
    return out, extend(take(m1_ref[...]), get_plane(ups_ref, 8, 9), None, None)


def y_send_1_kernel(fm_ref, m1_ref, ups_ref, downs_ref, up_ref, down_ref):
    fields, m1 = x_extended_1(fm_ref, m1_ref, ups_ref, downs_ref, (0, 11, 12))
    send_planes([f[1] for f in fields] + [f[2] for f in fields] + [m1[1]], up_ref)
    send_planes([f[0] for f in fields], down_ref)


def stress_of(disp, modulus):
    grads = []
    for u in disp:
        s, d = u[1:] + u[:-1], u[1:] - u[:-1]
        sn = next_x(s)
        ss, xd = sn + s, sn - s
        yd = next_x(d) + d
        grads.append((xd + next_z(xd), yd + next_z(yd), next_z(ss) - ss))
    m = 0.25 * modulus
    exx, eyy, ezz = grads[0][0], grads[1][1], grads[2][2]
    trace = exx + eyy + ezz
    return (
        m * (2.0 * exx + trace),
        m * (2.0 * eyy + trace),
        m * (2.0 * ezz + trace),
        m * (grads[1][0] + grads[0][1]),
        m * (grads[2][1] + grads[1][2]),
        m * (grads[0][2] + grads[2][0]),
    )


def force_of(stress):
    xx, yy, zz, xy, yz, zx = stress
    out = []
    for a, b, c in ((xx, xy, zx), (xy, yy, yz), (zx, yz, zz)):
        az, bz, cz = a + prev_z(a), b + prev_z(b), prev_z(c) - c
        ac = (prev_x(az) - az) + (prev_x(cz) + cz)
        by = prev_x(bz) + bz
        out.append(-0.25 * ((ac[:-1] + ac[1:]) + (by[:-1] - by[1:])))
    return out


def gather_rows(disp, lanes_ref, rows_ref):
    hot = rows_ref[...]
    values = []
    for c in range(3):
        hi, lo = split2(disp[c])
        field = jnp.concatenate([hi, lo], axis=0)
        picked = lax.dot_general(field, hot, (((0,), (0,)), ((), ())), preferred_element_type=F32)
        values.append(jnp.sum(picked * lanes_ref[...].astype(F32), axis=0, keepdims=True))
    return values


def second_step_kernel(
    fm_ref, c0_ref, m1_ref, xu_ref, xd_ref, yu_ref, yd_ref, c1_ref, coords_ref, nodes_ref,
    out_ref, state_ref, rows_ref, lanes_ref, square_ref,
):
    fields, m1 = x_extended_1(fm_ref, m1_ref, xu_ref, xd_ref, range(13))
    zero = jnp.zeros((1, 16, 256), F32)
    for n in range(4):
        low, add = get_plane(yu_ref, n, 9), get_plane(yu_ref, 4 + n, 9)
        own = fields[n]
        fields[n] = jnp.concatenate(
            [low[None], (own[0] + add)[None], own[1:12], (own[12] + get_plane(yd_ref, n, 4))[None]],
            axis=0,
        )
    m1 = jnp.concatenate([get_plane(yu_ref, 8, 9)[None], m1[:12]], axis=0)
    mass = fields[3]
    inv = jnp.where(mass > 0.0, DT / jnp.where(mass > 0.0, mass, 1.0), 0.0)
    disp1 = [DT * (inv * fields[c]) for c in range(3)]
    force = force_of([jnp.concatenate([x, zero], axis=0) for x in stress_of(disp1, m1)])
    inv = inv[1:]
    row = iota((13, 16, 256), 1)
    good = (row > 0) & (row < 10)
    disp2s, vel2s = [], []
    for c in range(3):
        c1 = jnp.concatenate([fill16(c1_ref[c]), jnp.zeros((1, 16, 128), F32)], axis=0)
        c1 = shift_rows(both(c1, jnp.zeros((13, 16, 128), F32)), 1)
        total = fields[c][1:]
        accel = inv * (total - shift_rows(c0_ref[c], 1))
        vel2 = inv * total + inv * force[c] + (accel + inv * c1)
        disp2 = disp1[c][1:] + DT * vel2
        back = [shift_rows(jnp.where(good, x, 0.0), -1) for x in (disp2, vel2, accel)]
        disp2s.append(back[0])
        vel2s.append(back[1])
        state_ref[c] = back[0]
        state_ref[3 + c] = back[1]
        state_ref[6 + c] = back[2]
    state_ref[9] = shift_rows(jnp.where(good, inv, 0.0), -1)
    for s in range(16):
        at = slice(128 * s, 128 * s + 128)
        r, l = row_and_lane(nodes_ref[s : s + 1, :].astype(F32))
        hot = one_hot(r, 96).astype(BF16)
        rows_ref[0:96, at] = hot
        rows_ref[96:192, at] = hot
        lanes_ref[:, at] = one_hot(l, 128).astype(BF16)
    for first, disp in (
        (0, [shift_rows(d[1:13], -1)[:, :8, :128] for d in disp1]),
        (LATE, [d[0:12, :8, :128] for d in disp2s]),
    ):
        values = gather_rows([d.reshape(96, 128) for d in disp], lanes_ref, rows_ref)
        for c in range(3):
            block = jnp.concatenate(
                [values[c][:, 128 * s : 128 * s + 128] for s in range(16)], axis=0
            ) + coords_ref[c]
            for dest in range(8):
                out_ref[dest, first + 16 * c : first + 16 * c + 16, :] = block
    rows = planes_to_rows(pack([x[:, :, :128] for x in disp2s + vel2s], 5), square_ref)
    for dest in range(8):
        out_ref[dest, PLANES_2:ROWS_2, :] = rows


UP_LIST = (
    [(n, 0) for n in range(3)] + [(n, 1) for n in range(3)] + [(n, 1) for n in (3, 4, 5, 9)]
    + [(10, 0), (10, 1), (11, 1)]
)
DOWN_LIST = (
    [(n, p) for p in (0, 1, 2) for n in range(3)]
    + [(n, p) for p in (0, 1) for n in (3, 4, 5)]
    + [(n, 0) for n in (6, 7, 8)]
    + [(9, 0), (9, 1), (10, 0), (10, 1), (11, 0)]
)
UPS, DOWNS = len(UP_LIST), len(DOWN_LIST)


def plane_of(ref, listed, n, p):
    return get_plane(ref, listed.index((n, p)), len(listed)) if (n, p) in listed else None


def late_contact_kernel(
    at_ref, list_ref, task_ref, first_ref, all_ref, state_ref, stiff_ref, alive_ref,
    own_ref, up_ref, down_ref,
    turned_ref, force_ref, sum_ref, lhs_ref, lanes_ref, square_ref, *rims,
):
    me = at_ref[2]
    zplanes = neighbour_planes(all_ref, PLANES_2, 5, me, square_ref, 13)
    mplanes = neighbour_planes(first_ref, PLANES, 4, me, square_ref, 12)
    top = (iota((13, 16, 128), 2) == 0) & (me == 7)
    zero = jnp.zeros((1, 16, 256), F32)

    def with_rim(own, n):
        return both(own[:, :, :128], jnp.where(top, own[:, :, 128:], unpack(zplanes, n, 5)))

    inv = state_ref[9]
    own_ref[9] = inv
    for c in range(3):
        own_ref[c] = with_rim(state_ref[c], c)
        own_ref[3 + c] = with_rim(state_ref[3 + c], 3 + c) + state_ref[6 + c]
        own_ref[6 + c] = state_ref[6 + c]
    for n, step in ((10, 2), (11, 3)):
        m = both(fill16(stiff_ref[...] * alive_ref[step].astype(F32)), unpack(mplanes, 3 + step, 4))
        own_ref[n] = jnp.concatenate([m, zero], axis=0)
    for step, first_row, n in ((2, 0, 3), (3, LATE, 6)):
        pair_loop(list_ref, step, first_row, me, all_ref, turned_ref, force_ref, sum_ref)
        own = scatter_own(sum_ref, first_ref, me, lhs_ref, lanes_ref)
        rim = contact_rim(list_ref, task_ref, step, first_row, me, all_ref, first_ref, rims, square_ref)
        for c in range(3):
            full = both(fill16(own[c]), unpack(rim, c))
            own_ref[n + c, 0:12] = own_ref[n + c, 0:12] + own_ref[9, 0:12] * full
    send_planes([row_plane(own_ref[n], 6 + p) for n, p in UP_LIST], up_ref)
    send_planes([row_plane(own_ref[n], p) for n, p in DOWN_LIST], down_ref)


def x_extended_2(own_ref, ups_ref, downs_ref, at_last, lines):
    row = iota((len(lines), 16, 256), 1)
    keep = (row < 8) | ((row == 8) & at_last)

    def lift(plane):
        return jnp.stack([jnp.broadcast_to(plane[j : j + 1], (16, 256)) for j in lines])

    out = []
    for n in range(12):
        x = jnp.stack([own_ref[n, j] for j in lines])
        x = shift_rows(jnp.where(keep, x, 0.0), 2)
        for ref, listed, first, count in ((ups_ref, UP_LIST, 0, 2), (downs_ref, DOWN_LIST, 10, 3)):
            for p in range(count):
                got = plane_of(ref, listed, n, p)
                if got is not None:
                    add = lift(got)
                    if first + p == 10:
                        x = jnp.where((row == 10) & jnp.logical_not(at_last), add, x)
                    else:
                        x = jnp.where(row == first + p, add, x)
        out.append(x)
    return out


def y_send_2_kernel(at_ref, own_ref, ups_ref, downs_ref, up_ref, down_ref):
    fields = x_extended_2(own_ref, ups_ref, downs_ref, at_ref[0] == 7, (0, 1, 2, 10, 11))
    send_planes([fields[n][3 + p] for n, p in UP_LIST], up_ref)
    send_planes([fields[n][p] for n, p in DOWN_LIST], down_ref)


def last_kernel(at_ref, own_ref, xu_ref, xd_ref, yu_ref, yd_ref, vel_ref, stress_ref):
    fields = x_extended_2(own_ref, xu_ref, xd_ref, at_ref[0] == 7, range(13))
    y_last = at_ref[1] == 3
    none = jnp.zeros((16, 256), F32)
    wide = []
    for n in range(12):
        planes = [plane_of(yu_ref, UP_LIST, n, p) for p in (0, 1)]
        planes += [fields[n][j] for j in range(12)]
        after = [plane_of(yd_ref, DOWN_LIST, n, p) for p in (0, 1, 2)]
        after = [none if p is None else p for p in after]
        after[0] = jnp.where(y_last, fields[n][12], after[0])
        planes = [none if p is None else p for p in planes] + after
        wide.append(jnp.stack(planes))
    disp2, vh3, g3, inv, m2, m3 = wide[0:3], wide[3:6], wide[6:9], wide[9], wide[10], wide[11]
    force = force_of(stress_of(disp2, m2[:16]))
    vel3 = [vh3[c][1:16] + inv[1:16] * force[c] for c in range(3)]
    disp3 = [disp2[c][1:16] + DT * vel3[c] for c in range(3)]
    force = force_of(stress_of(disp3, m3[1:15]))
    vel4 = [vel3[c][1:14] + (inv[2:15] * force[c] + g3[c][2:15]) for c in range(3)]
    disp4 = [disp3[c][1:14] + DT * vel4[c] for c in range(3)]
    stress = stress_of(disp4, m3[2:14])
    for n in range(6):
        stress_ref[n] = shift_rows(stress[n][:, :, :128], -2)[:, :8, :]
    for c in range(3):
        s = vel4[c][1:] + vel4[c][:-1]
        s = s + next_x(s)
        s = s + next_z(s)
        vel_ref[c] = shift_rows(0.125 * s[:, :, :128], -2)[:, :8, :]


def call(kernel, outs, specs, scratch=()):
    return pl.pallas_call(
        kernel,
        out_shape=[jax.ShapeDtypeStruct(s, d) for s, d in outs],
        in_specs=specs,
        out_specs=[VMEM] * len(outs),
        scratch_shapes=list(scratch),
        compiler_params=PARAMS,
    )


def share(blocks):
    return lax.all_to_all(blocks, "gz", split_axis=0, concat_axis=0, tiled=True)


def neighbours(up, down, axis):
    count = lax.axis_size(axis)
    ahead = [(i, i + 1) for i in range(count - 1)]
    return lax.ppermute(up, axis, ahead), lax.ppermute(down, axis, [(j, i) for i, j in ahead])


TURNED = pltpu.VMEM((17, 4, 3, 8, 128), F32)
SUMS = pltpu.VMEM((3, 16, 128), F32)
RIM = [
    pltpu.VMEM((3, 384, 128), BF16),
    pltpu.VMEM((3, 96, 128), BF16),
    pltpu.VMEM((3, 32, 128), BF16),
    pltpu.VMEM((16, 128), F32),
]
LHS = pltpu.VMEM((576, 2048), BF16)
LANES = pltpu.VMEM((128, 2048), BF16)
SQUARE = pltpu.VMEM((128, 128), F32)


def per_device(stiffness, density, load, alive, surf_coords, surf_nodes, routes, pairs):
    at = jnp.stack([lax.axis_index(a) for a in ("gx", "gy", "gz")]).astype(jnp.int32)
    stiffness, density = jnp.swapaxes(stiffness, 0, 1), jnp.swapaxes(density, 0, 1)
    load, alive = jnp.swapaxes(load, 1, 2), jnp.swapaxes(alive, 1, 2)
    coords = jnp.swapaxes(surf_coords, 0, 1)
    pairs = jnp.swapaxes(pairs[:, 0], 1, 2)
    (payload,) = call(prep_kernel, [((8, ROWS_1, 128), F32)], [SMEM] + [VMEM] * 8, [SQUARE])(
        at, coords, routes, pairs, surf_nodes, stiffness, density, load, alive
    )
    everyone = share(payload)
    lists, tasks = call(plan_kernel, [((12, 512), jnp.int32), ((4, 4, 8, 128), F32)], [SMEM, VMEM])(at, everyone)
    fm, c0, m1, up, down = call(
        first_contact_kernel,
        [((4, 13, 16, 256), F32), ((3, 13, 16, 256), F32), ((13, 16, 256), F32), ((10, 16, 128), F32),
         ((5, 16, 128), F32)],
        [SMEM, SMEM] + [VMEM] * 6,
        [TURNED, TURNED, SUMS, LHS, LANES, SQUARE] + RIM,
    )(at, lists, tasks, everyone, load, density, stiffness, alive)
    xu, xd = neighbours(up, down, "gx")
    (c1,) = call(
        step_contact_kernel,
        [((3, 12, 8, 128), F32)],
        [SMEM, SMEM, VMEM],
        [TURNED, TURNED, SUMS, LHS, LANES],
    )(at, lists, everyone)
    up, down = call(y_send_1_kernel, [((10, 16, 128), F32), ((5, 16, 128), F32)], [VMEM] * 4)(
        fm, m1, xu, xd
    )
    yu, yd = neighbours(up, down, "gy")
    payload, state = call(
        second_step_kernel,
        [((8, ROWS_2, 128), F32), ((10, 13, 16, 256), F32)],
        [VMEM] * 10,
        [pltpu.VMEM((192, 2048), BF16), LANES, SQUARE],
    )(fm, c0, m1, xu, xd, yu, yd, c1, coords, surf_nodes)
    late = share(payload)
    own, up, down = call(
        late_contact_kernel,
        [((12, 13, 16, 256), F32), ((UPS + 1, 16, 128), F32), ((DOWNS + 2, 16, 128), F32)],
        [SMEM, SMEM] + [VMEM] * 6,
        [TURNED, TURNED, SUMS, LHS, LANES, SQUARE] + RIM,
    )(at, lists, tasks, everyone, late, state, stiffness, alive)
    xu, xd = neighbours(up, down, "gx")
    up, down = call(
        y_send_2_kernel,
        [((UPS + 1, 16, 128), F32), ((DOWNS + 2, 16, 128), F32)],
        [SMEM] + [VMEM] * 3,
    )(at, own, xu, xd)
    yu, yd = neighbours(up, down, "gy")
    vel, stress = call(
        last_kernel,
        [((3, 12, 8, 128), F32), ((6, 12, 8, 128), F32)],
        [SMEM] + [VMEM] * 5,
    )(at, own, xu, xd, yu, yd)
    return jnp.swapaxes(vel, 1, 2), jnp.swapaxes(stress, 1, 2)


def solution(mesh):
    return jax.shard_map(
        per_device,
        mesh=mesh,
        in_specs=(
            P("gx", "gy", "gz"),
            P("gx", "gy", "gz"),
            P(None, "gx", "gy", "gz"),
            P(None, "gx", "gy", "gz"),
            P(("gx", "gy", "gz"), None, None),
            P(("gx", "gy", "gz"), None),
            P(None, ("gx", "gy", "gz")),
            P(None, ("gx", "gy", "gz"), None, None),
        ),
        out_specs=(P(None, "gx", "gy", "gz"), P(None, "gx", "gy", "gz")),
        check_vma=False,
    )
```

```python
import functools
import math
import jax
import jax.numpy as jnp
from jax import lax
from jax.experimental import pallas as pl
from jax.experimental.pallas import tpu as pltpu
from jax.sharding import PartitionSpec as P

F32 = jnp.float32
BF16 = jnp.bfloat16
SCALE = math.sqrt(math.log2(math.e) / 0.08)
DT = 0.2
PARAMS = pltpu.CompilerParams(vmem_limit_bytes=28 * 2**20)
VMEM = pl.BlockSpec(memory_space=pltpu.VMEM)
SMEM = pl.BlockSpec(memory_space=pltpu.SMEM)
HELD = pl.BlockSpec(memory_space=pltpu.VMEM)
FAR = pl.BlockSpec(memory_space=pltpu.HBM)
KEYS, PAIRS, NODES, PLANES = 48, 52, 56, 72
ROWS_1 = 104
LATE, PLANES_2 = 48, 96
ROWS_2 = 128
PLANE_ROWS = 32


def split2(x):
    hi = x.astype(BF16)
    return hi, (x - hi.astype(F32)).astype(BF16)


def iota(shape, dim):
    return lax.broadcasted_iota(jnp.int32, shape, dim)


def rim_lanes(shape, above=3):
    lane = iota(shape, len(shape) - 1)
    return (lane >= 126) | (lane < above)


def roll_last(x, shift):
    shift = shift % x.shape[-1]
    return pltpu.roll(x, shift, x.ndim - 1) if shift else x


def pack(tiles, stride=8):
    total = None
    for f, tile in enumerate(tiles):
        part = roll_last(jnp.where(rim_lanes(tile.shape, min(stride - 2, 3)), tile, 0.0), stride * f)
        total = part if total is None else total + part
    return total


def unpack(packed, f, stride=8):
    return jnp.where(
        rim_lanes(packed.shape, min(stride - 2, 3)), roll_last(packed, -stride * f), 0.0
    )


def both(main, rim):
    return jnp.concatenate([main, rim], axis=-1)


def fill16(x):
    pad = 16 - x.shape[-2]
    if not pad:
        return x
    return jnp.concatenate([x, jnp.zeros(x.shape[:-2] + (pad, x.shape[-1]), x.dtype)], axis=-2)


def next_x(x):
    return pltpu.roll(x, x.shape[1] - 1, 1)


def prev_x(x):
    return pltpu.roll(x, 1, 1)


def next_z(x):
    return roll_last(x, -1)


def prev_z(x):
    return roll_last(x, 1)


def planes_to_rows(packed, square_ref):
    square_ref[...] = jnp.zeros_like(square_ref)
    for j in range(packed.shape[0]):
        square_ref[9 * j : 9 * j + 9, :] = packed[j, 0:9, :]
    return jnp.transpose(roll_last(square_ref[...], 2))[0:PLANE_ROWS]


def rows_to_planes(rows, square_ref, planes):
    full = jnp.concatenate([rows, jnp.zeros((128 - PLANE_ROWS, 128), F32)], axis=0)
    square_ref[...] = roll_last(jnp.transpose(full), -2)
    return jnp.stack([fill16(square_ref[9 * j : 9 * j + 9, :]) for j in range(planes)])


def neighbour_planes(all_ref, first_row, stride, me, square_ref, planes):
    low = all_ref[jnp.maximum(me - 1, 0), first_row : first_row + PLANE_ROWS, :]
    up = all_ref[jnp.minimum(me + 1, 7), first_row : first_row + PLANE_ROWS, :]
    kind = iota((PLANE_ROWS, 128), 0) % stride
    low = jnp.where((kind < 2) & (me > 0), low, 0.0)
    up = jnp.where((kind >= 2) & (me < 7), up, 0.0)
    return rows_to_planes(low + up, square_ref, planes)


def spread(x, first):
    to = (iota((x.shape[1], 128), 1) == iota((x.shape[1], 128), 0) + first).astype(BF16)
    return jnp.dot(x.astype(BF16), to, preferred_element_type=F32)


def prep_kernel(at_ref, *refs):
    far, (out_ref, field_ref, square_ref), near, sems = refs[:8], refs[8:11], refs[11:19], refs[19]
    copies = [pltpu.make_async_copy(a, b, sems.at[n]) for n, (a, b) in enumerate(zip(far, near))]
    for copy in copies:
        copy.start()
    for copy in copies:
        copy.wait()
    coords_ref, routes_ref, pairs_ref, nodes_ref, stiff_ref, dens_ref, load_ref, alive_ref = near
    me = at_ref[2]
    for c in range(3):
        field_ref[c] = load_ref[c]
    field_ref[3] = dens_ref[...]
    for step in (1, 2, 3):
        field_ref[3 + step] = stiff_ref[...] * alive_ref[step].astype(F32)
    rows = planes_to_rows(pack([fill16(field_ref[n]) for n in range(7)], 4), square_ref)
    nodes = nodes_ref[...].astype(F32)
    routes = routes_ref[...].astype(F32)
    rank = jnp.zeros((4, 16), F32)
    later = iota((4, 16), 1)
    for s in range(15):
        same = jnp.broadcast_to(routes[:, s : s + 1], (4, 16)) == routes
        rank = rank + jnp.where(same & (later > s), 1.0, 0.0)
    keys = spread(routes * 32.0 + rank + 4.0 * me.astype(F32), 16 * me)
    lists = spread(pairs_ref[:, 0, :].astype(F32), 0) + spread(pairs_ref[:, 1, :].astype(F32), 64)
    for dest in range(8):
        for c in range(3):
            out_ref[dest, 16 * c : 16 * c + 16, :] = coords_ref[c]
        out_ref[dest, KEYS : KEYS + 4, :] = keys
        out_ref[dest, PAIRS : PAIRS + 4, :] = lists
        out_ref[dest, NODES : NODES + 16, :] = nodes
        out_ref[dest, PLANES:ROWS_1, :] = rows


def plan_kernel(at_ref, all_ref, list_ref, task_ref):
    me = at_ref[2]
    lane = iota((1, 128), 1)
    block_of = iota((128, 128), 0).astype(F32)
    eye = iota((128, 128), 0) == iota((128, 128), 1)
    upper = (iota((128, 128), 0) < iota((128, 128), 1)).astype(BF16)
    place = iota((128, 128), 0).astype(F32)
    row8 = iota((8, 128), 0)
    src_of = iota((128, 1), 0) // 16

    def nodes_at(src, wants, real):
        ids = all_ref[src, NODES : NODES + 16, :]
        k = ids - 128.0 * jnp.floor(ids * (1.0 / 128.0))
        hit = k == wants[0]
        for want in wants[1:]:
            hit = hit | (k == want)
        count = jnp.sum(jnp.where(hit, 1.0, 0.0), axis=1, keepdims=True)
        return jnp.where(src_of == real, jnp.concatenate([count] * 8, axis=0), 0.0)

    low = nodes_at(jnp.maximum(me - 1, 0), (127.0,), me - 1)
    up = jnp.minimum(me + 1, 7)
    up0, up01 = nodes_at(up, (0.0,), me + 1), nodes_at(up, (0.0, 1.0), me + 1)
    rims = {0: low + up0, 2: low + up01, 3: up0}
    mine_first = (16 * me).astype(F32)

    def prefix(x):
        return jnp.dot(jnp.broadcast_to(x, (8, 128)).astype(BF16), upper, preferred_element_type=F32)[0:1]

    for step in range(4):
        keys = all_ref[0, KEYS + step : KEYS + 1 + step, :]
        for src in range(1, 8):
            keys = keys + all_ref[src, KEYS + step : KEYS + 1 + step, :]
        key_col = jnp.sum(jnp.where(eye, keys, 0.0), axis=1, keepdims=True)
        base = jnp.zeros((1, 1), F32)
        tasks = jnp.zeros((1, 1), F32)
        spots, codes = [], []
        for row in range(4):
            even = all_ref[2 * row, PAIRS + step : PAIRS + 1 + step, :]
            odd = all_ref[2 * row + 1, PAIRS + step : PAIRS + 1 + step, :]
            left = lane < 64
            first = jnp.where(left, even, pltpu.roll(odd, 64, 1))
            second = jnp.where(left, pltpu.roll(even, 64, 1), odd)
            box = jnp.where(left, 64.0 * row, 64.0 * row + 32.0)
            hit_first = key_col == first + box
            hit_second = key_col == second + box
            p_block = jnp.sum(jnp.where(hit_first, block_of + 1.0, 0.0), axis=0, keepdims=True) - 1.0
            r_block = jnp.sum(jnp.where(hit_second, block_of + 1.0, 0.0), axis=0, keepdims=True) - 1.0
            p_slot = p_block - mine_first
            live = r_block >= 0.0
            mine = live & (p_slot >= 0.0) & (p_slot < 16.0)
            sel = jnp.where(mine, 1.0, 0.0)
            spots.append(jnp.where(mine, prefix(sel) + base, -1.0))
            base = base + jnp.sum(sel, axis=1, keepdims=True)
            code = jnp.where(
                row8 == 0, jnp.broadcast_to(p_slot, (8, 128)), jnp.broadcast_to(r_block, (8, 128))
            )
            codes.append(jnp.where(jnp.broadcast_to(mine, (8, 128)), code, 0.0).astype(BF16))
            if step in rims:
                count = jnp.sum(jnp.where(hit_first, rims[step], 0.0), axis=0, keepdims=True)
                count = jnp.where(live, count, 0.0)
                start = prefix(count) + tasks
                tasks = tasks + jnp.sum(count, axis=1, keepdims=True)
                high = jnp.floor(start * (1.0 / 256.0))
                rim_block = jnp.where(p_slot < 0.0, p_slot + 16.0, p_slot)
                some = jnp.broadcast_to(count > 0.0, (8, 128))
                table = jnp.zeros((8, 128), F32)
                for n, line in enumerate((rim_block, r_block, high, start - 256.0 * high, start, count)):
                    table = jnp.where(row8 == n, jnp.broadcast_to(line, (8, 128)), table)
                task_ref[step, row] = jnp.where(some, table, 0.0)
        list_ref[4 + step : 5 + step, :] = jnp.broadcast_to(base, (1, 512)).astype(jnp.int32)
        list_ref[8 + step : 9 + step, :] = jnp.broadcast_to(tasks, (1, 512)).astype(jnp.int32)
        count = jnp.max(base)
        for part in range(4):

            def write(part=part, spots=spots, codes=codes, base=base, step=step):
                total = jnp.zeros((8, 128), F32)
                for row in range(4):
                    onehot = jnp.where(place == spots[row] - 128.0 * part, 1.0, 0.0).astype(BF16)
                    total = total + lax.dot_general(
                        codes[row], onehot, (((1,), (1,)), ((), ())), preferred_element_type=F32
                    )
                used = (lane + 128 * part).astype(F32) < base
                code = jnp.where(used, total[0:1] * 128.0 + total[1:2], 16.0 * 128.0)
                list_ref[step : step + 1, 128 * part : 128 * part + 128] = code.astype(jnp.int32)

            if part == 0:
                write()
            else:
                pl.when(count + 8.0 > 128.0 * part)(write)


UNROLL = 8


def pair_loop(list_ref, step, first_row, me, all_ref, turned_ref, force_ref, sum_ref):
    force_ref[...] = jnp.zeros_like(force_ref)
    for c in range(3):
        turned_ref[16, :, c] = jnp.zeros((4, 8, 128), F32)
        for s in range(16):
            wide = jnp.broadcast_to(all_ref[me, first_row + 16 * c + s : first_row + 16 * c + s + 1, :] * SCALE, (8, 128))
            for a in range(4):
                turned_ref[s, a, c] = roll_last(wide, 32 * a)

    def one(q):
        code = list_ref[step, q]
        slot = lax.shift_right_logical(code, 7)
        src = lax.shift_right_logical(code & 127, 4)
        line = first_row + (code & 15)
        xj = []
        for c in range(3):
            wide = jnp.broadcast_to(all_ref[src, pl.ds(line + 16 * c, 1), :] * SCALE, (8, 128))
            wide = pltpu.roll(wide, 0, 1, stride=1, stride_axis=0)
            xj.append([roll_last(wide, 8 * b) for b in range(4)])
        out = []
        for a in range(4):
            xi = [turned_ref[slot, a, c] for c in range(3)]
            acc = [None] * 3
            for b in range(4):
                diff = [xi[c] - xj[c][b] for c in range(3)]
                dist = diff[0] * diff[0] + diff[1] * diff[1] + diff[2] * diff[2]
                w = jnp.exp2(-dist)
                acc = [w * diff[c] if b == 0 else acc[c] + w * diff[c] for c in range(3)]
            out.append(acc)
        return slot, out

    def body(g, carry):
        done = [one(g * UNROLL + u) for u in range(UNROLL)]
        for slot, out in done:
            for a in range(4):
                for c in range(3):
                    force_ref[slot, a, c] += out[a][c]
        return carry

    lax.fori_loop(0, (list_ref[4 + step, 0] + (UNROLL - 1)) // UNROLL, body, 0)
    for c in range(3):
        total = force_ref[0:16, 0, c]
        for a in range(1, 4):
            total = total + roll_last(force_ref[0:16, a, c], -32 * a)
        sum_ref[c] = jnp.sum(total, axis=1) * (1.0 / SCALE)


def row_and_lane(ids):
    line = jnp.floor(ids * (1.0 / 128.0))
    lane = ids - 128.0 * line
    i = jnp.floor((line + 0.5) * (1.0 / 12.0))
    return 8.0 * line - 95.0 * i, lane


def one_hot(at, rows):
    return jnp.where(iota((rows, 128), 0).astype(F32) == at, 1.0, 0.0)


def scatter_own(sum_ref, all_ref, me, lhs_ref, lanes_ref):
    for s in range(16):
        at = slice(128 * s, 128 * s + 128)
        row, lane = row_and_lane(all_ref[me, NODES + s : NODES + s + 1, :])
        hot = one_hot(row, 96)
        lanes_ref[:, at] = one_hot(lane, 128).astype(BF16)
        for c in range(3):
            hi, lo = split2(sum_ref[c, s : s + 1, :])
            lhs_ref[96 * c : 96 * c + 96, at] = (hot * hi.astype(F32)).astype(BF16)
            lhs_ref[288 + 96 * c : 384 + 96 * c, at] = (hot * lo.astype(F32)).astype(BF16)
    out = lax.dot_general(
        lhs_ref[...], lanes_ref[...], (((1,), (1,)), ((), ())), preferred_element_type=F32
    )
    return (out[:288] + out[288:]).reshape(3, 12, 8, 128)


def split3(x):
    hi, rest = x.astype(BF16), x
    rest = rest - hi.astype(F32)
    mid = rest.astype(BF16)
    return jnp.concatenate([hi, mid, (rest - mid.astype(F32)).astype(BF16)], axis=0)


def contact_rim(list_ref, task_ref, step, first_row, me, pos_ref, ids_ref, rim, square_ref):
    all_ref, near_ref, info_ref, sum_ref = rim
    low, up = jnp.maximum(me - 1, 0), jnp.minimum(me + 1, 7)
    for c in range(3):
        at = first_row + 16 * c
        block = jnp.concatenate([pos_ref[src, at : at + 16, :] for src in range(8)], axis=0)
        all_ref[c] = split3(block * SCALE)
        block = jnp.concatenate([pos_ref[low, at : at + 16, :], pos_ref[up, at : at + 16, :]], axis=0)
        near_ref[c] = split3(block * SCALE)
    ids = jnp.concatenate(
        [ids_ref[low, NODES : NODES + 16, :], ids_ref[up, NODES : NODES + 16, :]], axis=0
    )
    line, lane = row_and_lane(ids)
    below = iota((32, 128), 0) < 16
    ghost = (below & (lane == 127.0)) | (jnp.logical_not(below) & (lane == 0.0))
    if step == 2:
        ghost = ghost | (jnp.logical_not(below) & (lane == 1.0))
    upper = (iota((128, 128), 0) < iota((128, 128), 1)).astype(BF16)
    rank = jnp.dot(jnp.where(ghost, 1.0, 0.0).astype(BF16), upper, preferred_element_type=F32)
    info_ref[0] = jnp.where(ghost, rank, 255.0).astype(BF16)
    info_ref[1] = line.astype(BF16)
    info_ref[2] = jnp.where(below, 0.0, lane + 1.0).astype(BF16)
    sum_ref[...] = jnp.zeros_like(sum_ref)
    tasks = list_ref[8 + step, 0]

    def pick(table, hot):
        return lax.dot_general(table, hot, (((0,), (0,)), ((), ())), preferred_element_type=F32)

    def body(part, carry):
        first = part * 128
        number = (iota((128, 128), 0) + first).astype(F32)
        found = jnp.zeros((8, 128), F32)
        for row in range(4):
            entry = task_ref[step, row]
            start, count = entry[4:5], entry[5:6]
            hot = jnp.where((number >= start) & (number < start + count), 1.0, 0.0).astype(BF16)
            found = found + lax.dot_general(
                entry.astype(BF16), hot, (((1,), (1,)), ((), ())), preferred_element_type=F32
            )
        here = (iota((1, 128), 1) + first).astype(F32)
        nth = here - (256.0 * found[2:3] + found[3:4])
        live = here < tasks.astype(F32)
        hot_p = jnp.where(iota((32, 128), 0).astype(F32) == found[0:1], 1.0, 0.0).astype(BF16)
        hot_r = jnp.where(iota((128, 128), 0).astype(F32) == found[1:2], 1.0, 0.0).astype(BF16)
        match = pick(info_ref[0], hot_p) == nth
        line = jnp.sum(jnp.where(match, pick(info_ref[1], hot_p), 0.0), axis=0, keepdims=True)
        plane = jnp.sum(jnp.where(match, pick(info_ref[2], hot_p), 0.0), axis=0, keepdims=True)
        hot_p3 = jnp.concatenate([hot_p] * 3, axis=0)
        hot_r3 = jnp.concatenate([hot_r] * 3, axis=0)
        xi, xj = [], []
        for c in range(3):
            xi.append(jnp.sum(jnp.where(match, pick(near_ref[c], hot_p3), 0.0), axis=0, keepdims=True))
            xj.append(pick(all_ref[c], hot_r3))
        diff = [xi[c] - xj[c] for c in range(3)]
        dist = diff[0] * diff[0] + diff[1] * diff[1] + diff[2] * diff[2]
        w = jnp.exp2(-dist)
        lines = []
        for want in range(3):
            for c in range(3):
                f = jnp.sum(w * diff[c], axis=0, keepdims=True) * (1.0 / SCALE)
                lines.append(jnp.where(live & (plane == want), f, 0.0))
        lines.append(jnp.zeros((7, 128), F32))
        hi, lo = split2(jnp.concatenate(lines, axis=0))
        hot = one_hot(line, 128).astype(BF16)
        got = lax.dot_general(
            jnp.concatenate([hi, lo], axis=0), hot, (((1,), (1,)), ((), ())), preferred_element_type=F32
        )
        sum_ref[...] += got[0:16] + got[16:32]
        return carry

    lax.fori_loop(0, (tasks + 127) // 128, body, 0)
    square_ref[...] = jnp.zeros_like(square_ref)
    for want, k in enumerate((127, 0, 1)):
        for c in range(3):
            at = (k + 8 * c) % 128
            square_ref[at : at + 1, :] = sum_ref[3 * want + c : 3 * want + c + 1, :]
    return fill16(jnp.transpose(square_ref[...])[0:96].reshape(12, 8, 128))


def node_sum(elements):
    e = 0.125 * elements
    e = e + prev_z(e)
    e = e + prev_x(e)
    zero = jnp.zeros((1,) + e.shape[1:], F32)
    return jnp.concatenate([e, zero], axis=0) + jnp.concatenate([zero, e], axis=0)


def send_planes(planes, out_ref):
    count = len(planes)
    for n, plane in enumerate(planes):
        out_ref[n] = plane[:, :128]
    for g in range(0, count, 16):
        out_ref[count + g // 16] = pack([p[:, 128:] for p in planes[g : g + 16]])


def get_plane(ref, n, count):
    return both(ref[n], unpack(ref[count + n // 16], n % 16))


def row_plane(x, i):
    return fill16(x[:, i, :])


def first_contact_kernel(
    at_ref, list_ref, task_ref, all_ref, field_ref,
    fm_ref, c0_ref, m1_ref, up_ref, down_ref,
    turned_ref, force_ref, sum_ref, lhs_ref, lanes_ref, square_ref, *rim,
):
    me = at_ref[2]
    planes = neighbour_planes(all_ref, PLANES, 4, me, square_ref, 12)
    sums = [node_sum(both(fill16(field_ref[n]), unpack(planes, n, 4))) for n in range(4)]
    m1 = both(fill16(field_ref[4]), unpack(planes, 4, 4))
    zero = jnp.zeros((1, 16, 256), F32)
    m1 = jnp.concatenate([m1, zero], axis=0)
    m1_ref[...] = m1
    fm_ref[3] = sums[3]
    for c in range(3):
        fm_ref[c] = sums[c]
    pair_loop(list_ref, 0, 0, me, all_ref, turned_ref, force_ref, sum_ref)
    own = scatter_own(sum_ref, all_ref, me, lhs_ref, lanes_ref)
    rim = contact_rim(list_ref, task_ref, 0, 0, me, all_ref, all_ref, rim, square_ref)
    for c in range(3):
        full = jnp.concatenate([both(fill16(own[c]), unpack(rim, c)), zero], axis=0)
        c0_ref[c] = full
        fm_ref[c] = fm_ref[c] + full
    ups = [row_plane(fm_ref[n], 7) for n in range(4)] + [row_plane(fm_ref[n], 8) for n in range(4)]
    send_planes(ups + [row_plane(m1, 7)], up_ref)
    send_planes([row_plane(fm_ref[n], 0) for n in range(4)], down_ref)


def step_contact_kernel(
    at_ref, list_ref, all_ref, out_ref, turned_ref, force_ref, sum_ref, lhs_ref, lanes_ref
):
    me = at_ref[2]
    pair_loop(list_ref, 1, 0, me, all_ref, turned_ref, force_ref, sum_ref)
    out_ref[...] = scatter_own(sum_ref, all_ref, me, lhs_ref, lanes_ref)


def shift_rows(x, by):
    return pltpu.roll(x, by % x.shape[1], 1)


def x_extended_1(fm_ref, m1_ref, ups_ref, downs_ref, pick):
    lines = sorted(pick)
    row = iota((len(lines), 16, 256), 1)

    def lift(plane):
        return jnp.stack([jnp.broadcast_to(plane[j : j + 1], (16, 256)) for j in lines])

    def take(x):
        return jnp.stack([x[j] for j in lines])

    def extend(x, low, add, high):
        if add is not None:
            x = x + jnp.where(row == 0, lift(add), 0.0) + jnp.where(row == 8, lift(high), 0.0)
            x = jnp.where(row < 9, x, 0.0)
        else:
            x = jnp.where(row < 8, x, 0.0)
        return jnp.where(row == 0, lift(low), shift_rows(x, 1))

    out = [
        extend(
            take(fm_ref[n]),
            get_plane(ups_ref, n, 9),
            get_plane(ups_ref, 4 + n, 9),
            get_plane(downs_ref, n, 4),
        )
        for n in range(4)
    ]
    return out, extend(take(m1_ref[...]), get_plane(ups_ref, 8, 9), None, None)


def y_send_1_kernel(fm_ref, m1_ref, ups_ref, downs_ref, up_ref, down_ref):
    fields, m1 = x_extended_1(fm_ref, m1_ref, ups_ref, downs_ref, (0, 11, 12))
    send_planes([f[1] for f in fields] + [f[2] for f in fields] + [m1[1]], up_ref)
    send_planes([f[0] for f in fields], down_ref)


def stress_of(disp, modulus):
    grads = []
    for u in disp:
        s, d = u[1:] + u[:-1], u[1:] - u[:-1]
        sn = next_x(s)
        ss, xd = sn + s, sn - s
        yd = next_x(d) + d
        grads.append((xd + next_z(xd), yd + next_z(yd), next_z(ss) - ss))
    m = 0.25 * modulus
    exx, eyy, ezz = grads[0][0], grads[1][1], grads[2][2]
    trace = exx + eyy + ezz
    return (
        m * (2.0 * exx + trace),
        m * (2.0 * eyy + trace),
        m * (2.0 * ezz + trace),
        m * (grads[1][0] + grads[0][1]),
        m * (grads[2][1] + grads[1][2]),
        m * (grads[0][2] + grads[2][0]),
    )


def force_of(stress):
    xx, yy, zz, xy, yz, zx = stress
    out = []
    for a, b, c in ((xx, xy, zx), (xy, yy, yz), (zx, yz, zz)):
        az, bz, cz = a + prev_z(a), b + prev_z(b), prev_z(c) - c
        ac = (prev_x(az) - az) + (prev_x(cz) + cz)
        by = prev_x(bz) + bz
        out.append(-0.25 * ((ac[:-1] + ac[1:]) + (by[:-1] - by[1:])))
    return out


def gather_rows(disp, lanes_ref, rows_ref):
    hot = rows_ref[...]
    values = []
    for c in range(3):
        hi, lo = split2(disp[c])
        field = jnp.concatenate([hi, lo], axis=0)
        picked = lax.dot_general(field, hot, (((0,), (0,)), ((), ())), preferred_element_type=F32)
        values.append(jnp.sum(picked * lanes_ref[...].astype(F32), axis=0, keepdims=True))
    return values


def second_step_kernel(
    at_ref, fm_ref, c0_ref, m1_ref, xu_ref, xd_ref, yu_ref, yd_ref, c1_ref, all_ref,
    out_ref, state_ref, rows_ref, lanes_ref, square_ref,
):
    fields, m1 = x_extended_1(fm_ref, m1_ref, xu_ref, xd_ref, range(13))
    zero = jnp.zeros((1, 16, 256), F32)
    for n in range(4):
        low, add = get_plane(yu_ref, n, 9), get_plane(yu_ref, 4 + n, 9)
        own = fields[n]
        fields[n] = jnp.concatenate(
            [low[None], (own[0] + add)[None], own[1:12], (own[12] + get_plane(yd_ref, n, 4))[None]],
            axis=0,
        )
    m1 = jnp.concatenate([get_plane(yu_ref, 8, 9)[None], m1[:12]], axis=0)
    mass = fields[3]
    inv = jnp.where(mass > 0.0, DT / jnp.where(mass > 0.0, mass, 1.0), 0.0)
    disp1 = [DT * (inv * fields[c]) for c in range(3)]
    force = force_of([jnp.concatenate([x, zero], axis=0) for x in stress_of(disp1, m1)])
    inv = inv[1:]
    row = iota((13, 16, 256), 1)
    good = (row > 0) & (row < 10)
    disp2s, vel2s = [], []
    for c in range(3):
        c1 = jnp.concatenate([fill16(c1_ref[c]), jnp.zeros((1, 16, 128), F32)], axis=0)
        c1 = shift_rows(both(c1, jnp.zeros((13, 16, 128), F32)), 1)
        total = fields[c][1:]
        accel = inv * (total - shift_rows(c0_ref[c], 1))
        vel2 = inv * total + inv * force[c] + (accel + inv * c1)
        disp2 = disp1[c][1:] + DT * vel2
        back = [shift_rows(jnp.where(good, x, 0.0), -1) for x in (disp2, vel2, accel)]
        disp2s.append(back[0])
        vel2s.append(back[1])
        state_ref[c] = back[0]
        state_ref[3 + c] = back[1]
        state_ref[6 + c] = back[2]
    state_ref[9] = shift_rows(jnp.where(good, inv, 0.0), -1)
    me = at_ref[2]
    for s in range(16):
        at = slice(128 * s, 128 * s + 128)
        r, l = row_and_lane(all_ref[me, NODES + s : NODES + s + 1, :])
        hot = one_hot(r, 96).astype(BF16)
        rows_ref[0:96, at] = hot
        rows_ref[96:192, at] = hot
        lanes_ref[:, at] = one_hot(l, 128).astype(BF16)
    for first, disp in (
        (0, [shift_rows(d[1:13], -1)[:, :8, :128] for d in disp1]),
        (LATE, [d[0:12, :8, :128] for d in disp2s]),
    ):
        values = gather_rows([d.reshape(96, 128) for d in disp], lanes_ref, rows_ref)
        for c in range(3):
            block = jnp.concatenate(
                [values[c][:, 128 * s : 128 * s + 128] for s in range(16)], axis=0
            ) + all_ref[me, 16 * c : 16 * c + 16, :]
            for dest in range(8):
                out_ref[dest, first + 16 * c : first + 16 * c + 16, :] = block
    rows = planes_to_rows(pack([x[:, :, :128] for x in disp2s + vel2s], 5), square_ref)
    for dest in range(8):
        out_ref[dest, PLANES_2:ROWS_2, :] = rows


UP_LIST = (
    [(n, 0) for n in range(3)] + [(n, 1) for n in range(3)] + [(n, 1) for n in (3, 4, 5, 9)]
    + [(10, 0), (10, 1), (11, 1)]
)
DOWN_LIST = (
    [(n, p) for p in (0, 1, 2) for n in range(3)]
    + [(n, p) for p in (0, 1) for n in (3, 4, 5)]
    + [(n, 0) for n in (6, 7, 8)]
    + [(9, 0), (9, 1), (10, 0), (10, 1), (11, 0)]
)
UPS, DOWNS = len(UP_LIST), len(DOWN_LIST)


def plane_of(ref, listed, n, p):
    return get_plane(ref, listed.index((n, p)), len(listed)) if (n, p) in listed else None


def late_contact_kernel(
    at_ref, list_ref, task_ref, first_ref, all_ref, state_ref, field_ref,
    own_ref, up_ref, down_ref,
    turned_ref, force_ref, sum_ref, lhs_ref, lanes_ref, square_ref, *rims,
):
    me = at_ref[2]
    zplanes = neighbour_planes(all_ref, PLANES_2, 5, me, square_ref, 13)
    mplanes = neighbour_planes(first_ref, PLANES, 4, me, square_ref, 12)
    top = (iota((13, 16, 128), 2) == 0) & (me == 7)
    zero = jnp.zeros((1, 16, 256), F32)

    def with_rim(own, n):
        return both(own[:, :, :128], jnp.where(top, own[:, :, 128:], unpack(zplanes, n, 5)))

    inv = state_ref[9]
    own_ref[9] = inv
    for c in range(3):
        own_ref[c] = with_rim(state_ref[c], c)
        own_ref[3 + c] = with_rim(state_ref[3 + c], 3 + c) + state_ref[6 + c]
        own_ref[6 + c] = state_ref[6 + c]
    for n, step in ((10, 2), (11, 3)):
        m = both(fill16(field_ref[3 + step]), unpack(mplanes, 3 + step, 4))
        own_ref[n] = jnp.concatenate([m, zero], axis=0)
    for step, first_row, n in ((2, 0, 3), (3, LATE, 6)):
        pair_loop(list_ref, step, first_row, me, all_ref, turned_ref, force_ref, sum_ref)
        own = scatter_own(sum_ref, first_ref, me, lhs_ref, lanes_ref)
        rim = contact_rim(list_ref, task_ref, step, first_row, me, all_ref, first_ref, rims, square_ref)
        for c in range(3):
            full = both(fill16(own[c]), unpack(rim, c))
            own_ref[n + c, 0:12] = own_ref[n + c, 0:12] + own_ref[9, 0:12] * full
    send_planes([row_plane(own_ref[n], 6 + p) for n, p in UP_LIST], up_ref)
    send_planes([row_plane(own_ref[n], p) for n, p in DOWN_LIST], down_ref)


def x_extended_2(own_ref, ups_ref, downs_ref, at_last, lines):
    row = iota((len(lines), 16, 256), 1)
    keep = (row < 8) | ((row == 8) & at_last)

    def lift(plane):
        return jnp.stack([jnp.broadcast_to(plane[j : j + 1], (16, 256)) for j in lines])

    out = []
    for n in range(12):
        x = jnp.stack([own_ref[n, j] for j in lines])
        x = shift_rows(jnp.where(keep, x, 0.0), 2)
        for ref, listed, first, count in ((ups_ref, UP_LIST, 0, 2), (downs_ref, DOWN_LIST, 10, 3)):
            for p in range(count):
                got = plane_of(ref, listed, n, p)
                if got is not None:
                    add = lift(got)
                    if first + p == 10:
                        x = jnp.where((row == 10) & jnp.logical_not(at_last), add, x)
                    else:
                        x = jnp.where(row == first + p, add, x)
        out.append(x)
    return out


def y_send_2_kernel(at_ref, own_ref, ups_ref, downs_ref, up_ref, down_ref):
    fields = x_extended_2(own_ref, ups_ref, downs_ref, at_ref[0] == 7, (0, 1, 2, 10, 11))
    send_planes([fields[n][3 + p] for n, p in UP_LIST], up_ref)
    send_planes([fields[n][p] for n, p in DOWN_LIST], down_ref)


def last_kernel(at_ref, own_ref, xu_ref, xd_ref, yu_ref, yd_ref, vel_ref, stress_ref):
    fields = x_extended_2(own_ref, xu_ref, xd_ref, at_ref[0] == 7, range(13))
    y_last = at_ref[1] == 3
    none = jnp.zeros((16, 256), F32)
    wide = []
    for n in range(12):
        planes = [plane_of(yu_ref, UP_LIST, n, p) for p in (0, 1)]
        planes += [fields[n][j] for j in range(12)]
        after = [plane_of(yd_ref, DOWN_LIST, n, p) for p in (0, 1, 2)]
        after = [none if p is None else p for p in after]
        after[0] = jnp.where(y_last, fields[n][12], after[0])
        planes = [none if p is None else p for p in planes] + after
        wide.append(jnp.stack(planes))
    disp2, vh3, g3, inv, m2, m3 = wide[0:3], wide[3:6], wide[6:9], wide[9], wide[10], wide[11]
    force = force_of(stress_of(disp2, m2[:16]))
    vel3 = [vh3[c][1:16] + inv[1:16] * force[c] for c in range(3)]
    disp3 = [disp2[c][1:16] + DT * vel3[c] for c in range(3)]
    force = force_of(stress_of(disp3, m3[1:15]))
    vel4 = [vel3[c][1:14] + (inv[2:15] * force[c] + g3[c][2:15]) for c in range(3)]
    disp4 = [disp3[c][1:14] + DT * vel4[c] for c in range(3)]
    stress = stress_of(disp4, m3[2:14])
    for n in range(6):
        stress_ref[n] = shift_rows(stress[n][:, :, :128], -2)[:, :8, :]
    for c in range(3):
        s = vel4[c][1:] + vel4[c][:-1]
        s = s + next_x(s)
        s = s + next_z(s)
        vel_ref[c] = shift_rows(0.125 * s[:, :, :128], -2)[:, :8, :]


def call(kernel, outs, specs, scratch=(), held=()):
    def run(*args):
        spaces = [pltpu.VMEM if spec is HELD else pltpu.HBM if spec is FAR else None for spec in specs]
        args = [
            a if space is None else pltpu.with_memory_space_constraint(a, space)
            for a, space in zip(args, spaces)
        ]
        return pl.pallas_call(
            kernel,
            out_shape=[
                pltpu.VMEM(s, d) if n in held else jax.ShapeDtypeStruct(s, d)
                for n, (s, d) in enumerate(outs)
            ],
            in_specs=specs,
            out_specs=[VMEM] * len(outs),
            scratch_shapes=list(scratch),
            compiler_params=PARAMS,
        )(*args)

    return run


def share(blocks):
    return lax.all_to_all(blocks, "gz", split_axis=0, concat_axis=0, tiled=True)


def neighbours(up, down, axis):
    count = lax.axis_size(axis)
    ahead = [(i, i + 1) for i in range(count - 1)]
    return lax.ppermute(up, axis, ahead), lax.ppermute(down, axis, [(j, i) for i, j in ahead])


TURNED = pltpu.VMEM((17, 4, 3, 8, 128), F32)
SUMS = pltpu.VMEM((3, 16, 128), F32)
RIM = [
    pltpu.VMEM((3, 384, 128), BF16),
    pltpu.VMEM((3, 96, 128), BF16),
    pltpu.VMEM((3, 32, 128), BF16),
    pltpu.VMEM((16, 128), F32),
]
LHS = pltpu.VMEM((576, 2048), BF16)
LANES = pltpu.VMEM((128, 2048), BF16)
SQUARE = pltpu.VMEM((128, 128), F32)


def per_device(stiffness, density, load, alive, surf_coords, surf_nodes, routes, pairs):
    at = jnp.stack([lax.axis_index(a) for a in ("gx", "gy", "gz")]).astype(jnp.int32)
    stiffness, density = jnp.swapaxes(stiffness, 0, 1), jnp.swapaxes(density, 0, 1)
    load, alive = jnp.swapaxes(load, 1, 2), jnp.swapaxes(alive, 1, 2)
    coords = jnp.swapaxes(surf_coords, 0, 1)
    pairs = jnp.swapaxes(pairs[:, 0], 1, 2)
    params = (coords, routes, pairs, surf_nodes, stiffness, density, load, alive)
    payload, fields = call(
        prep_kernel,
        [((8, ROWS_1, 128), F32), ((7, 12, 8, 128), F32)],
        [SMEM] + [FAR] * 8,
        [SQUARE] + [pltpu.VMEM(p.shape, p.dtype) for p in params] + [pltpu.SemaphoreType.DMA((8,))],
        (1,),
    )(at, *params)
    everyone = share(payload)
    lists, tasks = call(plan_kernel, [((12, 512), jnp.int32), ((4, 4, 8, 128), F32)], [SMEM, HELD], (), (1,))(at, everyone)
    fm, c0, m1, up, down = call(
        first_contact_kernel,
        [((4, 13, 16, 256), F32), ((3, 13, 16, 256), F32), ((13, 16, 256), F32), ((10, 16, 128), F32),
         ((5, 16, 128), F32)],
        [SMEM, SMEM, HELD, HELD, HELD],
        [TURNED, TURNED, SUMS, LHS, LANES, SQUARE] + RIM,
        (0, 1, 2),
    )(at, lists, tasks, everyone, fields)
    xu, xd = neighbours(up, down, "gx")
    (c1,) = call(
        step_contact_kernel,
        [((3, 12, 8, 128), F32)],
        [SMEM, SMEM, HELD],
        [TURNED, TURNED, SUMS, LHS, LANES],
        (0,),
    )(at, lists, everyone)
    up, down = call(y_send_1_kernel, [((10, 16, 128), F32), ((5, 16, 128), F32)], [HELD] * 4)(
        fm, m1, xu, xd
    )
    yu, yd = neighbours(up, down, "gy")
    payload, state = call(
        second_step_kernel,
        [((8, ROWS_2, 128), F32), ((10, 13, 16, 256), F32)],
        [SMEM] + [HELD] * 9,
        [pltpu.VMEM((192, 2048), BF16), LANES, SQUARE],
        (1,),
    )(at, fm, c0, m1, xu, xd, yu, yd, c1, everyone)
    late = share(payload)
    own, up, down = call(
        late_contact_kernel,
        [((12, 13, 16, 256), F32), ((UPS + 1, 16, 128), F32), ((DOWNS + 2, 16, 128), F32)],
        [SMEM, SMEM] + [HELD] * 5,
        [TURNED, TURNED, SUMS, LHS, LANES, SQUARE] + RIM,
        (0,),
    )(at, lists, tasks, everyone, late, state, fields)
    xu, xd = neighbours(up, down, "gx")
    up, down = call(
        y_send_2_kernel,
        [((UPS + 1, 16, 128), F32), ((DOWNS + 2, 16, 128), F32)],
        [SMEM] + [HELD] * 3,
    )(at, own, xu, xd)
    yu, yd = neighbours(up, down, "gy")
    vel, stress = call(
        last_kernel,
        [((3, 12, 8, 128), F32), ((6, 12, 8, 128), F32)],
        [SMEM] + [HELD] * 5,
    )(at, own, xu, xd, yu, yd)
    return jnp.swapaxes(vel, 1, 2), jnp.swapaxes(stress, 1, 2)


def solution(mesh):
    return jax.shard_map(
        per_device,
        mesh=mesh,
        in_specs=(
            P("gx", "gy", "gz"),
            P("gx", "gy", "gz"),
            P(None, "gx", "gy", "gz"),
            P(None, "gx", "gy", "gz"),
            P(("gx", "gy", "gz"), None, None),
            P(("gx", "gy", "gz"), None),
            P(None, ("gx", "gy", "gz")),
            P(None, ("gx", "gy", "gz"), None, None),
        ),
        out_specs=(P(None, "gx", "gy", "gz"), P(None, "gx", "gy", "gz")),
        check_vma=False,
    )
```

```python
import functools
import math
import jax
import jax.numpy as jnp
from jax import lax
from jax.experimental import pallas as pl
from jax.experimental.pallas import tpu as pltpu
from jax.sharding import PartitionSpec as P

F32 = jnp.float32
BF16 = jnp.bfloat16
SCALE = math.sqrt(math.log2(math.e) / 0.08)
DT = 0.2
PARAMS = pltpu.CompilerParams(vmem_limit_bytes=20 * 2**20)
VMEM = pl.BlockSpec(memory_space=pltpu.VMEM)
SMEM = pl.BlockSpec(memory_space=pltpu.SMEM)
HELD = pl.BlockSpec(memory_space=pltpu.VMEM)
FAR = pl.BlockSpec(memory_space=pltpu.HBM)
KEYS, PAIRS, NODES, PLANES = 48, 52, 56, 72
ROWS_1 = 104
LATE, PLANES_2 = 48, 96
ROWS_2 = 128
PLANE_ROWS = 32


def split2(x):
    hi = x.astype(BF16)
    return hi, (x - hi.astype(F32)).astype(BF16)


def iota(shape, dim):
    return lax.broadcasted_iota(jnp.int32, shape, dim)


def rim_lanes(shape, above=3):
    lane = iota(shape, len(shape) - 1)
    return (lane >= 126) | (lane < above)


def roll_last(x, shift):
    shift = shift % x.shape[-1]
    return pltpu.roll(x, shift, x.ndim - 1) if shift else x


def pack(tiles, stride=8):
    total = None
    for f, tile in enumerate(tiles):
        part = roll_last(jnp.where(rim_lanes(tile.shape, min(stride - 2, 3)), tile, 0.0), stride * f)
        total = part if total is None else total + part
    return total


def unpack(packed, f, stride=8):
    return jnp.where(
        rim_lanes(packed.shape, min(stride - 2, 3)), roll_last(packed, -stride * f), 0.0
    )


def both(main, rim):
    return jnp.concatenate([main, rim], axis=-1)


def fill16(x):
    pad = 16 - x.shape[-2]
    if not pad:
        return x
    return jnp.concatenate([x, jnp.zeros(x.shape[:-2] + (pad, x.shape[-1]), x.dtype)], axis=-2)


def next_x(x):
    return pltpu.roll(x, x.shape[1] - 1, 1)


def prev_x(x):
    return pltpu.roll(x, 1, 1)


def next_z(x):
    return roll_last(x, -1)


def prev_z(x):
    return roll_last(x, 1)


def planes_to_rows(packed, square_ref):
    square_ref[...] = jnp.zeros_like(square_ref)
    for j in range(packed.shape[0]):
        square_ref[9 * j : 9 * j + 9, :] = packed[j, 0:9, :]
    return jnp.transpose(roll_last(square_ref[...], 2))[0:PLANE_ROWS]


def rows_to_planes(rows, square_ref, planes):
    full = jnp.concatenate([rows, jnp.zeros((128 - PLANE_ROWS, 128), F32)], axis=0)
    square_ref[...] = roll_last(jnp.transpose(full), -2)
    return jnp.stack([fill16(square_ref[9 * j : 9 * j + 9, :]) for j in range(planes)])


def neighbour_planes(all_ref, first_row, stride, me, square_ref, planes):
    low = all_ref[jnp.maximum(me - 1, 0), first_row : first_row + PLANE_ROWS, :]
    up = all_ref[jnp.minimum(me + 1, 7), first_row : first_row + PLANE_ROWS, :]
    kind = iota((PLANE_ROWS, 128), 0) % stride
    low = jnp.where((kind < 2) & (me > 0), low, 0.0)
    up = jnp.where((kind >= 2) & (me < 7), up, 0.0)
    return rows_to_planes(low + up, square_ref, planes)


def spread(x, first):
    to = (iota((x.shape[1], 128), 1) == iota((x.shape[1], 128), 0) + first).astype(BF16)
    return jnp.dot(x.astype(BF16), to, preferred_element_type=F32)


def prep_kernel(at_ref, *refs):
    far, (out_ref, field_ref, square_ref) = refs[:8], refs[8:11]
    near, sems = refs[11:19], refs[19]
    copies = [pltpu.make_async_copy(a, b, sems.at[n]) for n, (a, b) in enumerate(zip(far, near))]
    for copy in copies:
        copy.start()
    for copy in copies:
        copy.wait()
    coords_ref, routes_ref, pairs_ref, nodes_ref, stiff_ref, dens_ref, load_ref, alive_ref = near
    me = at_ref[2]
    for c in range(3):
        field_ref[c] = load_ref[c]
    field_ref[3] = dens_ref[...]
    for step in (1, 2, 3):
        field_ref[3 + step] = stiff_ref[...] * alive_ref[step].astype(F32)
    rows = planes_to_rows(pack([fill16(field_ref[n]) for n in range(7)], 4), square_ref)
    nodes = nodes_ref[...].astype(F32)
    routes = routes_ref[...].astype(F32)
    rank = jnp.zeros((4, 16), F32)
    later = iota((4, 16), 1)
    for s in range(15):
        same = jnp.broadcast_to(routes[:, s : s + 1], (4, 16)) == routes
        rank = rank + jnp.where(same & (later > s), 1.0, 0.0)
    keys = spread(routes * 32.0 + rank + 4.0 * me.astype(F32), 16 * me)
    lists = spread(pairs_ref[:, 0, :].astype(F32), 0) + spread(pairs_ref[:, 1, :].astype(F32), 64)
    for dest in range(8):
        for c in range(3):
            out_ref[dest, 16 * c : 16 * c + 16, :] = coords_ref[c]
        out_ref[dest, KEYS : KEYS + 4, :] = keys
        out_ref[dest, PAIRS : PAIRS + 4, :] = lists
        out_ref[dest, NODES : NODES + 16, :] = nodes
        out_ref[dest, PLANES:ROWS_1, :] = rows


def plan_kernel(at_ref, all_ref, *refs, steps):
    list_ref, task_ref = refs[-2:]
    me = at_ref[2]
    lane = iota((1, 128), 1)
    block_of = iota((128, 128), 0).astype(F32)
    eye = iota((128, 128), 0) == iota((128, 128), 1)
    upper = (iota((128, 128), 0) < iota((128, 128), 1)).astype(BF16)
    place = iota((128, 128), 0).astype(F32)
    row8 = iota((8, 128), 0)
    src_of = iota((128, 1), 0) // 16

    def nodes_at(src, wants, real):
        ids = all_ref[src, NODES : NODES + 16, :]
        k = ids - 128.0 * jnp.floor(ids * (1.0 / 128.0))
        hit = k == wants[0]
        for want in wants[1:]:
            hit = hit | (k == want)
        count = jnp.sum(jnp.where(hit, 1.0, 0.0), axis=1, keepdims=True)
        return jnp.where(src_of == real, jnp.concatenate([count] * 8, axis=0), 0.0)

    low = nodes_at(jnp.maximum(me - 1, 0), (127.0,), me - 1)
    up = jnp.minimum(me + 1, 7)
    up0, up01 = nodes_at(up, (0.0,), me + 1), nodes_at(up, (0.0, 1.0), me + 1)
    rims = {0: low + up0, 2: low + up01, 3: up0}
    mine_first = (16 * me).astype(F32)

    def prefix(x):
        return jnp.dot(jnp.broadcast_to(x, (8, 128)).astype(BF16), upper, preferred_element_type=F32)[0:1]

    for step in steps:
        keys = all_ref[0, KEYS + step : KEYS + 1 + step, :]
        for src in range(1, 8):
            keys = keys + all_ref[src, KEYS + step : KEYS + 1 + step, :]
        key_col = jnp.sum(jnp.where(eye, keys, 0.0), axis=1, keepdims=True)
        base = jnp.zeros((1, 1), F32)
        tasks = jnp.zeros((1, 1), F32)
        spots, codes = [], []
        for row in range(4):
            even = all_ref[2 * row, PAIRS + step : PAIRS + 1 + step, :]
            odd = all_ref[2 * row + 1, PAIRS + step : PAIRS + 1 + step, :]
            left = lane < 64
            first = jnp.where(left, even, pltpu.roll(odd, 64, 1))
            second = jnp.where(left, pltpu.roll(even, 64, 1), odd)
            box = jnp.where(left, 64.0 * row, 64.0 * row + 32.0)
            hit_first = key_col == first + box
            hit_second = key_col == second + box
            p_block = jnp.sum(jnp.where(hit_first, block_of + 1.0, 0.0), axis=0, keepdims=True) - 1.0
            r_block = jnp.sum(jnp.where(hit_second, block_of + 1.0, 0.0), axis=0, keepdims=True) - 1.0
            p_slot = p_block - mine_first
            live = r_block >= 0.0
            mine = live & (p_slot >= 0.0) & (p_slot < 16.0)
            sel = jnp.where(mine, 1.0, 0.0)
            spots.append(jnp.where(mine, prefix(sel) + base, -1.0))
            base = base + jnp.sum(sel, axis=1, keepdims=True)
            code = jnp.where(
                row8 == 0, jnp.broadcast_to(p_slot, (8, 128)), jnp.broadcast_to(r_block, (8, 128))
            )
            codes.append(jnp.where(jnp.broadcast_to(mine, (8, 128)), code, 0.0).astype(BF16))
            if step in rims:
                count = jnp.sum(jnp.where(hit_first, rims[step], 0.0), axis=0, keepdims=True)
                count = jnp.where(live, count, 0.0)
                start = prefix(count) + tasks
                tasks = tasks + jnp.sum(count, axis=1, keepdims=True)
                high = jnp.floor(start * (1.0 / 256.0))
                rim_block = jnp.where(p_slot < 0.0, p_slot + 16.0, p_slot)
                some = jnp.broadcast_to(count > 0.0, (8, 128))
                table = jnp.zeros((8, 128), F32)
                for n, line in enumerate((rim_block, r_block, high, start - 256.0 * high, start, count)):
                    table = jnp.where(row8 == n, jnp.broadcast_to(line, (8, 128)), table)
                task_ref[step, row] = jnp.where(some, table, 0.0)
        list_ref[4 + step : 5 + step, :] = jnp.broadcast_to(base, (1, 512)).astype(jnp.int32)
        list_ref[8 + step : 9 + step, :] = jnp.broadcast_to(tasks, (1, 512)).astype(jnp.int32)
        count = jnp.max(base)
        for part in range(4):

            def write(part=part, spots=spots, codes=codes, base=base, step=step):
                total = jnp.zeros((8, 128), F32)
                for row in range(4):
                    onehot = jnp.where(place == spots[row] - 128.0 * part, 1.0, 0.0).astype(BF16)
                    total = total + lax.dot_general(
                        codes[row], onehot, (((1,), (1,)), ((), ())), preferred_element_type=F32
                    )
                used = (lane + 128 * part).astype(F32) < base
                code = jnp.where(used, total[0:1] * 128.0 + total[1:2], 16.0 * 128.0)
                list_ref[step : step + 1, 128 * part : 128 * part + 128] = code.astype(jnp.int32)

            if part == 0:
                write()
            else:
                pl.when(count + 8.0 > 128.0 * part)(write)


UNROLL = 8


def pair_loop(list_ref, step, first_row, me, all_ref, turned_ref, force_ref, part=(0, 1)):
    for c in range(3):
        turned_ref[16, :, c] = jnp.zeros((4, 8, 128), F32)
        for s in range(16):
            wide = jnp.broadcast_to(all_ref[me, first_row + 16 * c + s : first_row + 16 * c + s + 1, :] * SCALE, (8, 128))
            for a in range(4):
                turned_ref[s, a, c] = roll_last(wide, 32 * a)

    def one(q):
        code = list_ref[step, q]
        slot = lax.shift_right_logical(code, 7)
        src = lax.shift_right_logical(code & 127, 4)
        line = first_row + (code & 15)
        xj = []
        for c in range(3):
            wide = jnp.broadcast_to(all_ref[src, pl.ds(line + 16 * c, 1), :] * SCALE, (8, 128))
            wide = pltpu.roll(wide, 0, 1, stride=1, stride_axis=0)
            xj.append([roll_last(wide, 8 * b) for b in range(4)])
        out = []
        for a in range(4):
            xi = [turned_ref[slot, a, c] for c in range(3)]
            acc = [None] * 3
            for b in range(4):
                diff = [xi[c] - xj[c][b] for c in range(3)]
                dist = diff[0] * diff[0] + diff[1] * diff[1] + diff[2] * diff[2]
                w = jnp.exp2(-dist)
                acc = [w * diff[c] if b == 0 else acc[c] + w * diff[c] for c in range(3)]
            out.append(acc)
        return slot, out

    def body(g, carry):
        done = [one(g * UNROLL + u) for u in range(UNROLL)]
        for slot, out in done:
            for a in range(4):
                for c in range(3):
                    force_ref[slot, a, c] += out[a][c]
        return carry

    groups = (list_ref[4 + step, 0] + (UNROLL - 1)) // UNROLL
    at, of = part
    lax.fori_loop(groups * at // of, groups * (at + 1) // of, body, 0)


def block_sums(force_ref, sum_ref):
    for c in range(3):
        total = force_ref[0:16, 0, c]
        for a in range(1, 4):
            total = total + roll_last(force_ref[0:16, a, c], -32 * a)
        sum_ref[c] = jnp.sum(total, axis=1) * (1.0 / SCALE)


def row_and_lane(ids):
    line = jnp.floor(ids * (1.0 / 128.0))
    lane = ids - 128.0 * line
    i = jnp.floor((line + 0.5) * (1.0 / 12.0))
    return 8.0 * line - 95.0 * i, lane


def one_hot(at, rows):
    return jnp.where(iota((rows, 128), 0).astype(F32) == at, 1.0, 0.0)


def hot_rows_lanes(ids):
    row, lane = row_and_lane(ids)
    return one_hot(row, 96).astype(BF16), one_hot(lane, 128)


def first_plan_kernel(at_ref, all_ref, list_ref, task_ref, rows_ref, lanes_ref):
    plan_kernel(at_ref, all_ref, list_ref, task_ref, steps=(0, 1))
    for s in range(16):
        at = slice(128 * s, 128 * s + 128)
        rows_ref[:, at], lanes = hot_rows_lanes(all_ref[at_ref[2], NODES + s : NODES + s + 1, :])
        lanes_ref[at, :] = jnp.transpose(lanes).astype(BF16)


def scatter_own(force_ref, sum_ref, rows_ref, lanes_ref, lhs_ref):
    block_sums(force_ref, sum_ref)
    for s in range(16):
        at = slice(128 * s, 128 * s + 128)
        hot = rows_ref[:, at]
        for c in range(3):
            hi, lo = split2(sum_ref[c, s : s + 1, :])
            lhs_ref[96 * c : 96 * c + 96, at] = hot * hi
            lhs_ref[288 + 96 * c : 384 + 96 * c, at] = hot * lo
    out = jnp.dot(lhs_ref[...], lanes_ref[...], preferred_element_type=F32)
    return (out[:288] + out[288:]).reshape(3, 12, 8, 128)


def split3(x):
    hi, rest = x.astype(BF16), x
    rest = rest - hi.astype(F32)
    mid = rest.astype(BF16)
    return jnp.concatenate([hi, mid, (rest - mid.astype(F32)).astype(BF16)], axis=0)


def contact_rim(list_ref, task_ref, step, first_row, me, pos_ref, ids_ref, rim, square_ref):
    all_ref, near_ref, info_ref, sum_ref = rim
    low, up = jnp.maximum(me - 1, 0), jnp.minimum(me + 1, 7)
    for c in range(3):
        at = first_row + 16 * c
        block = jnp.concatenate([pos_ref[src, at : at + 16, :] for src in range(8)], axis=0)
        all_ref[c] = split3(block * SCALE)
        block = jnp.concatenate([pos_ref[low, at : at + 16, :], pos_ref[up, at : at + 16, :]], axis=0)
        near_ref[c] = split3(block * SCALE)
    ids = jnp.concatenate(
        [ids_ref[low, NODES : NODES + 16, :], ids_ref[up, NODES : NODES + 16, :]], axis=0
    )
    line, lane = row_and_lane(ids)
    below = iota((32, 128), 0) < 16
    ghost = (below & (lane == 127.0)) | (jnp.logical_not(below) & (lane == 0.0))
    if step == 2:
        ghost = ghost | (jnp.logical_not(below) & (lane == 1.0))
    upper = (iota((128, 128), 0) < iota((128, 128), 1)).astype(BF16)
    rank = jnp.dot(jnp.where(ghost, 1.0, 0.0).astype(BF16), upper, preferred_element_type=F32)
    info_ref[0] = jnp.where(ghost, rank, 255.0).astype(BF16)
    info_ref[1] = line.astype(BF16)
    info_ref[2] = jnp.where(below, 0.0, lane + 1.0).astype(BF16)
    sum_ref[...] = jnp.zeros_like(sum_ref)
    tasks = list_ref[8 + step, 0]

    def pick(table, hot):
        return lax.dot_general(table, hot, (((0,), (0,)), ((), ())), preferred_element_type=F32)

    def body(part, carry):
        first = part * 128
        number = (iota((128, 128), 0) + first).astype(F32)
        found = jnp.zeros((8, 128), F32)
        for row in range(4):
            entry = task_ref[step, row]
            start, count = entry[4:5], entry[5:6]
            hot = jnp.where((number >= start) & (number < start + count), 1.0, 0.0).astype(BF16)
            found = found + lax.dot_general(
                entry.astype(BF16), hot, (((1,), (1,)), ((), ())), preferred_element_type=F32
            )
        here = (iota((1, 128), 1) + first).astype(F32)
        nth = here - (256.0 * found[2:3] + found[3:4])
        live = here < tasks.astype(F32)
        hot_p = jnp.where(iota((32, 128), 0).astype(F32) == found[0:1], 1.0, 0.0).astype(BF16)
        hot_r = jnp.where(iota((128, 128), 0).astype(F32) == found[1:2], 1.0, 0.0).astype(BF16)
        match = pick(info_ref[0], hot_p) == nth
        line = jnp.sum(jnp.where(match, pick(info_ref[1], hot_p), 0.0), axis=0, keepdims=True)
        plane = jnp.sum(jnp.where(match, pick(info_ref[2], hot_p), 0.0), axis=0, keepdims=True)
        hot_p3 = jnp.concatenate([hot_p] * 3, axis=0)
        hot_r3 = jnp.concatenate([hot_r] * 3, axis=0)
        xi, xj = [], []
        for c in range(3):
            xi.append(jnp.sum(jnp.where(match, pick(near_ref[c], hot_p3), 0.0), axis=0, keepdims=True))
            xj.append(pick(all_ref[c], hot_r3))
        diff = [xi[c] - xj[c] for c in range(3)]
        dist = diff[0] * diff[0] + diff[1] * diff[1] + diff[2] * diff[2]
        w = jnp.exp2(-dist)
        lines = []
        for want in range(3):
            for c in range(3):
                f = jnp.sum(w * diff[c], axis=0, keepdims=True) * (1.0 / SCALE)
                lines.append(jnp.where(live & (plane == want), f, 0.0))
        lines.append(jnp.zeros((7, 128), F32))
        hi, lo = split2(jnp.concatenate(lines, axis=0))
        hot = one_hot(line, 128).astype(BF16)
        got = lax.dot_general(
            jnp.concatenate([hi, lo], axis=0), hot, (((1,), (1,)), ((), ())), preferred_element_type=F32
        )
        sum_ref[...] += got[0:16] + got[16:32]
        return carry

    lax.fori_loop(0, (tasks + 127) // 128, body, 0)
    square_ref[...] = jnp.zeros_like(square_ref)
    for want, k in enumerate((127, 0, 1)):
        for c in range(3):
            at = (k + 8 * c) % 128
            square_ref[at : at + 1, :] = sum_ref[3 * want + c : 3 * want + c + 1, :]
    return fill16(jnp.transpose(square_ref[...])[0:96].reshape(12, 8, 128))


def node_sum(elements):
    e = 0.125 * elements
    e = e + prev_z(e)
    e = e + prev_x(e)
    zero = jnp.zeros((1,) + e.shape[1:], F32)
    return jnp.concatenate([e, zero], axis=0) + jnp.concatenate([zero, e], axis=0)


def send_planes(planes, out_ref):
    count = len(planes)
    for n, plane in enumerate(planes):
        out_ref[n] = plane[:, :128]
    for g in range(0, count, 16):
        out_ref[count + g // 16] = pack([p[:, 128:] for p in planes[g : g + 16]])


def get_plane(ref, n, count):
    return both(ref[n], unpack(ref[count + n // 16], n % 16))


def row_plane(x, i):
    return fill16(x[:, i, :])


def first_contact_kernel(
    at_ref, list_ref, task_ref, all_ref, field_ref, rows_ref, lanes_ref,
    fm_ref, c0_ref, m1_ref, up_ref, down_ref,
    turned_ref, force_ref, sum_ref, lhs_ref, square_ref, *rim,
):
    me = at_ref[2]
    planes = neighbour_planes(all_ref, PLANES, 4, me, square_ref, 12)
    sums = [node_sum(both(fill16(field_ref[n]), unpack(planes, n, 4))) for n in range(4)]
    m1 = both(fill16(field_ref[4]), unpack(planes, 4, 4))
    zero = jnp.zeros((1, 16, 256), F32)
    m1 = jnp.concatenate([m1, zero], axis=0)
    m1_ref[...] = m1
    fm_ref[3] = sums[3]
    for c in range(3):
        fm_ref[c] = sums[c]
    force_ref[...] = jnp.zeros_like(force_ref)
    pair_loop(list_ref, 0, 0, me, all_ref, turned_ref, force_ref)
    own = scatter_own(force_ref, sum_ref, rows_ref, lanes_ref, lhs_ref)
    rim = contact_rim(list_ref, task_ref, 0, 0, me, all_ref, all_ref, rim, square_ref)
    for c in range(3):
        full = jnp.concatenate([both(fill16(own[c]), unpack(rim, c)), zero], axis=0)
        c0_ref[c] = full
        fm_ref[c] = fm_ref[c] + full
    ups = [row_plane(fm_ref[n], 7) for n in range(4)] + [row_plane(fm_ref[n], 8) for n in range(4)]
    send_planes(ups + [row_plane(m1, 7)], up_ref)
    send_planes([row_plane(fm_ref[n], 0) for n in range(4)], down_ref)


def step_contact_kernel(
    at_ref, list_ref, all_ref, rows_ref, lanes_ref, out_ref, turned_ref, force_ref, sum_ref, lhs_ref
):
    force_ref[...] = jnp.zeros_like(force_ref)
    pair_loop(list_ref, 1, 0, at_ref[2], all_ref, turned_ref, force_ref)
    out_ref[...] = scatter_own(force_ref, sum_ref, rows_ref, lanes_ref, lhs_ref)


def shift_rows(x, by):
    return pltpu.roll(x, by % x.shape[1], 1)


def x_extended_1(fm_ref, m1_ref, ups_ref, downs_ref, pick):
    lines = sorted(pick)
    row = iota((len(lines), 16, 256), 1)

    def lift(plane):
        return jnp.stack([jnp.broadcast_to(plane[j : j + 1], (16, 256)) for j in lines])

    def take(x):
        return jnp.stack([x[j] for j in lines])

    def extend(x, low, add, high):
        if add is not None:
            x = x + jnp.where(row == 0, lift(add), 0.0) + jnp.where(row == 8, lift(high), 0.0)
            x = jnp.where(row < 9, x, 0.0)
        else:
            x = jnp.where(row < 8, x, 0.0)
        return jnp.where(row == 0, lift(low), shift_rows(x, 1))

    out = [
        extend(
            take(fm_ref[n]),
            get_plane(ups_ref, n, 9),
            get_plane(ups_ref, 4 + n, 9),
            get_plane(downs_ref, n, 4),
        )
        for n in range(4)
    ]
    return out, extend(take(m1_ref[...]), get_plane(ups_ref, 8, 9), None, None)


def y_send_1_kernel(fm_ref, m1_ref, ups_ref, downs_ref, task_ref, up_ref, down_ref):
    fields, m1 = x_extended_1(fm_ref, m1_ref, ups_ref, downs_ref, (0, 11, 12))
    send_planes([f[1] for f in fields] + [f[2] for f in fields] + [m1[1]], up_ref)
    send_planes([f[0] for f in fields], down_ref)


def stress_of(disp, modulus):
    grads = []
    for u in disp:
        s, d = u[1:] + u[:-1], u[1:] - u[:-1]
        sn = next_x(s)
        ss, xd = sn + s, sn - s
        yd = next_x(d) + d
        grads.append((xd + next_z(xd), yd + next_z(yd), next_z(ss) - ss))
    m = 0.25 * modulus
    exx, eyy, ezz = grads[0][0], grads[1][1], grads[2][2]
    trace = exx + eyy + ezz
    return (
        m * (2.0 * exx + trace),
        m * (2.0 * eyy + trace),
        m * (2.0 * ezz + trace),
        m * (grads[1][0] + grads[0][1]),
        m * (grads[2][1] + grads[1][2]),
        m * (grads[0][2] + grads[2][0]),
    )


def force_of(stress):
    xx, yy, zz, xy, yz, zx = stress
    out = []
    for a, b, c in ((xx, xy, zx), (xy, yy, yz), (zx, yz, zz)):
        az, bz, cz = a + prev_z(a), b + prev_z(b), prev_z(c) - c
        ac = (prev_x(az) - az) + (prev_x(cz) + cz)
        by = prev_x(bz) + bz
        out.append(-0.25 * ((ac[:-1] + ac[1:]) + (by[:-1] - by[1:])))
    return out


def gather_rows(disp, lanes_ref, rows_ref):
    hot = rows_ref[...]
    values = []
    for c in range(3):
        picked = [
            lax.dot_general(part, hot, (((0,), (0,)), ((), ())), preferred_element_type=F32)
            for part in split2(disp[c])
        ]
        picked = picked[0] + picked[1]
        values.append(jnp.sum(picked * lanes_ref[...], axis=0, keepdims=True))
    return values


def second_step_kernel(
    at_ref, fm_ref, c0_ref, m1_ref, xu_ref, xd_ref, yu_ref, yd_ref, c1_ref, all_ref, rows_ref,
    out_ref, state_ref, square_ref, lanes_ref,
):
    fields, m1 = x_extended_1(fm_ref, m1_ref, xu_ref, xd_ref, range(13))
    zero = jnp.zeros((1, 16, 256), F32)
    for n in range(4):
        low, add = get_plane(yu_ref, n, 9), get_plane(yu_ref, 4 + n, 9)
        own = fields[n]
        fields[n] = jnp.concatenate(
            [low[None], (own[0] + add)[None], own[1:12], (own[12] + get_plane(yd_ref, n, 4))[None]],
            axis=0,
        )
    m1 = jnp.concatenate([get_plane(yu_ref, 8, 9)[None], m1[:12]], axis=0)
    mass = fields[3]
    inv = jnp.where(mass > 0.0, DT / jnp.where(mass > 0.0, mass, 1.0), 0.0)
    disp1 = [DT * (inv * fields[c]) for c in range(3)]
    force = force_of([jnp.concatenate([x, zero], axis=0) for x in stress_of(disp1, m1)])
    inv = inv[1:]
    row = iota((13, 16, 256), 1)
    good = (row > 0) & (row < 10)
    disp2s, vel2s = [], []
    for c in range(3):
        c1 = jnp.concatenate([fill16(c1_ref[c]), jnp.zeros((1, 16, 128), F32)], axis=0)
        c1 = shift_rows(both(c1, jnp.zeros((13, 16, 128), F32)), 1)
        total = fields[c][1:]
        accel = inv * (total - shift_rows(c0_ref[c], 1))
        vel2 = inv * total + inv * force[c] + (accel + inv * c1)
        disp2 = disp1[c][1:] + DT * vel2
        back = [shift_rows(jnp.where(good, x, 0.0), -1) for x in (disp2, vel2, accel)]
        disp2s.append(back[0])
        vel2s.append(back[1])
        state_ref[c] = back[0]
        state_ref[3 + c] = back[1]
        state_ref[6 + c] = back[2]
    state_ref[9] = shift_rows(jnp.where(good, inv, 0.0), -1)
    me = at_ref[2]
    for s in range(16):
        lanes_ref[:, 128 * s : 128 * s + 128] = hot_rows_lanes(all_ref[me, NODES + s : NODES + s + 1, :])[1]
    for first, disp in (
        (0, [shift_rows(d[1:13], -1)[:, :8, :128] for d in disp1]),
        (LATE, [d[0:12, :8, :128] for d in disp2s]),
    ):
        values = gather_rows([d.reshape(96, 128) for d in disp], lanes_ref, rows_ref)
        for c in range(3):
            block = jnp.concatenate(
                [values[c][:, 128 * s : 128 * s + 128] for s in range(16)], axis=0
            ) + all_ref[me, 16 * c : 16 * c + 16, :]
            for dest in range(8):
                out_ref[dest, first + 16 * c : first + 16 * c + 16, :] = block
    rows = planes_to_rows(pack([x[:, :, :128] for x in disp2s + vel2s], 5), square_ref)
    for dest in range(8):
        out_ref[dest, PLANES_2:ROWS_2, :] = rows


UP_LIST = (
    [(n, 0) for n in range(3)] + [(n, 1) for n in range(3)] + [(n, 1) for n in (3, 4, 5, 9)]
    + [(10, 0), (10, 1), (11, 1)]
)
DOWN_LIST = (
    [(n, p) for p in (0, 1, 2) for n in range(3)]
    + [(n, p) for p in (0, 1) for n in (3, 4, 5)]
    + [(n, 0) for n in (6, 7, 8)]
    + [(9, 0), (9, 1), (10, 0), (10, 1), (11, 0)]
)
UPS, DOWNS = len(UP_LIST), len(DOWN_LIST)


def plane_of(ref, listed, n, p):
    return get_plane(ref, listed.index((n, p)), len(listed)) if (n, p) in listed else None


def late_contact_kernel(
    at_ref, list_ref, task_ref, first_ref, all_ref, state_ref, field_ref, rows_ref, lanes_ref,
    own_ref, up_ref, down_ref,
    turned_ref, force_ref, sum_ref, lhs_ref, square_ref, *rims,
):
    me = at_ref[2]
    zplanes = neighbour_planes(all_ref, PLANES_2, 5, me, square_ref, 13)
    mplanes = neighbour_planes(first_ref, PLANES, 4, me, square_ref, 12)
    top = (iota((13, 16, 128), 2) == 0) & (me == 7)
    zero = jnp.zeros((1, 16, 256), F32)

    def with_rim(own, n):
        return both(own[:, :, :128], jnp.where(top, own[:, :, 128:], unpack(zplanes, n, 5)))

    inv = state_ref[9]
    own_ref[9] = inv
    for c in range(3):
        own_ref[c] = with_rim(state_ref[c], c)
        own_ref[3 + c] = with_rim(state_ref[3 + c], 3 + c) + state_ref[6 + c]
        own_ref[6 + c] = state_ref[6 + c]
    for n, step in ((10, 2), (11, 3)):
        m = both(fill16(field_ref[3 + step]), unpack(mplanes, 3 + step, 4))
        own_ref[n] = jnp.concatenate([m, zero], axis=0)
    for step, first_row, n in ((2, 0, 3), (3, LATE, 6)):
        force_ref[...] = jnp.zeros_like(force_ref)
        pair_loop(list_ref, step, first_row, me, all_ref, turned_ref, force_ref)
        own = scatter_own(force_ref, sum_ref, rows_ref, lanes_ref, lhs_ref)
        rim = contact_rim(list_ref, task_ref, step, first_row, me, all_ref, first_ref, rims, square_ref)
        for c in range(3):
            full = both(fill16(own[c]), unpack(rim, c))
            own_ref[n + c, 0:12] = own_ref[n + c, 0:12] + own_ref[9, 0:12] * full
    send_planes([row_plane(own_ref[n], 6 + p) for n, p in UP_LIST], up_ref)
    send_planes([row_plane(own_ref[n], p) for n, p in DOWN_LIST], down_ref)


def x_extended_2(own_ref, ups_ref, downs_ref, at_last, lines):
    row = iota((len(lines), 16, 256), 1)
    keep = (row < 8) | ((row == 8) & at_last)

    def lift(plane):
        return jnp.stack([jnp.broadcast_to(plane[j : j + 1], (16, 256)) for j in lines])

    out = []
    for n in range(12):
        x = jnp.stack([own_ref[n, j] for j in lines])
        x = shift_rows(jnp.where(keep, x, 0.0), 2)
        for ref, listed, first, count in ((ups_ref, UP_LIST, 0, 2), (downs_ref, DOWN_LIST, 10, 3)):
            for p in range(count):
                got = plane_of(ref, listed, n, p)
                if got is not None:
                    add = lift(got)
                    if first + p == 10:
                        x = jnp.where((row == 10) & jnp.logical_not(at_last), add, x)
                    else:
                        x = jnp.where(row == first + p, add, x)
        out.append(x)
    return out


def y_send_2_kernel(at_ref, own_ref, ups_ref, downs_ref, up_ref, down_ref):
    fields = x_extended_2(own_ref, ups_ref, downs_ref, at_ref[0] == 7, (0, 1, 2, 10, 11))
    send_planes([fields[n][3 + p] for n, p in UP_LIST], up_ref)
    send_planes([fields[n][p] for n, p in DOWN_LIST], down_ref)


def last_kernel(at_ref, own_ref, xu_ref, xd_ref, yu_ref, yd_ref, vel_ref, stress_ref):
    fields = x_extended_2(own_ref, xu_ref, xd_ref, at_ref[0] == 7, range(13))
    y_last = at_ref[1] == 3
    none = jnp.zeros((16, 256), F32)
    wide = []
    for n in range(12):
        planes = [plane_of(yu_ref, UP_LIST, n, p) for p in (0, 1)]
        planes += [fields[n][j] for j in range(12)]
        after = [plane_of(yd_ref, DOWN_LIST, n, p) for p in (0, 1, 2)]
        after = [none if p is None else p for p in after]
        after[0] = jnp.where(y_last, fields[n][12], after[0])
        planes = [none if p is None else p for p in planes] + after
        wide.append(jnp.stack(planes))
    disp2, vh3, g3, inv, m2, m3 = wide[0:3], wide[3:6], wide[6:9], wide[9], wide[10], wide[11]
    force = force_of(stress_of(disp2, m2[:16]))
    vel3 = [vh3[c][1:16] + inv[1:16] * force[c] for c in range(3)]
    disp3 = [disp2[c][1:16] + DT * vel3[c] for c in range(3)]
    force = force_of(stress_of(disp3, m3[1:15]))
    vel4 = [vel3[c][1:14] + (inv[2:15] * force[c] + g3[c][2:15]) for c in range(3)]
    disp4 = [disp3[c][1:14] + DT * vel4[c] for c in range(3)]
    stress = stress_of(disp4, m3[2:14])
    for n in range(6):
        stress_ref[n] = shift_rows(stress[n][:, :, :128], -2)[:, :8, :]
    for c in range(3):
        s = vel4[c][1:] + vel4[c][:-1]
        s = s + next_x(s)
        s = s + next_z(s)
        vel_ref[c] = shift_rows(0.125 * s[:, :, :128], -2)[:, :8, :]


def call(kernel, outs, specs, scratch=(), held=()):
    def run(*args):
        spaces = [pltpu.VMEM if spec is HELD else pltpu.HBM if spec is FAR else None for spec in specs]
        args = [
            a if space is None else pltpu.with_memory_space_constraint(a, space)
            for a, space in zip(args, spaces)
        ]
        return pl.pallas_call(
            kernel,
            out_shape=[
                pltpu.VMEM(s, d) if n in held else jax.ShapeDtypeStruct(s, d)
                for n, (s, d) in enumerate(outs)
            ],
            in_specs=specs,
            out_specs=[VMEM] * len(outs),
            scratch_shapes=list(scratch),
            compiler_params=PARAMS,
        )(*args)

    return run


def share(blocks):
    return lax.all_to_all(blocks, "gz", split_axis=0, concat_axis=0, tiled=True)


def neighbours(up, down, axis):
    count = lax.axis_size(axis)
    ahead = [(i, i + 1) for i in range(count - 1)]
    return lax.ppermute(up, axis, ahead), lax.ppermute(down, axis, [(j, i) for i, j in ahead])


TURNED = pltpu.VMEM((17, 4, 3, 8, 128), F32)
SUMS = pltpu.VMEM((3, 16, 128), F32)
RIM = [
    pltpu.VMEM((3, 384, 128), BF16),
    pltpu.VMEM((3, 96, 128), BF16),
    pltpu.VMEM((3, 32, 128), BF16),
    pltpu.VMEM((16, 128), F32),
]
LHS = pltpu.VMEM((576, 2048), BF16)
SQUARE = pltpu.VMEM((128, 128), F32)


def per_device(stiffness, density, load, alive, surf_coords, surf_nodes, routes, pairs):
    at = jnp.stack([lax.axis_index(a) for a in ("gx", "gy", "gz")]).astype(jnp.int32)
    stiffness, density = jnp.swapaxes(stiffness, 0, 1), jnp.swapaxes(density, 0, 1)
    load, alive = jnp.swapaxes(load, 1, 2), jnp.swapaxes(alive, 1, 2)
    coords = jnp.swapaxes(surf_coords, 0, 1)
    pairs = jnp.swapaxes(pairs[:, 0], 1, 2)
    params = (coords, routes, pairs, surf_nodes, stiffness, density, load, alive)
    payload, fields = call(
        prep_kernel,
        [((8, ROWS_1, 128), F32), ((7, 12, 8, 128), F32)],
        [SMEM] + [FAR] * 8,
        [SQUARE] + [pltpu.VMEM(p.shape, p.dtype) for p in params] + [pltpu.SemaphoreType.DMA((8,))],
        (1,),
    )(at, *params)
    everyone = share(payload)
    plan_out = [((12, 512), jnp.int32), ((4, 4, 8, 128), F32)]
    lists, tasks, *hot = call(
        first_plan_kernel,
        plan_out + [((96, 2048), BF16), ((2048, 128), BF16)],
        [SMEM, HELD],
        (),
        (1, 2, 3),
    )(at, everyone)
    fm, c0, m1, up, down = call(
        first_contact_kernel,
        [((4, 13, 16, 256), F32), ((3, 13, 16, 256), F32), ((13, 16, 256), F32), ((10, 16, 128), F32),
         ((5, 16, 128), F32)],
        [SMEM, SMEM] + [HELD] * 5,
        [TURNED, TURNED, SUMS, LHS, SQUARE] + RIM,
        (0, 1, 2),
    )(at, lists, tasks, everyone, fields, *hot)
    xu, xd = neighbours(up, down, "gx")
    late_lists, late_tasks = call(
        functools.partial(plan_kernel, steps=(2, 3)), plan_out, [SMEM, HELD, HELD], (), (1,)
    )(at, everyone, m1)
    up, down = call(y_send_1_kernel, [((10, 16, 128), F32), ((5, 16, 128), F32)], [HELD] * 5)(
        fm, m1, xu, xd, late_tasks
    )
    yu, yd = neighbours(up, down, "gy")
    (c1,) = call(
        step_contact_kernel,
        [((3, 12, 8, 128), F32)],
        [SMEM, SMEM] + [HELD] * 3,
        [TURNED, TURNED, SUMS, LHS],
        (0,),
    )(at, lists, everyone, *hot)
    payload, state = call(
        second_step_kernel,
        [((8, ROWS_2, 128), F32), ((10, 13, 16, 256), F32)],
        [SMEM] + [HELD] * 10,
        [SQUARE, pltpu.VMEM((128, 2048), F32)],
        (1,),
    )(at, fm, c0, m1, xu, xd, yu, yd, c1, everyone, hot[0])
    late = share(payload)
    own, up, down = call(
        late_contact_kernel,
        [((12, 13, 16, 256), F32), ((UPS + 1, 16, 128), F32), ((DOWNS + 2, 16, 128), F32)],
        [SMEM, SMEM] + [HELD] * 7,
        [TURNED, TURNED, SUMS, LHS, SQUARE] + RIM,
        (0,),
    )(at, late_lists, late_tasks, everyone, late, state, fields, *hot)
    xu, xd = neighbours(up, down, "gx")
    up, down = call(
        y_send_2_kernel,
        [((UPS + 1, 16, 128), F32), ((DOWNS + 2, 16, 128), F32)],
        [SMEM] + [HELD] * 3,
    )(at, own, xu, xd)
    yu, yd = neighbours(up, down, "gy")
    vel, stress = call(
        last_kernel,
        [((3, 12, 8, 128), F32), ((6, 12, 8, 128), F32)],
        [SMEM] + [HELD] * 5,
    )(at, own, xu, xd, yu, yd)
    return jnp.swapaxes(vel, 1, 2), jnp.swapaxes(stress, 1, 2)


def solution(mesh):
    return jax.shard_map(
        per_device,
        mesh=mesh,
        in_specs=(
            P("gx", "gy", "gz"),
            P("gx", "gy", "gz"),
            P(None, "gx", "gy", "gz"),
            P(None, "gx", "gy", "gz"),
            P(("gx", "gy", "gz"), None, None),
            P(("gx", "gy", "gz"), None),
            P(None, ("gx", "gy", "gz")),
            P(None, ("gx", "gy", "gz"), None, None),
        ),
        out_specs=(P(None, "gx", "gy", "gz"), P(None, "gx", "gy", "gz")),
        check_vma=False,
    )
```

```python
import functools
import math
import jax
import jax.numpy as jnp
from jax import lax
from jax.experimental import pallas as pl
from jax.experimental.pallas import tpu as pltpu
from jax.sharding import PartitionSpec as P

F32 = jnp.float32
BF16 = jnp.bfloat16
SCALE = math.sqrt(math.log2(math.e) / 0.08)
DT = 0.2
PARAMS = pltpu.CompilerParams(vmem_limit_bytes=20 * 2**20)
VMEM = pl.BlockSpec(memory_space=pltpu.VMEM)
SMEM = pl.BlockSpec(memory_space=pltpu.SMEM)
HELD = pl.BlockSpec(memory_space=pltpu.VMEM)
FAR = pl.BlockSpec(memory_space=pltpu.HBM)
KEYS, PAIRS, NODES, PLANES = 48, 52, 56, 72
ROWS_1 = 104
LATE, PLANES_2 = 48, 96
ROWS_2 = 128
PLANE_ROWS = 32


def split2(x):
    hi = x.astype(BF16)
    return hi, (x - hi.astype(F32)).astype(BF16)


def iota(shape, dim):
    return lax.broadcasted_iota(jnp.int32, shape, dim)


def rim_lanes(shape, above=3):
    lane = iota(shape, len(shape) - 1)
    return (lane >= 126) | (lane < above)


def roll_last(x, shift):
    shift = shift % x.shape[-1]
    return pltpu.roll(x, shift, x.ndim - 1) if shift else x


def pack(tiles, stride=8):
    total = None
    for f, tile in enumerate(tiles):
        part = roll_last(jnp.where(rim_lanes(tile.shape, min(stride - 2, 3)), tile, 0.0), stride * f)
        total = part if total is None else total + part
    return total


def unpack(packed, f, stride=8):
    return jnp.where(
        rim_lanes(packed.shape, min(stride - 2, 3)), roll_last(packed, -stride * f), 0.0
    )


def both(main, rim):
    return jnp.concatenate([main, rim], axis=-1)


def fill16(x):
    pad = 16 - x.shape[-2]
    if not pad:
        return x
    return jnp.concatenate([x, jnp.zeros(x.shape[:-2] + (pad, x.shape[-1]), x.dtype)], axis=-2)


def next_x(x):
    return pltpu.roll(x, x.shape[1] - 1, 1)


def prev_x(x):
    return pltpu.roll(x, 1, 1)


def next_z(x):
    return roll_last(x, -1)


def prev_z(x):
    return roll_last(x, 1)


def planes_to_rows(packed, square_ref):
    square_ref[...] = jnp.zeros_like(square_ref)
    for j in range(packed.shape[0]):
        square_ref[9 * j : 9 * j + 9, :] = packed[j, 0:9, :]
    return jnp.transpose(roll_last(square_ref[...], 2))[0:PLANE_ROWS]


def rows_to_planes(rows, square_ref, planes):
    full = jnp.concatenate([rows, jnp.zeros((128 - PLANE_ROWS, 128), F32)], axis=0)
    square_ref[...] = roll_last(jnp.transpose(full), -2)
    return jnp.stack([fill16(square_ref[9 * j : 9 * j + 9, :]) for j in range(planes)])


def neighbour_planes(all_ref, first_row, stride, me, square_ref, planes):
    low = all_ref[jnp.maximum(me - 1, 0), first_row : first_row + PLANE_ROWS, :]
    up = all_ref[jnp.minimum(me + 1, 7), first_row : first_row + PLANE_ROWS, :]
    kind = iota((PLANE_ROWS, 128), 0) % stride
    low = jnp.where((kind < 2) & (me > 0), low, 0.0)
    up = jnp.where((kind >= 2) & (me < 7), up, 0.0)
    return rows_to_planes(low + up, square_ref, planes)


def spread(x, first):
    to = (iota((x.shape[1], 128), 1) == iota((x.shape[1], 128), 0) + first).astype(BF16)
    return jnp.dot(x.astype(BF16), to, preferred_element_type=F32)


def prep_kernel(at_ref, *refs):
    far, (out_ref, field_ref, square_ref) = refs[:8], refs[8:11]
    near, sems = refs[11:19], refs[19]
    copies = [pltpu.make_async_copy(a, b, sems.at[n]) for n, (a, b) in enumerate(zip(far, near))]
    for copy in copies:
        copy.start()
    for copy in copies:
        copy.wait()
    coords_ref, routes_ref, pairs_ref, nodes_ref, stiff_ref, dens_ref, load_ref, alive_ref = near
    me = at_ref[2]
    for c in range(3):
        field_ref[c] = load_ref[c]
    field_ref[3] = dens_ref[...]
    for step in (1, 2, 3):
        field_ref[3 + step] = stiff_ref[...] * alive_ref[step].astype(F32)
    rows = planes_to_rows(pack([fill16(field_ref[n]) for n in range(7)], 4), square_ref)
    nodes = nodes_ref[...].astype(F32)
    routes = routes_ref[...].astype(F32)
    rank = jnp.zeros((4, 16), F32)
    later = iota((4, 16), 1)
    for s in range(15):
        same = jnp.broadcast_to(routes[:, s : s + 1], (4, 16)) == routes
        rank = rank + jnp.where(same & (later > s), 1.0, 0.0)
    keys = spread(routes * 32.0 + rank + 4.0 * me.astype(F32), 16 * me)
    lists = spread(pairs_ref[:, 0, :].astype(F32), 0) + spread(pairs_ref[:, 1, :].astype(F32), 64)
    for dest in range(8):
        for c in range(3):
            out_ref[dest, 16 * c : 16 * c + 16, :] = coords_ref[c]
        out_ref[dest, KEYS : KEYS + 4, :] = keys
        out_ref[dest, PAIRS : PAIRS + 4, :] = lists
        out_ref[dest, NODES : NODES + 16, :] = nodes
        out_ref[dest, PLANES:ROWS_1, :] = rows


def plan_kernel(at_ref, all_ref, *refs, steps):
    list_ref, task_ref = refs[-2:]
    me = at_ref[2]
    lane = iota((1, 128), 1)
    block_of = iota((128, 128), 0).astype(F32)
    eye = iota((128, 128), 0) == iota((128, 128), 1)
    upper = (iota((128, 128), 0) < iota((128, 128), 1)).astype(BF16)
    place = iota((128, 128), 0).astype(F32)
    row8 = iota((8, 128), 0)
    src_of = iota((128, 1), 0) // 16

    def nodes_at(src, wants, real):
        ids = all_ref[src, NODES : NODES + 16, :]
        k = ids - 128.0 * jnp.floor(ids * (1.0 / 128.0))
        hit = k == wants[0]
        for want in wants[1:]:
            hit = hit | (k == want)
        count = jnp.sum(jnp.where(hit, 1.0, 0.0), axis=1, keepdims=True)
        return jnp.where(src_of == real, jnp.concatenate([count] * 8, axis=0), 0.0)

    low = nodes_at(jnp.maximum(me - 1, 0), (127.0,), me - 1)
    up = jnp.minimum(me + 1, 7)
    up0, up01 = nodes_at(up, (0.0,), me + 1), nodes_at(up, (0.0, 1.0), me + 1)
    rims = {0: low + up0, 2: low + up01, 3: up0}
    mine_first = (16 * me).astype(F32)

    def prefix(x):
        return jnp.dot(jnp.broadcast_to(x, (8, 128)).astype(BF16), upper, preferred_element_type=F32)[0:1]

    for step in steps:
        keys = all_ref[0, KEYS + step : KEYS + 1 + step, :]
        for src in range(1, 8):
            keys = keys + all_ref[src, KEYS + step : KEYS + 1 + step, :]
        key_col = jnp.sum(jnp.where(eye, keys, 0.0), axis=1, keepdims=True)
        base = jnp.zeros((1, 1), F32)
        tasks = jnp.zeros((1, 1), F32)
        spots, codes = [], []
        for row in range(4):
            even = all_ref[2 * row, PAIRS + step : PAIRS + 1 + step, :]
            odd = all_ref[2 * row + 1, PAIRS + step : PAIRS + 1 + step, :]
            left = lane < 64
            first = jnp.where(left, even, pltpu.roll(odd, 64, 1))
            second = jnp.where(left, pltpu.roll(even, 64, 1), odd)
            box = jnp.where(left, 64.0 * row, 64.0 * row + 32.0)
            hit_first = key_col == first + box
            hit_second = key_col == second + box
            p_block = jnp.sum(jnp.where(hit_first, block_of + 1.0, 0.0), axis=0, keepdims=True) - 1.0
            r_block = jnp.sum(jnp.where(hit_second, block_of + 1.0, 0.0), axis=0, keepdims=True) - 1.0
            p_slot = p_block - mine_first
            live = r_block >= 0.0
            mine = live & (p_slot >= 0.0) & (p_slot < 16.0)
            sel = jnp.where(mine, 1.0, 0.0)
            spots.append(jnp.where(mine, prefix(sel) + base, -1.0))
            base = base + jnp.sum(sel, axis=1, keepdims=True)
            code = jnp.where(
                row8 == 0, jnp.broadcast_to(p_slot, (8, 128)), jnp.broadcast_to(r_block, (8, 128))
            )
            codes.append(jnp.where(jnp.broadcast_to(mine, (8, 128)), code, 0.0).astype(BF16))
            if step in rims:
                count = jnp.sum(jnp.where(hit_first, rims[step], 0.0), axis=0, keepdims=True)
                count = jnp.where(live, count, 0.0)
                start = prefix(count) + tasks
                tasks = tasks + jnp.sum(count, axis=1, keepdims=True)
                high = jnp.floor(start * (1.0 / 256.0))
                rim_block = jnp.where(p_slot < 0.0, p_slot + 16.0, p_slot)
                some = jnp.broadcast_to(count > 0.0, (8, 128))
                table = jnp.zeros((8, 128), F32)
                for n, line in enumerate((rim_block, r_block, high, start - 256.0 * high, start, count)):
                    table = jnp.where(row8 == n, jnp.broadcast_to(line, (8, 128)), table)
                task_ref[step, row] = jnp.where(some, table, 0.0)
        list_ref[4 + step : 5 + step, :] = jnp.broadcast_to(base, (1, 512)).astype(jnp.int32)
        list_ref[8 + step : 9 + step, :] = jnp.broadcast_to(tasks, (1, 512)).astype(jnp.int32)
        count = jnp.max(base)
        for part in range(4):

            def write(part=part, spots=spots, codes=codes, base=base, step=step):
                total = jnp.zeros((8, 128), F32)
                for row in range(4):
                    onehot = jnp.where(place == spots[row] - 128.0 * part, 1.0, 0.0).astype(BF16)
                    total = total + lax.dot_general(
                        codes[row], onehot, (((1,), (1,)), ((), ())), preferred_element_type=F32
                    )
                used = (lane + 128 * part).astype(F32) < base
                code = jnp.where(used, total[0:1] * 128.0 + total[1:2], 16.0 * 128.0)
                list_ref[step : step + 1, 128 * part : 128 * part + 128] = code.astype(jnp.int32)

            if part == 0:
                write()
            else:
                pl.when(count + 16.0 > 128.0 * part)(write)


UNROLL = 16


def pair_loop(list_ref, step, first_row, me, all_ref, turned_ref, force_ref, part=(0, 1)):
    for c in range(3):
        turned_ref[16, :, c] = jnp.zeros((4, 8, 128), F32)
        for s in range(16):
            wide = jnp.broadcast_to(all_ref[me, first_row + 16 * c + s : first_row + 16 * c + s + 1, :] * SCALE, (8, 128))
            for a in range(4):
                turned_ref[s, a, c] = roll_last(wide, 32 * a)

    def one(q):
        code = list_ref[step, q]
        slot = lax.shift_right_logical(code, 7)
        src = lax.shift_right_logical(code & 127, 4)
        line = first_row + (code & 15)
        xj = []
        for c in range(3):
            wide = jnp.broadcast_to(all_ref[src, pl.ds(line + 16 * c, 1), :] * SCALE, (8, 128))
            wide = pltpu.roll(wide, 0, 1, stride=1, stride_axis=0)
            xj.append([roll_last(wide, 8 * b) for b in range(4)])
        out = []
        for a in range(4):
            xi = [turned_ref[slot, a, c] for c in range(3)]
            acc = [None] * 3
            for b in range(4):
                diff = [xi[c] - xj[c][b] for c in range(3)]
                dist = diff[0] * diff[0] + diff[1] * diff[1] + diff[2] * diff[2]
                w = jnp.exp2(-dist)
                acc = [w * diff[c] if b == 0 else acc[c] + w * diff[c] for c in range(3)]
            out.append(acc)
        return slot, out

    def body(g, carry):
        done = [one(g * UNROLL + u) for u in range(UNROLL)]
        for slot, out in done:
            for a in range(4):
                for c in range(3):
                    force_ref[slot, a, c] += out[a][c]
        return carry

    groups = (list_ref[4 + step, 0] + (UNROLL - 1)) // UNROLL
    at, of = part
    lax.fori_loop(groups * at // of, groups * (at + 1) // of, body, 0)


def block_sums(force_ref, sum_ref):
    for c in range(3):
        total = force_ref[0:16, 0, c]
        for a in range(1, 4):
            total = total + roll_last(force_ref[0:16, a, c], -32 * a)
        sum_ref[c] = jnp.sum(total, axis=1) * (1.0 / SCALE)


def row_and_lane(ids):
    line = jnp.floor(ids * (1.0 / 128.0))
    lane = ids - 128.0 * line
    i = jnp.floor((line + 0.5) * (1.0 / 12.0))
    return 8.0 * line - 95.0 * i, lane


def one_hot(at, rows):
    return jnp.where(iota((rows, 128), 0).astype(F32) == at, 1.0, 0.0)


def hot_rows_lanes(ids):
    row, lane = row_and_lane(ids)
    return one_hot(row, 96).astype(BF16), one_hot(lane, 128)


def first_plan_kernel(at_ref, all_ref, list_ref, task_ref, rows_ref, lanes_ref):
    plan_kernel(at_ref, all_ref, list_ref, task_ref, steps=(0, 1))
    for s in range(16):
        at = slice(128 * s, 128 * s + 128)
        rows_ref[:, at], lanes = hot_rows_lanes(all_ref[at_ref[2], NODES + s : NODES + s + 1, :])
        lanes_ref[at, :] = jnp.transpose(lanes).astype(BF16)


def scatter_own(force_ref, sum_ref, rows_ref, lanes_ref, lhs_ref):
    block_sums(force_ref, sum_ref)
    for s in range(16):
        at = slice(128 * s, 128 * s + 128)
        hot = rows_ref[:, at]
        for c in range(3):
            hi, lo = split2(sum_ref[c, s : s + 1, :])
            lhs_ref[96 * c : 96 * c + 96, at] = hot * hi
            lhs_ref[288 + 96 * c : 384 + 96 * c, at] = hot * lo
    out = jnp.dot(lhs_ref[...], lanes_ref[...], preferred_element_type=F32)
    return (out[:288] + out[288:]).reshape(3, 12, 8, 128)


def split3(x):
    hi, rest = x.astype(BF16), x
    rest = rest - hi.astype(F32)
    mid = rest.astype(BF16)
    return jnp.concatenate([hi, mid, (rest - mid.astype(F32)).astype(BF16)], axis=0)


def contact_rim(list_ref, task_ref, step, first_row, me, pos_ref, ids_ref, rim, square_ref):
    all_ref, near_ref, info_ref, sum_ref = rim
    low, up = jnp.maximum(me - 1, 0), jnp.minimum(me + 1, 7)
    for c in range(3):
        at = first_row + 16 * c
        block = jnp.concatenate([pos_ref[src, at : at + 16, :] for src in range(8)], axis=0)
        all_ref[c] = split3(block * SCALE)
        block = jnp.concatenate([pos_ref[low, at : at + 16, :], pos_ref[up, at : at + 16, :]], axis=0)
        near_ref[c] = split3(block * SCALE)
    ids = jnp.concatenate(
        [ids_ref[low, NODES : NODES + 16, :], ids_ref[up, NODES : NODES + 16, :]], axis=0
    )
    line, lane = row_and_lane(ids)
    below = iota((32, 128), 0) < 16
    ghost = (below & (lane == 127.0)) | (jnp.logical_not(below) & (lane == 0.0))
    if step == 2:
        ghost = ghost | (jnp.logical_not(below) & (lane == 1.0))
    upper = (iota((128, 128), 0) < iota((128, 128), 1)).astype(BF16)
    rank = jnp.dot(jnp.where(ghost, 1.0, 0.0).astype(BF16), upper, preferred_element_type=F32)
    info_ref[0] = jnp.where(ghost, rank, 255.0).astype(BF16)
    info_ref[1] = line.astype(BF16)
    info_ref[2] = jnp.where(below, 0.0, lane + 1.0).astype(BF16)
    sum_ref[...] = jnp.zeros_like(sum_ref)
    tasks = list_ref[8 + step, 0]

    def pick(table, hot):
        return lax.dot_general(table, hot, (((0,), (0,)), ((), ())), preferred_element_type=F32)

    def body(part, carry):
        first = part * 128
        number = (iota((128, 128), 0) + first).astype(F32)
        found = jnp.zeros((8, 128), F32)
        for row in range(4):
            entry = task_ref[step, row]
            start, count = entry[4:5], entry[5:6]
            hot = jnp.where((number >= start) & (number < start + count), 1.0, 0.0).astype(BF16)
            found = found + lax.dot_general(
                entry.astype(BF16), hot, (((1,), (1,)), ((), ())), preferred_element_type=F32
            )
        here = (iota((1, 128), 1) + first).astype(F32)
        nth = here - (256.0 * found[2:3] + found[3:4])
        live = here < tasks.astype(F32)
        hot_p = jnp.where(iota((32, 128), 0).astype(F32) == found[0:1], 1.0, 0.0).astype(BF16)
        hot_r = jnp.where(iota((128, 128), 0).astype(F32) == found[1:2], 1.0, 0.0).astype(BF16)
        match = pick(info_ref[0], hot_p) == nth
        line = jnp.sum(jnp.where(match, pick(info_ref[1], hot_p), 0.0), axis=0, keepdims=True)
        plane = jnp.sum(jnp.where(match, pick(info_ref[2], hot_p), 0.0), axis=0, keepdims=True)
        hot_p3 = jnp.concatenate([hot_p] * 3, axis=0)
        hot_r3 = jnp.concatenate([hot_r] * 3, axis=0)
        xi, xj = [], []
        for c in range(3):
            xi.append(jnp.sum(jnp.where(match, pick(near_ref[c], hot_p3), 0.0), axis=0, keepdims=True))
            xj.append(pick(all_ref[c], hot_r3))
        diff = [xi[c] - xj[c] for c in range(3)]
        dist = diff[0] * diff[0] + diff[1] * diff[1] + diff[2] * diff[2]
        w = jnp.exp2(-dist)
        lines = []
        for want in range(3):
            for c in range(3):
                f = jnp.sum(w * diff[c], axis=0, keepdims=True) * (1.0 / SCALE)
                lines.append(jnp.where(live & (plane == want), f, 0.0))
        lines.append(jnp.zeros((7, 128), F32))
        hi, lo = split2(jnp.concatenate(lines, axis=0))
        hot = one_hot(line, 128).astype(BF16)
        got = lax.dot_general(
            jnp.concatenate([hi, lo], axis=0), hot, (((1,), (1,)), ((), ())), preferred_element_type=F32
        )
        sum_ref[...] += got[0:16] + got[16:32]
        return carry

    lax.fori_loop(0, (tasks + 127) // 128, body, 0)
    square_ref[...] = jnp.zeros_like(square_ref)
    for want, k in enumerate((127, 0, 1)):
        for c in range(3):
            at = (k + 8 * c) % 128
            square_ref[at : at + 1, :] = sum_ref[3 * want + c : 3 * want + c + 1, :]
    return fill16(jnp.transpose(square_ref[...])[0:96].reshape(12, 8, 128))


def node_sum(elements):
    e = 0.125 * elements
    e = e + prev_z(e)
    e = e + prev_x(e)
    zero = jnp.zeros((1,) + e.shape[1:], F32)
    return jnp.concatenate([e, zero], axis=0) + jnp.concatenate([zero, e], axis=0)


def send_planes(planes, out_ref):
    count = len(planes)
    for n, plane in enumerate(planes):
        out_ref[n] = plane[:, :128]
    for g in range(0, count, 16):
        out_ref[count + g // 16] = pack([p[:, 128:] for p in planes[g : g + 16]])


def get_plane(ref, n, count):
    return both(ref[n], unpack(ref[count + n // 16], n % 16))


class Halves:
    def __init__(self, main, rim):
        self.refs = (main, rim)

    def __getitem__(self, at):
        return both(*[ref[at] for ref in self.refs])

    def __setitem__(self, at, value):
        self.refs[0][at] = value[..., :128]
        self.refs[1][at] = value[..., 128:]

    def row(self, n, i):
        lines = pl.ds(208 * n + i, 13, stride=16)
        flat = [ref.reshape(ref.shape[0] * 208, 128) for ref in self.refs]
        return fill16(both(*[ref[lines, :] for ref in flat]))

    def set_row(self, n, i, plane):
        lines = pl.ds(208 * n + i, 13, stride=16)
        for t, ref in enumerate(self.refs):
            ref.reshape(ref.shape[0] * 208, 128)[lines, :] = plane[:13, 128 * t : 128 * t + 128]


def first_contact_kernel(
    at_ref, list_ref, task_ref, all_ref, field_ref, rows_ref, lanes_ref,
    fm_main_ref, fm_rim_ref, c0_ref, m1_ref, up_ref, down_ref,
    turned_ref, force_ref, sum_ref, lhs_ref, square_ref, *rim,
):
    me = at_ref[2]
    fm = Halves(fm_main_ref, fm_rim_ref)
    planes = neighbour_planes(all_ref, PLANES, 4, me, square_ref, 12)
    sums = [node_sum(both(fill16(field_ref[n]), unpack(planes, n, 4))) for n in range(4)]
    m1 = both(fill16(field_ref[4]), unpack(planes, 4, 4))
    zero = jnp.zeros((1, 16, 256), F32)
    m1 = jnp.concatenate([m1, zero], axis=0)
    m1_ref[...] = m1
    fm[3] = sums[3]
    for c in range(3):
        fm[c] = sums[c]
    force_ref[...] = jnp.zeros_like(force_ref)
    pair_loop(list_ref, 0, 0, me, all_ref, turned_ref, force_ref)
    own = scatter_own(force_ref, sum_ref, rows_ref, lanes_ref, lhs_ref)
    rim = contact_rim(list_ref, task_ref, 0, 0, me, all_ref, all_ref, rim, square_ref)
    for c in range(3):
        full = jnp.concatenate([both(fill16(own[c]), unpack(rim, c)), zero], axis=0)
        c0_ref[c] = full
        fm[c] = fm[c] + full
    ups = [fm.row(n, 7) for n in range(4)] + [fm.row(n, 8) for n in range(4)]
    send_planes(ups + [fill16(m1[:, 7, :])], up_ref)
    send_planes([fm.row(n, 0) for n in range(4)], down_ref)


def step_contact_kernel(
    at_ref, list_ref, all_ref, rows_ref, lanes_ref, out_ref, turned_ref, force_ref, sum_ref, lhs_ref
):
    force_ref[...] = jnp.zeros_like(force_ref)
    pair_loop(list_ref, 1, 0, at_ref[2], all_ref, turned_ref, force_ref)
    out_ref[...] = scatter_own(force_ref, sum_ref, rows_ref, lanes_ref, lhs_ref)


def shift_rows(x, by):
    return pltpu.roll(x, by % x.shape[1], 1)


def x_extended_1(fm, m1_ref, ups_ref, downs_ref, pick):
    lines = sorted(pick)
    row = iota((len(lines), 16, 256), 1)

    def lift(plane):
        return jnp.stack([jnp.broadcast_to(plane[j : j + 1], (16, 256)) for j in lines])

    def take(x):
        return jnp.stack([x[j] for j in lines])

    def extend(x, low, add, high):
        if add is not None:
            x = x + jnp.where(row == 0, lift(add), 0.0) + jnp.where(row == 8, lift(high), 0.0)
            x = jnp.where(row < 9, x, 0.0)
        else:
            x = jnp.where(row < 8, x, 0.0)
        return jnp.where(row == 0, lift(low), shift_rows(x, 1))

    out = [
        extend(
            take(fm[n]),
            get_plane(ups_ref, n, 9),
            get_plane(ups_ref, 4 + n, 9),
            get_plane(downs_ref, n, 4),
        )
        for n in range(4)
    ]
    return out, extend(take(m1_ref[...]), get_plane(ups_ref, 8, 9), None, None)


def y_send_1_kernel(fm_main_ref, fm_rim_ref, m1_ref, ups_ref, downs_ref, task_ref, up_ref, down_ref):
    fields, m1 = x_extended_1(Halves(fm_main_ref, fm_rim_ref), m1_ref, ups_ref, downs_ref, (0, 11, 12))
    send_planes([f[1] for f in fields] + [f[2] for f in fields] + [m1[1]], up_ref)
    send_planes([f[0] for f in fields], down_ref)


def stress_of(disp, modulus):
    grads = []
    for u in disp:
        s, d = u[1:] + u[:-1], u[1:] - u[:-1]
        sn = next_x(s)
        ss, xd = sn + s, sn - s
        yd = next_x(d) + d
        grads.append((xd + next_z(xd), yd + next_z(yd), next_z(ss) - ss))
    m = 0.25 * modulus
    exx, eyy, ezz = grads[0][0], grads[1][1], grads[2][2]
    trace = exx + eyy + ezz
    return (
        m * (2.0 * exx + trace),
        m * (2.0 * eyy + trace),
        m * (2.0 * ezz + trace),
        m * (grads[1][0] + grads[0][1]),
        m * (grads[2][1] + grads[1][2]),
        m * (grads[0][2] + grads[2][0]),
    )


def force_of(stress):
    xx, yy, zz, xy, yz, zx = stress
    out = []
    for a, b, c in ((xx, xy, zx), (xy, yy, yz), (zx, yz, zz)):
        az, bz, cz = a + prev_z(a), b + prev_z(b), prev_z(c) - c
        ac = (prev_x(az) - az) + (prev_x(cz) + cz)
        by = prev_x(bz) + bz
        out.append(-0.25 * ((ac[:-1] + ac[1:]) + (by[:-1] - by[1:])))
    return out


def gather_rows(disp, lanes_ref, rows_ref):
    hot = rows_ref[...]
    values = []
    for c in range(3):
        picked = [
            lax.dot_general(part, hot, (((0,), (0,)), ((), ())), preferred_element_type=F32)
            for part in split2(disp[c])
        ]
        picked = picked[0] + picked[1]
        values.append(jnp.sum(picked * lanes_ref[...], axis=0, keepdims=True))
    return values


def second_step_kernel(
    at_ref, fm_main_ref, fm_rim_ref, c0_ref, m1_ref, xu_ref, xd_ref, yu_ref, yd_ref, c1_ref, all_ref, rows_ref,
    out_ref, state_ref, square_ref, lanes_ref,
):
    fields, m1 = x_extended_1(Halves(fm_main_ref, fm_rim_ref), m1_ref, xu_ref, xd_ref, range(13))
    zero = jnp.zeros((1, 16, 256), F32)
    for n in range(4):
        low, add = get_plane(yu_ref, n, 9), get_plane(yu_ref, 4 + n, 9)
        own = fields[n]
        fields[n] = jnp.concatenate(
            [low[None], (own[0] + add)[None], own[1:12], (own[12] + get_plane(yd_ref, n, 4))[None]],
            axis=0,
        )
    m1 = jnp.concatenate([get_plane(yu_ref, 8, 9)[None], m1[:12]], axis=0)
    mass = fields[3]
    inv = jnp.where(mass > 0.0, DT / jnp.where(mass > 0.0, mass, 1.0), 0.0)
    disp1 = [DT * (inv * fields[c]) for c in range(3)]
    force = force_of([jnp.concatenate([x, zero], axis=0) for x in stress_of(disp1, m1)])
    inv = inv[1:]
    row = iota((13, 16, 256), 1)
    good = (row > 0) & (row < 10)
    disp2s, vel2s = [], []
    for c in range(3):
        c1 = jnp.concatenate([fill16(c1_ref[c]), jnp.zeros((1, 16, 128), F32)], axis=0)
        c1 = shift_rows(both(c1, jnp.zeros((13, 16, 128), F32)), 1)
        total = fields[c][1:]
        accel = inv * (total - shift_rows(c0_ref[c], 1))
        vel2 = inv * total + inv * force[c] + (accel + inv * c1)
        disp2 = disp1[c][1:] + DT * vel2
        back = [shift_rows(jnp.where(good, x, 0.0), -1) for x in (disp2, vel2, accel)]
        disp2s.append(back[0])
        vel2s.append(back[1])
        state_ref[c] = back[0]
        state_ref[3 + c] = back[1]
        state_ref[6 + c] = back[2]
    state_ref[9] = shift_rows(jnp.where(good, inv, 0.0), -1)
    me = at_ref[2]
    for s in range(16):
        lanes_ref[:, 128 * s : 128 * s + 128] = hot_rows_lanes(all_ref[me, NODES + s : NODES + s + 1, :])[1]
    for first, disp in (
        (0, [shift_rows(d[1:13], -1)[:, :8, :128] for d in disp1]),
        (LATE, [d[0:12, :8, :128] for d in disp2s]),
    ):
        values = gather_rows([d.reshape(96, 128) for d in disp], lanes_ref, rows_ref)
        for c in range(3):
            block = jnp.concatenate(
                [values[c][:, 128 * s : 128 * s + 128] for s in range(16)], axis=0
            ) + all_ref[me, 16 * c : 16 * c + 16, :]
            for dest in range(8):
                out_ref[dest, first + 16 * c : first + 16 * c + 16, :] = block
    rows = planes_to_rows(pack([x[:, :, :128] for x in disp2s + vel2s], 5), square_ref)
    for dest in range(8):
        out_ref[dest, PLANES_2:ROWS_2, :] = rows


UP_LIST = (
    [(n, 0) for n in range(3)] + [(n, 1) for n in range(3)] + [(n, 1) for n in (3, 4, 5, 9)]
    + [(10, 0), (10, 1), (11, 1)]
)
DOWN_LIST = (
    [(n, p) for p in (0, 1, 2) for n in range(3)]
    + [(n, p) for p in (0, 1) for n in (3, 4, 5)]
    + [(n, 0) for n in (6, 7, 8)]
    + [(9, 0), (9, 1), (10, 0), (10, 1), (11, 0)]
)
UPS, DOWNS = len(UP_LIST), len(DOWN_LIST)


def plane_of(ref, listed, n, p):
    return get_plane(ref, listed.index((n, p)), len(listed)) if (n, p) in listed else None


def late_contact_kernel(
    at_ref, list_ref, task_ref, first_ref, all_ref, state_ref, field_ref, rows_ref, lanes_ref,
    main_ref, rim_ref, up_ref, down_ref,
    turned_ref, force_ref, sum_ref, lhs_ref, square_ref, *rims,
):
    me = at_ref[2]
    own = Halves(main_ref, rim_ref)
    zplanes = neighbour_planes(all_ref, PLANES_2, 5, me, square_ref, 13)
    mplanes = neighbour_planes(first_ref, PLANES, 4, me, square_ref, 12)
    top = (iota((13, 16, 128), 2) == 0) & (me == 7)
    zero = jnp.zeros((1, 16, 256), F32)

    def with_rim(x, n):
        return both(x[:, :, :128], jnp.where(top, x[:, :, 128:], unpack(zplanes, n, 5)))

    inv = state_ref[9]
    own[9] = inv
    for c in range(3):
        own[c] = with_rim(state_ref[c], c)
        own[3 + c] = with_rim(state_ref[3 + c], 3 + c) + state_ref[6 + c]
        own[6 + c] = state_ref[6 + c]
    for n, step in ((10, 2), (11, 3)):
        m = both(fill16(field_ref[3 + step]), unpack(mplanes, 3 + step, 4))
        own[n] = jnp.concatenate([m, zero], axis=0)
    for step, first_row, n in ((2, 0, 3), (3, LATE, 6)):
        force_ref[...] = jnp.zeros_like(force_ref)
        pair_loop(list_ref, step, first_row, me, all_ref, turned_ref, force_ref)
        got = scatter_own(force_ref, sum_ref, rows_ref, lanes_ref, lhs_ref)
        rim = contact_rim(list_ref, task_ref, step, first_row, me, all_ref, first_ref, rims, square_ref)
        for c in range(3):
            full = both(fill16(got[c]), unpack(rim, c))
            own[n + c, 0:12] = own[n + c, 0:12] + own[9, 0:12] * full
    send_planes([own.row(n, 6 + p) for n, p in UP_LIST], up_ref)
    send_planes([own.row(n, p) for n, p in DOWN_LIST], down_ref)


def x_extended_2(own, ups_ref, downs_ref, at_last, lines):
    row = iota((len(lines), 16, 256), 1)
    keep = (row < 8) | ((row == 8) & at_last)

    def lift(plane):
        return jnp.stack([jnp.broadcast_to(plane[j : j + 1], (16, 256)) for j in lines])

    out = []
    for n in range(12):
        x = jnp.stack([own[n, j] for j in lines])
        x = shift_rows(jnp.where(keep, x, 0.0), 2)
        for ref, listed, first, count in ((ups_ref, UP_LIST, 0, 2), (downs_ref, DOWN_LIST, 10, 3)):
            for p in range(count):
                got = plane_of(ref, listed, n, p)
                if got is not None:
                    add = lift(got)
                    if first + p == 10:
                        x = jnp.where((row == 10) & jnp.logical_not(at_last), add, x)
                    else:
                        x = jnp.where(row == first + p, add, x)
        out.append(x)
    return out


def y_send_2_kernel(at_ref, main_ref, rim_ref, ups_ref, downs_ref, up_ref, down_ref):
    fields = x_extended_2(Halves(main_ref, rim_ref), ups_ref, downs_ref, at_ref[0] == 7, (0, 1, 2, 10, 11))
    send_planes([fields[n][3 + p] for n, p in UP_LIST], up_ref)
    send_planes([fields[n][p] for n, p in DOWN_LIST], down_ref)


def last_kernel(
    at_ref, main_ref, rim_ref, xu_ref, xd_ref, yu_ref, yd_ref, vel_ref, stress_ref, wide_main_ref, wide_rim_ref
):
    own, grown = Halves(main_ref, rim_ref), Halves(wide_main_ref, wide_rim_ref)
    at_last = at_ref[0] == 7
    row = iota((13, 16, 256), 1)
    for n in range(12):
        grown[n] = shift_rows(jnp.where((row < 8) | ((row == 8) & at_last), own[n], 0.0), 2)
        for ref, listed, first, count in ((xu_ref, UP_LIST, 0, 2), (xd_ref, DOWN_LIST, 10, 3)):
            for p in range(count):
                got = plane_of(ref, listed, n, p)
                if got is None:
                    continue
                if first + p == 10:
                    got = jnp.where(at_last, own.row(n, 8), got)
                grown.set_row(n, first + p, got)
    fields = [grown[n] for n in range(12)]
    y_last = at_ref[1] == 3
    none = jnp.zeros((16, 256), F32)
    wide = []
    for n in range(12):
        planes = [plane_of(yu_ref, UP_LIST, n, p) for p in (0, 1)]
        planes += [fields[n][j] for j in range(12)]
        after = [plane_of(yd_ref, DOWN_LIST, n, p) for p in (0, 1, 2)]
        after = [none if p is None else p for p in after]
        after[0] = jnp.where(y_last, fields[n][12], after[0])
        planes = [none if p is None else p for p in planes] + after
        wide.append(jnp.stack(planes))
    disp2, vh3, g3, inv, m2, m3 = wide[0:3], wide[3:6], wide[6:9], wide[9], wide[10], wide[11]
    force = force_of(stress_of(disp2, m2[:16]))
    vel3 = [vh3[c][1:16] + inv[1:16] * force[c] for c in range(3)]
    disp3 = [disp2[c][1:16] + DT * vel3[c] for c in range(3)]
    force = force_of(stress_of(disp3, m3[1:15]))
    vel4 = [vel3[c][1:14] + (inv[2:15] * force[c] + g3[c][2:15]) for c in range(3)]
    disp4 = [disp3[c][1:14] + DT * vel4[c] for c in range(3)]
    stress = stress_of(disp4, m3[2:14])
    for n in range(6):
        stress_ref[n] = shift_rows(stress[n][:, :, :128], -2)[:, :8, :]
    for c in range(3):
        s = vel4[c][1:] + vel4[c][:-1]
        s = s + next_x(s)
        s = s + next_z(s)
        vel_ref[c] = shift_rows(0.125 * s[:, :, :128], -2)[:, :8, :]


def call(kernel, outs, specs, scratch=(), held=()):
    def run(*args):
        spaces = [pltpu.VMEM if spec is HELD else pltpu.HBM if spec is FAR else None for spec in specs]
        args = [
            a if space is None else pltpu.with_memory_space_constraint(a, space)
            for a, space in zip(args, spaces)
        ]
        return pl.pallas_call(
            kernel,
            out_shape=[
                pltpu.VMEM(s, d) if n in held else jax.ShapeDtypeStruct(s, d)
                for n, (s, d) in enumerate(outs)
            ],
            in_specs=specs,
            out_specs=[VMEM] * len(outs),
            scratch_shapes=list(scratch),
            compiler_params=PARAMS,
        )(*args)

    return run


def share(blocks):
    return lax.all_to_all(blocks, "gz", split_axis=0, concat_axis=0, tiled=True)


def neighbours(up, down, axis):
    count = lax.axis_size(axis)
    ahead = [(i, i + 1) for i in range(count - 1)]
    return lax.ppermute(up, axis, ahead), lax.ppermute(down, axis, [(j, i) for i, j in ahead])


TURNED = pltpu.VMEM((17, 4, 3, 8, 128), F32)
SUMS = pltpu.VMEM((3, 16, 128), F32)
RIM = [
    pltpu.VMEM((3, 384, 128), BF16),
    pltpu.VMEM((3, 96, 128), BF16),
    pltpu.VMEM((3, 32, 128), BF16),
    pltpu.VMEM((16, 128), F32),
]
LHS = pltpu.VMEM((576, 2048), BF16)
SQUARE = pltpu.VMEM((128, 128), F32)


def per_device(stiffness, density, load, alive, surf_coords, surf_nodes, routes, pairs):
    at = jnp.stack([lax.axis_index(a) for a in ("gx", "gy", "gz")]).astype(jnp.int32)
    stiffness, density = jnp.swapaxes(stiffness, 0, 1), jnp.swapaxes(density, 0, 1)
    load, alive = jnp.swapaxes(load, 1, 2), jnp.swapaxes(alive, 1, 2)
    coords = jnp.swapaxes(surf_coords, 0, 1)
    pairs = jnp.swapaxes(pairs[:, 0], 1, 2)
    params = (coords, routes, pairs, surf_nodes, stiffness, density, load, alive)
    payload, fields = call(
        prep_kernel,
        [((8, ROWS_1, 128), F32), ((7, 12, 8, 128), F32)],
        [SMEM] + [FAR] * 8,
        [SQUARE] + [pltpu.VMEM(p.shape, p.dtype) for p in params] + [pltpu.SemaphoreType.DMA((8,))],
        (1,),
    )(at, *params)
    everyone = share(payload)
    plan_out = [((12, 512), jnp.int32), ((4, 4, 8, 128), F32)]
    lists, tasks, *hot = call(
        first_plan_kernel,
        plan_out + [((96, 2048), BF16), ((2048, 128), BF16)],
        [SMEM, HELD],
        (),
        (1, 2, 3),
    )(at, everyone)
    fm, fm_rim, c0, m1, up, down = call(
        first_contact_kernel,
        [((5, 13, 16, 128), F32)] * 2 + [((3, 13, 16, 256), F32), ((13, 16, 256), F32), ((10, 16, 128), F32),
         ((5, 16, 128), F32)],
        [SMEM, SMEM] + [HELD] * 5,
        [TURNED, TURNED, SUMS, LHS, SQUARE] + RIM,
        (0, 1, 2, 3),
    )(at, lists, tasks, everyone, fields, *hot)
    xu, xd = neighbours(up, down, "gx")
    late_lists, late_tasks = call(
        functools.partial(plan_kernel, steps=(2, 3)), plan_out, [SMEM, HELD, HELD], (), (1,)
    )(at, everyone, m1)
    up, down = call(y_send_1_kernel, [((10, 16, 128), F32), ((5, 16, 128), F32)], [HELD] * 6)(
        fm, fm_rim, m1, xu, xd, late_tasks
    )
    yu, yd = neighbours(up, down, "gy")
    (c1,) = call(
        step_contact_kernel,
        [((3, 12, 8, 128), F32)],
        [SMEM, SMEM] + [HELD] * 3,
        [TURNED, TURNED, SUMS, LHS],
        (0,),
    )(at, lists, everyone, *hot)
    payload, state = call(
        second_step_kernel,
        [((8, ROWS_2, 128), F32), ((10, 13, 16, 256), F32)],
        [SMEM] + [HELD] * 11,
        [SQUARE, pltpu.VMEM((128, 2048), F32)],
        (1,),
    )(at, fm, fm_rim, c0, m1, xu, xd, yu, yd, c1, everyone, hot[0])
    late = share(payload)
    own, own_rim, up, down = call(
        late_contact_kernel,
        [((13, 13, 16, 128), F32)] * 2 + [((UPS + 1, 16, 128), F32), ((DOWNS + 2, 16, 128), F32)],
        [SMEM, SMEM] + [HELD] * 7,
        [TURNED, TURNED, SUMS, LHS, SQUARE] + RIM,
        (0, 1),
    )(at, late_lists, late_tasks, everyone, late, state, fields, *hot)
    xu, xd = neighbours(up, down, "gx")
    up, down = call(
        y_send_2_kernel,
        [((UPS + 1, 16, 128), F32), ((DOWNS + 2, 16, 128), F32)],
        [SMEM] + [HELD] * 4,
    )(at, own, own_rim, xu, xd)
    yu, yd = neighbours(up, down, "gy")
    vel, stress = call(
        last_kernel,
        [((3, 12, 8, 128), F32), ((6, 12, 8, 128), F32)],
        [SMEM] + [HELD] * 6,
        [pltpu.VMEM((13, 13, 16, 128), F32)] * 2,
    )(at, own, own_rim, xu, xd, yu, yd)
    return jnp.swapaxes(vel, 1, 2), jnp.swapaxes(stress, 1, 2)


def solution(mesh):
    return jax.shard_map(
        per_device,
        mesh=mesh,
        in_specs=(
            P("gx", "gy", "gz"),
            P("gx", "gy", "gz"),
            P(None, "gx", "gy", "gz"),
            P(None, "gx", "gy", "gz"),
            P(("gx", "gy", "gz"), None, None),
            P(("gx", "gy", "gz"), None),
            P(None, ("gx", "gy", "gz")),
            P(None, ("gx", "gy", "gz"), None, None),
        ),
        out_specs=(P(None, "gx", "gy", "gz"), P(None, "gx", "gy", "gz")),
        check_vma=False,
    )
```

```python
import functools
import math
import jax
import jax.numpy as jnp
from jax import lax
from jax.experimental import pallas as pl
from jax.experimental.pallas import tpu as pltpu
from jax.sharding import PartitionSpec as P

F32 = jnp.float32
BF16 = jnp.bfloat16
SCALE = math.sqrt(math.log2(math.e) / 0.08)
DT = 0.2
PARAMS = pltpu.CompilerParams(vmem_limit_bytes=20 * 2**20)
VMEM = pl.BlockSpec(memory_space=pltpu.VMEM)
SMEM = pl.BlockSpec(memory_space=pltpu.SMEM)
HELD = pl.BlockSpec(memory_space=pltpu.VMEM)
FAR = pl.BlockSpec(memory_space=pltpu.HBM)
KEYS, PAIRS, NODES, PLANES = 48, 52, 56, 72
ROWS_1 = 104
LATE, PLANES_2 = 48, 96
ROWS_2 = 128
PLANE_ROWS = 32


def split2(x):
    hi = x.astype(BF16)
    return hi, (x - hi.astype(F32)).astype(BF16)


def iota(shape, dim):
    return lax.broadcasted_iota(jnp.int32, shape, dim)


def rim_lanes(shape, above=3):
    lane = iota(shape, len(shape) - 1)
    return (lane >= 126) | (lane < above)


def roll_last(x, shift):
    shift = shift % x.shape[-1]
    return pltpu.roll(x, shift, x.ndim - 1) if shift else x


def pack(tiles, stride=8):
    total = None
    for f, tile in enumerate(tiles):
        part = roll_last(jnp.where(rim_lanes(tile.shape, min(stride - 2, 3)), tile, 0.0), stride * f)
        total = part if total is None else total + part
    return total


def unpack(packed, f, stride=8):
    return jnp.where(
        rim_lanes(packed.shape, min(stride - 2, 3)), roll_last(packed, -stride * f), 0.0
    )


def both(main, rim):
    return jnp.concatenate([main, rim], axis=-1)


def fill16(x):
    pad = 16 - x.shape[-2]
    if not pad:
        return x
    return jnp.concatenate([x, jnp.zeros(x.shape[:-2] + (pad, x.shape[-1]), x.dtype)], axis=-2)


def next_x(x):
    return pltpu.roll(x, x.shape[1] - 1, 1)


def prev_x(x):
    return pltpu.roll(x, 1, 1)


def next_z(x):
    return roll_last(x, -1)


def prev_z(x):
    return roll_last(x, 1)


def planes_to_rows(packed, square_ref):
    square_ref[...] = jnp.zeros_like(square_ref)
    for j in range(packed.shape[0]):
        square_ref[9 * j : 9 * j + 9, :] = packed[j, 0:9, :]
    return jnp.transpose(roll_last(square_ref[...], 2))[0:PLANE_ROWS]


def rows_to_planes(rows, square_ref, planes):
    full = jnp.concatenate([rows, jnp.zeros((128 - PLANE_ROWS, 128), F32)], axis=0)
    square_ref[...] = roll_last(jnp.transpose(full), -2)
    return jnp.stack([fill16(square_ref[9 * j : 9 * j + 9, :]) for j in range(planes)])


def neighbour_planes(all_ref, first_row, stride, me, square_ref, planes):
    low = all_ref[jnp.maximum(me - 1, 0), first_row : first_row + PLANE_ROWS, :]
    up = all_ref[jnp.minimum(me + 1, 7), first_row : first_row + PLANE_ROWS, :]
    kind = iota((PLANE_ROWS, 128), 0) % stride
    low = jnp.where((kind < 2) & (me > 0), low, 0.0)
    up = jnp.where((kind >= 2) & (me < 7), up, 0.0)
    return rows_to_planes(low + up, square_ref, planes)


def spread(x, first):
    to = (iota((x.shape[1], 128), 1) == iota((x.shape[1], 128), 0) + first).astype(BF16)
    return jnp.dot(x.astype(BF16), to, preferred_element_type=F32)


def prep_kernel(at_ref, *refs):
    far, (out_ref, field_ref, square_ref) = refs[:8], refs[8:11]
    near, sems = refs[11:19], refs[19]
    copies = [pltpu.make_async_copy(a, b, sems.at[n]) for n, (a, b) in enumerate(zip(far, near))]
    for copy in copies:
        copy.start()
    for copy in copies:
        copy.wait()
    coords_ref, routes_ref, pairs_ref, nodes_ref, stiff_ref, dens_ref, load_ref, alive_ref = near
    me = at_ref[2]
    for c in range(3):
        field_ref[c] = load_ref[c]
    field_ref[3] = dens_ref[...]
    for step in (1, 2, 3):
        field_ref[3 + step] = stiff_ref[...] * alive_ref[step].astype(F32)
    rows = planes_to_rows(pack([fill16(field_ref[n]) for n in range(7)], 4), square_ref)
    nodes = nodes_ref[...].astype(F32)
    routes = routes_ref[...].astype(F32)
    rank = jnp.zeros((4, 16), F32)
    later = iota((4, 16), 1)
    for s in range(15):
        same = jnp.broadcast_to(routes[:, s : s + 1], (4, 16)) == routes
        rank = rank + jnp.where(same & (later > s), 1.0, 0.0)
    keys = spread(routes * 32.0 + rank + 4.0 * me.astype(F32), 16 * me)
    lists = spread(pairs_ref[:, 0, :].astype(F32), 0) + spread(pairs_ref[:, 1, :].astype(F32), 64)
    for dest in range(8):
        for c in range(3):
            out_ref[dest, 16 * c : 16 * c + 16, :] = coords_ref[c]
        out_ref[dest, KEYS : KEYS + 4, :] = keys
        out_ref[dest, PAIRS : PAIRS + 4, :] = lists
        out_ref[dest, NODES : NODES + 16, :] = nodes
        out_ref[dest, PLANES:ROWS_1, :] = rows


def plan_kernel(at_ref, all_ref, *refs, steps):
    list_ref, task_ref = refs[-2:]
    me = at_ref[2]
    lane = iota((1, 128), 1)
    block_of = iota((128, 128), 0).astype(F32)
    eye = iota((128, 128), 0) == iota((128, 128), 1)
    upper = (iota((128, 128), 0) < iota((128, 128), 1)).astype(BF16)
    place = iota((128, 128), 0).astype(F32)
    row8 = iota((8, 128), 0)
    src_of = iota((128, 1), 0) // 16

    def nodes_at(src, wants, real):
        ids = all_ref[src, NODES : NODES + 16, :]
        k = ids - 128.0 * jnp.floor(ids * (1.0 / 128.0))
        hit = k == wants[0]
        for want in wants[1:]:
            hit = hit | (k == want)
        count = jnp.sum(jnp.where(hit, 1.0, 0.0), axis=1, keepdims=True)
        return jnp.where(src_of == real, jnp.concatenate([count] * 8, axis=0), 0.0)

    low = nodes_at(jnp.maximum(me - 1, 0), (127.0,), me - 1)
    up = jnp.minimum(me + 1, 7)
    up0, up01 = nodes_at(up, (0.0,), me + 1), nodes_at(up, (0.0, 1.0), me + 1)
    rims = {0: low + up0, 2: low + up01, 3: up0}
    mine_first = (16 * me).astype(F32)

    def prefix(x):
        return jnp.dot(jnp.broadcast_to(x, (8, 128)).astype(BF16), upper, preferred_element_type=F32)[0:1]

    for step in steps:
        keys = all_ref[0, KEYS + step : KEYS + 1 + step, :]
        for src in range(1, 8):
            keys = keys + all_ref[src, KEYS + step : KEYS + 1 + step, :]
        key_col = jnp.sum(jnp.where(eye, keys, 0.0), axis=1, keepdims=True)
        base = jnp.zeros((1, 1), F32)
        tasks = jnp.zeros((1, 1), F32)
        spots, codes = [], []
        for row in range(4):
            even = all_ref[2 * row, PAIRS + step : PAIRS + 1 + step, :]
            odd = all_ref[2 * row + 1, PAIRS + step : PAIRS + 1 + step, :]
            left = lane < 64
            first = jnp.where(left, even, pltpu.roll(odd, 64, 1))
            second = jnp.where(left, pltpu.roll(even, 64, 1), odd)
            box = jnp.where(left, 64.0 * row, 64.0 * row + 32.0)
            hit_first = key_col == first + box
            hit_second = key_col == second + box
            p_block = jnp.sum(jnp.where(hit_first, block_of + 1.0, 0.0), axis=0, keepdims=True) - 1.0
            r_block = jnp.sum(jnp.where(hit_second, block_of + 1.0, 0.0), axis=0, keepdims=True) - 1.0
            p_slot = p_block - mine_first
            live = r_block >= 0.0
            mine = live & (p_slot >= 0.0) & (p_slot < 16.0)
            sel = jnp.where(mine, 1.0, 0.0)
            spots.append(jnp.where(mine, prefix(sel) + base, -1.0))
            base = base + jnp.sum(sel, axis=1, keepdims=True)
            code = jnp.where(
                row8 == 0, jnp.broadcast_to(p_slot, (8, 128)), jnp.broadcast_to(r_block, (8, 128))
            )
            codes.append(jnp.where(jnp.broadcast_to(mine, (8, 128)), code, 0.0).astype(BF16))
            if step in rims:
                count = jnp.sum(jnp.where(hit_first, rims[step], 0.0), axis=0, keepdims=True)
                count = jnp.where(live, count, 0.0)
                start = prefix(count) + tasks
                tasks = tasks + jnp.sum(count, axis=1, keepdims=True)
                high = jnp.floor(start * (1.0 / 256.0))
                rim_block = jnp.where(p_slot < 0.0, p_slot + 16.0, p_slot)
                some = jnp.broadcast_to(count > 0.0, (8, 128))
                table = jnp.zeros((8, 128), F32)
                for n, line in enumerate((rim_block, r_block, high, start - 256.0 * high, start, count)):
                    table = jnp.where(row8 == n, jnp.broadcast_to(line, (8, 128)), table)
                task_ref[step, row] = jnp.where(some, table, 0.0)
        list_ref[4 + step : 5 + step, :] = jnp.broadcast_to(base, (1, 512)).astype(jnp.int32)
        list_ref[8 + step : 9 + step, :] = jnp.broadcast_to(tasks, (1, 512)).astype(jnp.int32)
        count = jnp.max(base)
        for part in range(4):

            def write(part=part, spots=spots, codes=codes, base=base, step=step):
                total = jnp.zeros((8, 128), F32)
                for row in range(4):
                    onehot = jnp.where(place == spots[row] - 128.0 * part, 1.0, 0.0).astype(BF16)
                    total = total + lax.dot_general(
                        codes[row], onehot, (((1,), (1,)), ((), ())), preferred_element_type=F32
                    )
                used = (lane + 128 * part).astype(F32) < base
                code = jnp.where(used, total[0:1] * 128.0 + total[1:2], 16.0 * 128.0)
                list_ref[step : step + 1, 128 * part : 128 * part + 128] = code.astype(jnp.int32)

            if part == 0:
                write()
            else:
                pl.when(count + 16.0 > 128.0 * part)(write)


UNROLL = 16


def pair_loop(list_ref, step, first_row, me, all_ref, turned_ref, force_ref, part=(0, 1)):
    for c in range(3):
        turned_ref[16, :, c] = jnp.zeros((4, 8, 128), F32)
        for s in range(16):
            wide = jnp.broadcast_to(all_ref[me, first_row + 16 * c + s : first_row + 16 * c + s + 1, :] * SCALE, (8, 128))
            for a in range(4):
                turned_ref[s, a, c] = roll_last(wide, 32 * a)

    def one(q):
        code = list_ref[step, q]
        slot = lax.shift_right_logical(code, 7)
        src = lax.shift_right_logical(code & 127, 4)
        line = first_row + (code & 15)
        xj = []
        for c in range(3):
            wide = jnp.broadcast_to(all_ref[src, pl.ds(line + 16 * c, 1), :] * SCALE, (8, 128))
            wide = pltpu.roll(wide, 0, 1, stride=1, stride_axis=0)
            xj.append([roll_last(wide, 8 * b) for b in range(4)])
        out = []
        for a in range(4):
            xi = [turned_ref[slot, a, c] for c in range(3)]
            acc = [None] * 3
            for b in range(4):
                diff = [xi[c] - xj[c][b] for c in range(3)]
                dist = diff[0] * diff[0] + diff[1] * diff[1] + diff[2] * diff[2]
                w = jnp.exp2(-dist)
                acc = [w * diff[c] if b == 0 else acc[c] + w * diff[c] for c in range(3)]
            out.append(acc)
        return slot, out

    def body(g, carry):
        done = [one(g * UNROLL + u) for u in range(UNROLL)]
        for slot, out in done:
            for a in range(4):
                for c in range(3):
                    force_ref[slot, a, c] += out[a][c]
        return carry

    groups = (list_ref[4 + step, 0] + (UNROLL - 1)) // UNROLL
    at, of = part
    lax.fori_loop(groups * at // of, groups * (at + 1) // of, body, 0)


def block_sums(force_ref, sum_ref):
    for c in range(3):
        total = force_ref[0:16, 0, c]
        for a in range(1, 4):
            total = total + roll_last(force_ref[0:16, a, c], -32 * a)
        sum_ref[c] = jnp.sum(total, axis=1) * (1.0 / SCALE)


def row_and_lane(ids):
    line = jnp.floor(ids * (1.0 / 128.0))
    lane = ids - 128.0 * line
    i = jnp.floor((line + 0.5) * (1.0 / 12.0))
    return 8.0 * line - 95.0 * i, lane


def one_hot(at, rows):
    return jnp.where(iota((rows, 128), 0).astype(F32) == at, 1.0, 0.0)


def hot_rows_lanes(ids):
    row, lane = row_and_lane(ids)
    return one_hot(row, 96).astype(BF16), one_hot(lane, 128)


def first_plan_kernel(at_ref, all_ref, list_ref, task_ref, rows_ref, lanes_ref):
    plan_kernel(at_ref, all_ref, list_ref, task_ref, steps=(0, 1))
    for s in range(16):
        at = slice(128 * s, 128 * s + 128)
        rows_ref[:, at], lanes = hot_rows_lanes(all_ref[at_ref[2], NODES + s : NODES + s + 1, :])
        lanes_ref[at, :] = jnp.transpose(lanes).astype(BF16)


def scatter_own(force_ref, sum_ref, rows_ref, lanes_ref, lhs_ref):
    block_sums(force_ref, sum_ref)
    for s in range(16):
        at = slice(128 * s, 128 * s + 128)
        hot = rows_ref[:, at]
        for c in range(3):
            hi, lo = split2(sum_ref[c, s : s + 1, :])
            lhs_ref[96 * c : 96 * c + 96, at] = hot * hi
            lhs_ref[288 + 96 * c : 384 + 96 * c, at] = hot * lo
    out = jnp.dot(lhs_ref[...], lanes_ref[...], preferred_element_type=F32)
    return (out[:288] + out[288:]).reshape(3, 12, 8, 128)


def split3(x, axis=0):
    hi, rest = x.astype(BF16), x
    rest = rest - hi.astype(F32)
    mid = rest.astype(BF16)
    return jnp.concatenate([hi, mid, (rest - mid.astype(F32)).astype(BF16)], axis=axis)


def contact_rim(list_ref, task_ref, step, first_row, me, pos_ref, ids_ref, rim, square_ref):
    all_ref, near_ref, info_ref, sum_ref = rim
    low, up = jnp.maximum(me - 1, 0), jnp.minimum(me + 1, 7)
    for c in range(3):
        at = first_row + 16 * c
        block = jnp.concatenate([pos_ref[src, at : at + 16, :] for src in range(8)], axis=0)
        all_ref[c] = split3(jnp.transpose(block * SCALE), 1)
        block = jnp.concatenate([pos_ref[low, at : at + 16, :], pos_ref[up, at : at + 16, :]], axis=0)
        near_ref[c] = split3(block * SCALE)
    ids = jnp.concatenate(
        [ids_ref[low, NODES : NODES + 16, :], ids_ref[up, NODES : NODES + 16, :]], axis=0
    )
    line, lane = row_and_lane(ids)
    below = iota((32, 128), 0) < 16
    ghost = (below & (lane == 127.0)) | (jnp.logical_not(below) & (lane == 0.0))
    if step == 2:
        ghost = ghost | (jnp.logical_not(below) & (lane == 1.0))
    upper = (iota((128, 128), 0) < iota((128, 128), 1)).astype(BF16)
    rank = jnp.dot(jnp.where(ghost, 1.0, 0.0).astype(BF16), upper, preferred_element_type=F32)
    info_ref[0] = jnp.where(ghost, rank, 255.0).astype(BF16)
    info_ref[1] = line.astype(BF16)
    info_ref[2] = jnp.where(below, 0.0, lane + 1.0).astype(BF16)
    sum_ref[...] = jnp.zeros_like(sum_ref)
    tasks = list_ref[8 + step, 0]

    def pick(table, hot):
        return lax.dot_general(table, hot, (((0,), (0,)), ((), ())), preferred_element_type=F32)

    def body(part, carry):
        first = part * 128
        number = (iota((128, 128), 0) + first).astype(F32)
        found = jnp.zeros((8, 128), F32)
        for row in range(4):
            entry = task_ref[step, row]
            start, count = entry[4:5], entry[5:6]
            hot = jnp.where((number >= start) & (number < start + count), 1.0, 0.0).astype(BF16)
            found = found + lax.dot_general(
                entry.astype(BF16), hot, (((1,), (1,)), ((), ())), preferred_element_type=F32
            )
        here = (iota((1, 128), 1) + first).astype(F32)
        nth = here - (256.0 * found[2:3] + found[3:4])
        live = here < tasks.astype(F32)
        hot_p = jnp.where(iota((32, 128), 0).astype(F32) == found[0:1], 1.0, 0.0).astype(BF16)
        hot_r = jnp.where(iota((128, 128), 0).astype(F32) == found[1:2], 1.0, 0.0).astype(BF16)
        match = pick(info_ref[0], hot_p) == nth
        line = jnp.sum(jnp.where(match, pick(info_ref[1], hot_p), 0.0), axis=0, keepdims=True)
        plane = jnp.sum(jnp.where(match, pick(info_ref[2], hot_p), 0.0), axis=0, keepdims=True)
        hot_p3 = jnp.concatenate([hot_p] * 3, axis=0)
        hot_r3 = jnp.concatenate([hot_r] * 3, axis=0)
        xi, xj = [], []
        for c in range(3):
            xi.append(jnp.sum(jnp.where(match, pick(near_ref[c], hot_p3), 0.0), axis=0, keepdims=True))
            xj.append(jnp.dot(all_ref[c], hot_r3, preferred_element_type=F32))
        diff = [xi[c] - xj[c] for c in range(3)]
        dist = diff[0] * diff[0] + diff[1] * diff[1] + diff[2] * diff[2]
        w = jnp.exp2(-dist)
        lines = []
        for want in range(3):
            for c in range(3):
                f = jnp.sum(w * diff[c], axis=0, keepdims=True) * (1.0 / SCALE)
                lines.append(jnp.where(live & (plane == want), f, 0.0))
        lines.append(jnp.zeros((7, 128), F32))
        hi, lo = split2(jnp.concatenate(lines, axis=0))
        hot = one_hot(line, 128).astype(BF16)
        got = lax.dot_general(
            jnp.concatenate([hi, lo], axis=0), hot, (((1,), (1,)), ((), ())), preferred_element_type=F32
        )
        sum_ref[...] += got[0:16] + got[16:32]
        return carry

    lax.fori_loop(0, (tasks + 127) // 128, body, 0)
    square_ref[...] = jnp.zeros_like(square_ref)
    for want, k in enumerate((127, 0, 1)):
        for c in range(3):
            at = (k + 8 * c) % 128
            square_ref[at : at + 1, :] = sum_ref[3 * want + c : 3 * want + c + 1, :]
    return fill16(jnp.transpose(square_ref[...])[0:96].reshape(12, 8, 128))


def node_sum(elements):
    e = 0.125 * elements
    e = e + prev_z(e)
    e = e + prev_x(e)
    zero = jnp.zeros((1,) + e.shape[1:], F32)
    return jnp.concatenate([e, zero], axis=0) + jnp.concatenate([zero, e], axis=0)


def send_planes(planes, out_ref):
    count = len(planes)
    for n, plane in enumerate(planes):
        out_ref[n] = plane[:, :128]
    for g in range(0, count, 16):
        out_ref[count + g // 16] = pack([p[:, 128:] for p in planes[g : g + 16]])


def get_plane(ref, n, count):
    return both(ref[n], unpack(ref[count + n // 16], n % 16))


class Halves:
    def __init__(self, main, rim):
        self.refs = (main, rim)

    def __getitem__(self, at):
        return both(*[ref[at] for ref in self.refs])

    def __setitem__(self, at, value):
        self.refs[0][at] = value[..., :128]
        self.refs[1][at] = value[..., 128:]

    def row(self, n, i):
        lines = pl.ds(208 * n + i, 13, stride=16)
        flat = [ref.reshape(ref.shape[0] * 208, 128) for ref in self.refs]
        return fill16(both(*[ref[lines, :] for ref in flat]))

    def set_row(self, n, i, plane):
        lines = pl.ds(208 * n + i, 13, stride=16)
        for t, ref in enumerate(self.refs):
            ref.reshape(ref.shape[0] * 208, 128)[lines, :] = plane[:13, 128 * t : 128 * t + 128]


def first_contact_kernel(
    at_ref, list_ref, task_ref, all_ref, field_ref, rows_ref, lanes_ref,
    fm_main_ref, fm_rim_ref, c0_ref, m1_ref, up_ref, down_ref,
    turned_ref, force_ref, sum_ref, lhs_ref, square_ref, *rim,
):
    me = at_ref[2]
    fm = Halves(fm_main_ref, fm_rim_ref)
    planes = neighbour_planes(all_ref, PLANES, 4, me, square_ref, 12)
    sums = [node_sum(both(fill16(field_ref[n]), unpack(planes, n, 4))) for n in range(4)]
    m1 = both(fill16(field_ref[4]), unpack(planes, 4, 4))
    zero = jnp.zeros((1, 16, 256), F32)
    m1 = jnp.concatenate([m1, zero], axis=0)
    m1_ref[...] = m1
    fm[3] = sums[3]
    for c in range(3):
        fm[c] = sums[c]
    force_ref[...] = jnp.zeros_like(force_ref)
    pair_loop(list_ref, 0, 0, me, all_ref, turned_ref, force_ref)
    own = scatter_own(force_ref, sum_ref, rows_ref, lanes_ref, lhs_ref)
    rim = contact_rim(list_ref, task_ref, 0, 0, me, all_ref, all_ref, rim, square_ref)
    for c in range(3):
        full = jnp.concatenate([both(fill16(own[c]), unpack(rim, c)), zero], axis=0)
        c0_ref[c] = full
        fm[c] = fm[c] + full
    ups = [fm.row(n, 7) for n in range(4)] + [fm.row(n, 8) for n in range(4)]
    send_planes(ups + [fill16(m1[:, 7, :])], up_ref)
    send_planes([fm.row(n, 0) for n in range(4)], down_ref)


def step_contact_kernel(
    at_ref, list_ref, all_ref, rows_ref, lanes_ref, out_ref, turned_ref, force_ref, sum_ref, lhs_ref
):
    force_ref[...] = jnp.zeros_like(force_ref)
    pair_loop(list_ref, 1, 0, at_ref[2], all_ref, turned_ref, force_ref)
    out_ref[...] = scatter_own(force_ref, sum_ref, rows_ref, lanes_ref, lhs_ref)


def shift_rows(x, by):
    return pltpu.roll(x, by % x.shape[1], 1)


def x_extended_1(fm, m1_ref, ups_ref, downs_ref, pick):
    lines = sorted(pick)
    row = iota((len(lines), 16, 256), 1)

    def lift(plane):
        return jnp.stack([jnp.broadcast_to(plane[j : j + 1], (16, 256)) for j in lines])

    def take(x):
        return jnp.stack([x[j] for j in lines])

    def extend(x, low, add, high):
        if add is not None:
            x = x + jnp.where(row == 0, lift(add), 0.0) + jnp.where(row == 8, lift(high), 0.0)
            x = jnp.where(row < 9, x, 0.0)
        else:
            x = jnp.where(row < 8, x, 0.0)
        return jnp.where(row == 0, lift(low), shift_rows(x, 1))

    out = [
        extend(
            take(fm[n]),
            get_plane(ups_ref, n, 9),
            get_plane(ups_ref, 4 + n, 9),
            get_plane(downs_ref, n, 4),
        )
        for n in range(4)
    ]
    return out, extend(take(m1_ref[...]), get_plane(ups_ref, 8, 9), None, None)


def y_send_1_kernel(fm_main_ref, fm_rim_ref, m1_ref, ups_ref, downs_ref, task_ref, up_ref, down_ref):
    fields, m1 = x_extended_1(Halves(fm_main_ref, fm_rim_ref), m1_ref, ups_ref, downs_ref, (0, 11, 12))
    send_planes([f[1] for f in fields] + [f[2] for f in fields] + [m1[1]], up_ref)
    send_planes([f[0] for f in fields], down_ref)


def stress_of(disp, modulus):
    grads = []
    for u in disp:
        s, d = u[1:] + u[:-1], u[1:] - u[:-1]
        sn = next_x(s)
        ss, xd = sn + s, sn - s
        yd = next_x(d) + d
        grads.append((xd + next_z(xd), yd + next_z(yd), next_z(ss) - ss))
    m = 0.25 * modulus
    exx, eyy, ezz = grads[0][0], grads[1][1], grads[2][2]
    trace = exx + eyy + ezz
    return (
        m * (2.0 * exx + trace),
        m * (2.0 * eyy + trace),
        m * (2.0 * ezz + trace),
        m * (grads[1][0] + grads[0][1]),
        m * (grads[2][1] + grads[1][2]),
        m * (grads[0][2] + grads[2][0]),
    )


def force_of(stress):
    xx, yy, zz, xy, yz, zx = stress
    out = []
    for a, b, c in ((xx, xy, zx), (xy, yy, yz), (zx, yz, zz)):
        az, bz, cz = a + prev_z(a), b + prev_z(b), prev_z(c) - c
        ac = (prev_x(az) - az) + (prev_x(cz) + cz)
        by = prev_x(bz) + bz
        out.append(-0.25 * ((ac[:-1] + ac[1:]) + (by[:-1] - by[1:])))
    return out


def gather_rows(disp, lanes_ref, rows_ref):
    hot = rows_ref[...]
    values = []
    for c in range(3):
        picked = [
            lax.dot_general(part, hot, (((0,), (0,)), ((), ())), preferred_element_type=F32)
            for part in split2(disp[c])
        ]
        picked = picked[0] + picked[1]
        values.append(jnp.sum(picked * lanes_ref[...], axis=0, keepdims=True))
    return values


def second_step_kernel(
    at_ref, fm_main_ref, fm_rim_ref, c0_ref, m1_ref, xu_ref, xd_ref, yu_ref, yd_ref, c1_ref, all_ref, rows_ref,
    out_ref, state_ref, square_ref, lanes_ref,
):
    fields, m1 = x_extended_1(Halves(fm_main_ref, fm_rim_ref), m1_ref, xu_ref, xd_ref, range(13))
    zero = jnp.zeros((1, 16, 256), F32)
    for n in range(4):
        low, add = get_plane(yu_ref, n, 9), get_plane(yu_ref, 4 + n, 9)
        own = fields[n]
        fields[n] = jnp.concatenate(
            [low[None], (own[0] + add)[None], own[1:12], (own[12] + get_plane(yd_ref, n, 4))[None]],
            axis=0,
        )
    m1 = jnp.concatenate([get_plane(yu_ref, 8, 9)[None], m1[:12]], axis=0)
    mass = fields[3]
    inv = jnp.where(mass > 0.0, DT / jnp.where(mass > 0.0, mass, 1.0), 0.0)
    disp1 = [DT * (inv * fields[c]) for c in range(3)]
    force = force_of([jnp.concatenate([x, zero], axis=0) for x in stress_of(disp1, m1)])
    inv = inv[1:]
    row = iota((13, 16, 256), 1)
    good = (row > 0) & (row < 10)
    disp2s, vel2s = [], []
    for c in range(3):
        c1 = jnp.concatenate([fill16(c1_ref[c]), jnp.zeros((1, 16, 128), F32)], axis=0)
        c1 = shift_rows(both(c1, jnp.zeros((13, 16, 128), F32)), 1)
        total = fields[c][1:]
        accel = inv * (total - shift_rows(c0_ref[c], 1))
        vel2 = inv * total + inv * force[c] + (accel + inv * c1)
        disp2 = disp1[c][1:] + DT * vel2
        back = [shift_rows(jnp.where(good, x, 0.0), -1) for x in (disp2, vel2, accel)]
        disp2s.append(back[0])
        vel2s.append(back[1])
        state_ref[c] = back[0]
        state_ref[3 + c] = back[1]
        state_ref[6 + c] = back[2]
    state_ref[9] = shift_rows(jnp.where(good, inv, 0.0), -1)
    me = at_ref[2]
    for s in range(16):
        lanes_ref[:, 128 * s : 128 * s + 128] = hot_rows_lanes(all_ref[me, NODES + s : NODES + s + 1, :])[1]
    for first, disp in (
        (0, [shift_rows(d[1:13], -1)[:, :8, :128] for d in disp1]),
        (LATE, [d[0:12, :8, :128] for d in disp2s]),
    ):
        values = gather_rows([d.reshape(96, 128) for d in disp], lanes_ref, rows_ref)
        for c in range(3):
            block = jnp.concatenate(
                [values[c][:, 128 * s : 128 * s + 128] for s in range(16)], axis=0
            ) + all_ref[me, 16 * c : 16 * c + 16, :]
            for dest in range(8):
                out_ref[dest, first + 16 * c : first + 16 * c + 16, :] = block
    rows = planes_to_rows(pack([x[:, :, :128] for x in disp2s + vel2s], 5), square_ref)
    for dest in range(8):
        out_ref[dest, PLANES_2:ROWS_2, :] = rows


UP_LIST = (
    [(n, 0) for n in range(3)] + [(n, 1) for n in range(3)] + [(n, 1) for n in (3, 4, 5, 9)]
    + [(10, 0), (10, 1), (11, 1)]
)
DOWN_LIST = (
    [(n, p) for p in (0, 1, 2) for n in range(3)]
    + [(n, p) for p in (0, 1) for n in (3, 4, 5)]
    + [(n, 0) for n in (6, 7, 8)]
    + [(9, 0), (9, 1), (10, 0), (10, 1), (11, 0)]
)
UPS, DOWNS = len(UP_LIST), len(DOWN_LIST)


def plane_of(ref, listed, n, p):
    return get_plane(ref, listed.index((n, p)), len(listed)) if (n, p) in listed else None


def late_contact_kernel(
    at_ref, list_ref, task_ref, first_ref, all_ref, state_ref, field_ref, rows_ref, lanes_ref,
    main_ref, rim_ref, up_ref, down_ref,
    turned_ref, force_ref, sum_ref, lhs_ref, square_ref, *rims,
):
    me = at_ref[2]
    own = Halves(main_ref, rim_ref)
    zplanes = neighbour_planes(all_ref, PLANES_2, 5, me, square_ref, 13)
    mplanes = neighbour_planes(first_ref, PLANES, 4, me, square_ref, 12)
    top = (iota((13, 16, 128), 2) == 0) & (me == 7)
    zero = jnp.zeros((1, 16, 256), F32)

    def with_rim(x, n):
        return both(x[:, :, :128], jnp.where(top, x[:, :, 128:], unpack(zplanes, n, 5)))

    inv = state_ref[9]
    own[9] = inv
    for c in range(3):
        own[c] = with_rim(state_ref[c], c)
        own[3 + c] = with_rim(state_ref[3 + c], 3 + c) + state_ref[6 + c]
        own[6 + c] = state_ref[6 + c]
    for n, step in ((10, 2), (11, 3)):
        m = both(fill16(field_ref[3 + step]), unpack(mplanes, 3 + step, 4))
        own[n] = jnp.concatenate([m, zero], axis=0)
    for step, first_row, n in ((2, 0, 3), (3, LATE, 6)):
        force_ref[...] = jnp.zeros_like(force_ref)
        pair_loop(list_ref, step, first_row, me, all_ref, turned_ref, force_ref)
        got = scatter_own(force_ref, sum_ref, rows_ref, lanes_ref, lhs_ref)
        rim = contact_rim(list_ref, task_ref, step, first_row, me, all_ref, first_ref, rims, square_ref)
        for c in range(3):
            full = both(fill16(got[c]), unpack(rim, c))
            own[n + c, 0:12] = own[n + c, 0:12] + own[9, 0:12] * full
    send_planes([own.row(n, 6 + p) for n, p in UP_LIST], up_ref)
    send_planes([own.row(n, p) for n, p in DOWN_LIST], down_ref)


def x_extended_2(own, ups_ref, downs_ref, at_last, lines):
    row = iota((len(lines), 16, 256), 1)
    keep = (row < 8) | ((row == 8) & at_last)

    def lift(plane):
        return jnp.stack([jnp.broadcast_to(plane[j : j + 1], (16, 256)) for j in lines])

    out = []
    for n in range(12):
        x = jnp.stack([own[n, j] for j in lines])
        x = shift_rows(jnp.where(keep, x, 0.0), 2)
        for ref, listed, first, count in ((ups_ref, UP_LIST, 0, 2), (downs_ref, DOWN_LIST, 10, 3)):
            for p in range(count):
                got = plane_of(ref, listed, n, p)
                if got is not None:
                    add = lift(got)
                    if first + p == 10:
                        x = jnp.where((row == 10) & jnp.logical_not(at_last), add, x)
                    else:
                        x = jnp.where(row == first + p, add, x)
        out.append(x)
    return out


def y_send_2_kernel(at_ref, main_ref, rim_ref, ups_ref, downs_ref, up_ref, down_ref):
    fields = x_extended_2(Halves(main_ref, rim_ref), ups_ref, downs_ref, at_ref[0] == 7, (0, 1, 2, 10, 11))
    send_planes([fields[n][3 + p] for n, p in UP_LIST], up_ref)
    send_planes([fields[n][p] for n, p in DOWN_LIST], down_ref)


def last_kernel(
    at_ref, main_ref, rim_ref, xu_ref, xd_ref, yu_ref, yd_ref, vel_ref, stress_ref, wide_main_ref, wide_rim_ref
):
    own, grown = Halves(main_ref, rim_ref), Halves(wide_main_ref, wide_rim_ref)
    at_last = at_ref[0] == 7
    row = iota((13, 16, 256), 1)
    for n in range(12):
        grown[n] = shift_rows(jnp.where((row < 8) | ((row == 8) & at_last), own[n], 0.0), 2)
        for ref, listed, first, count in ((xu_ref, UP_LIST, 0, 2), (xd_ref, DOWN_LIST, 10, 3)):
            for p in range(count):
                got = plane_of(ref, listed, n, p)
                if got is None:
                    continue
                if first + p == 10:
                    got = jnp.where(at_last, own.row(n, 8), got)
                grown.set_row(n, first + p, got)
    fields = [grown[n] for n in range(12)]
    y_last = at_ref[1] == 3
    none = jnp.zeros((16, 256), F32)
    wide = []
    for n in range(12):
        planes = [plane_of(yu_ref, UP_LIST, n, p) for p in (0, 1)]
        planes += [fields[n][j] for j in range(12)]
        after = [plane_of(yd_ref, DOWN_LIST, n, p) for p in (0, 1, 2)]
        after = [none if p is None else p for p in after]
        after[0] = jnp.where(y_last, fields[n][12], after[0])
        planes = [none if p is None else p for p in planes] + after
        wide.append(jnp.stack(planes))
    disp2, vh3, g3, inv, m2, m3 = wide[0:3], wide[3:6], wide[6:9], wide[9], wide[10], wide[11]
    force = force_of(stress_of(disp2, m2[:16]))
    vel3 = [vh3[c][1:16] + inv[1:16] * force[c] for c in range(3)]
    disp3 = [disp2[c][1:16] + DT * vel3[c] for c in range(3)]
    force = force_of(stress_of(disp3, m3[1:15]))
    vel4 = [vel3[c][1:14] + (inv[2:15] * force[c] + g3[c][2:15]) for c in range(3)]
    disp4 = [disp3[c][1:14] + DT * vel4[c] for c in range(3)]
    stress = stress_of(disp4, m3[2:14])
    for n in range(6):
        stress_ref[n] = shift_rows(stress[n][:, :, :128], -2)[:, :8, :]
    for c in range(3):
        s = vel4[c][1:] + vel4[c][:-1]
        s = s + next_x(s)
        s = s + next_z(s)
        vel_ref[c] = shift_rows(0.125 * s[:, :, :128], -2)[:, :8, :]


def call(kernel, outs, specs, scratch=(), held=()):
    def run(*args):
        spaces = [pltpu.VMEM if spec is HELD else pltpu.HBM if spec is FAR else None for spec in specs]
        args = [
            a if space is None else pltpu.with_memory_space_constraint(a, space)
            for a, space in zip(args, spaces)
        ]
        return pl.pallas_call(
            kernel,
            out_shape=[
                pltpu.VMEM(s, d) if n in held else jax.ShapeDtypeStruct(s, d)
                for n, (s, d) in enumerate(outs)
            ],
            in_specs=specs,
            out_specs=[VMEM] * len(outs),
            scratch_shapes=list(scratch),
            compiler_params=PARAMS,
        )(*args)

    return run


def share(blocks):
    return lax.all_to_all(blocks, "gz", split_axis=0, concat_axis=0, tiled=True)


def neighbours(up, down, axis):
    count = lax.axis_size(axis)
    ahead = [(i, i + 1) for i in range(count - 1)]
    return lax.ppermute(up, axis, ahead), lax.ppermute(down, axis, [(j, i) for i, j in ahead])


TURNED = pltpu.VMEM((17, 4, 3, 8, 128), F32)
SUMS = pltpu.VMEM((3, 16, 128), F32)
RIM = [
    pltpu.VMEM((3, 128, 384), BF16),
    pltpu.VMEM((3, 96, 128), BF16),
    pltpu.VMEM((3, 32, 128), BF16),
    pltpu.VMEM((16, 128), F32),
]
LHS = pltpu.VMEM((576, 2048), BF16)
SQUARE = pltpu.VMEM((128, 128), F32)


def per_device(stiffness, density, load, alive, surf_coords, surf_nodes, routes, pairs):
    at = jnp.stack([lax.axis_index(a) for a in ("gx", "gy", "gz")]).astype(jnp.int32)
    stiffness, density = jnp.swapaxes(stiffness, 0, 1), jnp.swapaxes(density, 0, 1)
    load, alive = jnp.swapaxes(load, 1, 2), jnp.swapaxes(alive, 1, 2)
    coords = jnp.swapaxes(surf_coords, 0, 1)
    pairs = jnp.swapaxes(pairs[:, 0], 1, 2)
    params = (coords, routes, pairs, surf_nodes, stiffness, density, load, alive)
    payload, fields = call(
        prep_kernel,
        [((8, ROWS_1, 128), F32), ((7, 12, 8, 128), F32)],
        [SMEM] + [FAR] * 8,
        [SQUARE] + [pltpu.VMEM(p.shape, p.dtype) for p in params] + [pltpu.SemaphoreType.DMA((8,))],
        (1,),
    )(at, *params)
    everyone = share(payload)
    plan_out = [((12, 512), jnp.int32), ((4, 4, 8, 128), F32)]
    lists, tasks, *hot = call(
        first_plan_kernel,
        plan_out + [((96, 2048), BF16), ((2048, 128), BF16)],
        [SMEM, HELD],
        (),
        (1, 2, 3),
    )(at, everyone)
    fm, fm_rim, c0, m1, up, down = call(
        first_contact_kernel,
        [((5, 13, 16, 128), F32)] * 2 + [((3, 13, 16, 256), F32), ((13, 16, 256), F32), ((10, 16, 128), F32),
         ((5, 16, 128), F32)],
        [SMEM, SMEM] + [HELD] * 5,
        [TURNED, TURNED, SUMS, LHS, SQUARE] + RIM,
        (0, 1, 2, 3),
    )(at, lists, tasks, everyone, fields, *hot)
    xu, xd = neighbours(up, down, "gx")
    late_lists, late_tasks = call(
        functools.partial(plan_kernel, steps=(2, 3)), plan_out, [SMEM, HELD, HELD], (), (1,)
    )(at, everyone, m1)
    up, down = call(y_send_1_kernel, [((10, 16, 128), F32), ((5, 16, 128), F32)], [HELD] * 6)(
        fm, fm_rim, m1, xu, xd, late_tasks
    )
    yu, yd = neighbours(up, down, "gy")
    (c1,) = call(
        step_contact_kernel,
        [((3, 12, 8, 128), F32)],
        [SMEM, SMEM] + [HELD] * 3,
        [TURNED, TURNED, SUMS, LHS],
        (0,),
    )(at, lists, everyone, *hot)
    payload, state = call(
        second_step_kernel,
        [((8, ROWS_2, 128), F32), ((10, 13, 16, 256), F32)],
        [SMEM] + [HELD] * 11,
        [SQUARE, pltpu.VMEM((128, 2048), F32)],
        (1,),
    )(at, fm, fm_rim, c0, m1, xu, xd, yu, yd, c1, everyone, hot[0])
    late = share(payload)
    own, own_rim, up, down = call(
        late_contact_kernel,
        [((13, 13, 16, 128), F32)] * 2 + [((UPS + 1, 16, 128), F32), ((DOWNS + 2, 16, 128), F32)],
        [SMEM, SMEM] + [HELD] * 7,
        [TURNED, TURNED, SUMS, LHS, SQUARE] + RIM,
        (0, 1),
    )(at, late_lists, late_tasks, everyone, late, state, fields, *hot)
    xu, xd = neighbours(up, down, "gx")
    up, down = call(
        y_send_2_kernel,
        [((UPS + 1, 16, 128), F32), ((DOWNS + 2, 16, 128), F32)],
        [SMEM] + [HELD] * 4,
    )(at, own, own_rim, xu, xd)
    yu, yd = neighbours(up, down, "gy")
    vel, stress = call(
        last_kernel,
        [((3, 12, 8, 128), F32), ((6, 12, 8, 128), F32)],
        [SMEM] + [HELD] * 6,
        [pltpu.VMEM((13, 13, 16, 128), F32)] * 2,
    )(at, own, own_rim, xu, xd, yu, yd)
    return jnp.swapaxes(vel, 1, 2), jnp.swapaxes(stress, 1, 2)


def solution(mesh):
    return jax.shard_map(
        per_device,
        mesh=mesh,
        in_specs=(
            P("gx", "gy", "gz"),
            P("gx", "gy", "gz"),
            P(None, "gx", "gy", "gz"),
            P(None, "gx", "gy", "gz"),
            P(("gx", "gy", "gz"), None, None),
            P(("gx", "gy", "gz"), None),
            P(None, ("gx", "gy", "gz")),
            P(None, ("gx", "gy", "gz"), None, None),
        ),
        out_specs=(P(None, "gx", "gy", "gz"), P(None, "gx", "gy", "gz")),
        check_vma=False,
    )
```
